512 devices in a mesh: centre: 16 (over y, core), sample: 32 (over z, x).
Axes of the slice: x: 4, y: 8, z: 8, core: 2. Of those that a mesh axis runs over, the one named last changes fastest.
Arguments:
- centres: bfloat16 [1024, 32768], P(None, 'centre'), may hold values from -40 to 40
- pool: bfloat16 [1024, 32768], P('centre', 'sample'), may hold values from -40 to 40
- labels: int32 [32768], P('sample'), may hold values from 0 to 143
- picks: int32 [2, 16384], P(None, 'sample'), may hold values from 0 to 32767, as said below
- coefs: float32 [144, 32768], P(None, ('centre', 'sample')), may hold values from -192 to 1024000
Outputs:
- new_coefs: float32 [144, 32768], P(None, ('centre', 'sample'))
The draws below stay inside these ranges and needn't reach their ends.
Inputs may be any that keep to these rules, and one draw needn't show every extreme that they name: `picks`: entry b of a step's batch is a pool column in [(b // 512) * 1024, (b // 512 + 1) * 1024); entries may repeat.
All inputs are finite; a program needn't handle non-finite values.
Results may differ from the reference program's by a relative error of at most 0.00065.
Values may be sent and summed in bfloat16 or wider, within the bound.
No kernel may reach another device: no remote copies, remote signals or barrier semaphores. Data moves between devices by JAX's collectives and lax.ppermute only.
A program may use at most 64 MiB of HBM per device.

```python
import jax
import jax.numpy as jnp
from jax import lax

D = 1024
K = 144
STEPS = 2
BATCH_DEV = 512
POOL_DEV = 1024
CENTRES = 32768
BATCH = 16384
POOL = 32768
N_SAMPLE = 32


GROUP_SHARED = 0.05


GROUP_NOISE = 0.15


GROUP_LEVEL = 128.0


WAVE_AMPLITUDE = 2.5


WAVE_RATE = 0.35


def column_scales(key, count, lower, upper):
    return jnp.exp(jax.random.uniform(key, (count,), jnp.float32, jnp.log(lower), jnp.log(upper)))


def latent_map(key):
    return jax.random.truncated_normal(jax.random.fold_in(key, 5001), -4.0, 4.0, (D, 8), jnp.float32)


def centre_latents(key):
    return jax.random.truncated_normal(jax.random.fold_in(key, 5002), -4.0, 4.0, (8, CENTRES), jnp.float32)


def pool_latents(key):
    return jax.random.truncated_normal(jax.random.fold_in(key, 5003), -4.0, 4.0, (8, POOL), jnp.float32)


def prototypes(key):
    return jax.random.truncated_normal(jax.random.fold_in(key, 6001), -4.0, 4.0, (D, 2 * K), jnp.float32)


def centre_groups(key):
    return jax.random.randint(jax.random.fold_in(key, 6003), (CENTRES,), 0, 2 * K, jnp.int32)


def pool_groups(key):
    return jax.random.randint(jax.random.fold_in(key, 6004), (POOL,), 0, 2 * K, jnp.int32)


def grouped_columns(key, groups, latents, salt, lower, upper):
    scales = column_scales(jax.random.fold_in(key, 6002), 2 * K, lower, upper)
    base = jnp.take(prototypes(key), groups, axis=1)
    jitter = jax.random.truncated_normal(jax.random.fold_in(key, salt), -4.0, 4.0, (D, groups.shape[0]), jnp.float32)
    shared = jnp.dot(latent_map(key), latents, precision=lax.Precision.HIGHEST)
    return jnp.take(scales, groups)[None, :] * (base + GROUP_SHARED * shared + GROUP_NOISE * jitter)


def draw_centres(key, part):
    groups = centre_groups(key)
    columns = grouped_columns(key, groups, centre_latents(key), 11, 0.5, 2.0)
    return jnp.clip(columns, -40.0, 40.0).astype(jnp.bfloat16)


def draw_pool(key, part):
    groups = pool_groups(key)
    columns = grouped_columns(key, groups, pool_latents(key), 13, 0.5, 2.0)
    return jnp.clip(columns, -40.0, 40.0).astype(jnp.bfloat16)


def draw_picks(key, part):
    offsets = jax.random.randint(jax.random.fold_in(key, 31), (STEPS, BATCH), 0, POOL_DEV, jnp.int32)
    starts = jnp.arange(BATCH, dtype=jnp.int32) // BATCH_DEV * POOL_DEV
    return offsets + starts[None, :]


def draw_coefs(key, part):
    frequency = WAVE_RATE * jax.random.normal(jax.random.fold_in(key, 41), (256, 8), jnp.float32)
    phases = jax.random.uniform(jax.random.fold_in(key, 42), (256, 1), jnp.float32, -3.14159265, 3.14159265)
    wave_table = jnp.cos(jnp.dot(frequency, centre_latents(key), precision=lax.Precision.HIGHEST) + phases)
    groups = centre_groups(key)
    mixing = jax.random.uniform(jax.random.fold_in(key, 43), (K, 256), jnp.float32, -1.0, 1.0)
    jitter = jax.random.uniform(jax.random.fold_in(key, 22), (K, CENTRES), jnp.float32, -0.3, 0.3)
    group_table = GROUP_LEVEL * jax.random.uniform(jax.random.fold_in(key, 44), (K, 2 * K), jnp.float32, -1.0, 1.0)
    columns = WAVE_AMPLITUDE / 16.0 * jnp.dot(mixing, wave_table, precision=lax.Precision.HIGHEST) + jitter
    columns = columns + jnp.take(group_table, groups, axis=1)
    return columns.astype(jnp.float32)


def touch_ends(result, own_key, smallest, high):
    spot = [jax.random.randint(jax.random.fold_in(own_key, axis), (), 0, length) for axis, length in enumerate(result.shape)]
    widest = result.shape.index(max(result.shape))
    next_to = spot[:widest] + [(spot[widest] + 1) % result.shape[widest]] + spot[widest + 1:]
    return result.at[tuple(spot)].set(smallest).at[tuple(next_to)].set(high)


def setup_inputs(seed: int = 0) -> dict:
    streams_of = jax.random.split(jax.random.key(seed), 6)
    centres = draw_centres(jax.random.fold_in(streams_of[5], 71), 0)
    pool = draw_pool(jax.random.fold_in(streams_of[5], 71), 0)
    labels = touch_ends(jax.random.randint(streams_of[2], (POOL,), 0, K), jax.random.fold_in(streams_of[2], 1), 0, K - 1).astype(jnp.int32)
    picks = draw_picks(jax.random.fold_in(streams_of[5], 71), 0)
    coefs = draw_coefs(jax.random.fold_in(streams_of[5], 71), 0)
    return dict(centres=centres, pool=pool, labels=labels, picks=picks, coefs=coefs)


LOGIT_GAIN = 16.0
LENGTH_SCALE = 0.5
STEP_GAIN = 2048.0
EPS = 1e-06

def laplace(cross, sample_sq, centre_sq):
    mean_sq = (sample_sq[:, None] + centre_sq[None, :] - 2.0 * cross) / D
    return jnp.exp(-jnp.sqrt(mean_sq + EPS) / LENGTH_SCALE).astype(jnp.bfloat16)

def residual(logits, labs):
    classes = jnp.arange(K, dtype=jnp.int32)
    top = lax.optimization_barrier(jnp.max(logits, axis=0, keepdims=True))
    expo = jnp.exp(logits - top)
    probs = expo / lax.optimization_barrier(jnp.sum(expo, axis=0, keepdims=True))
    hot = (classes[:, None] == labs[None, :]).astype(jnp.float32)
    return (probs - hot).astype(jnp.bfloat16)

def reference(centres, pool, labels, picks, coefs):
    centre_sq = lax.optimization_barrier(jnp.sum(jnp.square(centres.astype(jnp.float32)), axis=0))
    for step in range(STEPS):
        blocks = picks[step].reshape(N_SAMPLE, BATCH_DEV)
        coef_half = coefs.astype(jnp.bfloat16)

        def visit(total, block):
            feats = jnp.take(pool, block, axis=1)
            cross = lax.dot_general(feats, centres, (((0,), (0,)), ((), ())), preferred_element_type=jnp.float32)
            sample_sq = lax.optimization_barrier(jnp.sum(jnp.square(feats.astype(jnp.float32)), axis=0))
            kern = laplace(cross, sample_sq, centre_sq)
            logits = lax.dot_general(coef_half, kern, (((1,), (1,)), ((), ())), preferred_element_type=jnp.float32)
            logits = logits * (LOGIT_GAIN / CENTRES)
            resid = residual(logits, jnp.take(labels, block))
            return (total + jnp.dot(resid, kern, preferred_element_type=jnp.float32), None)
        grad, _ = lax.scan(visit, jnp.zeros((K, CENTRES), jnp.float32), blocks)
        coefs = coefs - STEP_GAIN * LOGIT_GAIN / BATCH * grad
    return coefs
```

```python
import jax
import jax.numpy as jnp
from jax import lax
from jax.sharding import Mesh, PartitionSpec as P

STEPS = 2


LOGIT_GAIN = 16.0
LENGTH_SCALE = 0.5
STEP_GAIN = 2048.0
EPS = 1e-06

CENTRE = ("y", "core")
SAMPLE = ("z", "x")


def exchange(parts, axes):
    return lax.all_to_all(parts, axes, 0, 0, tiled=True)


def spread(array, axes):
    peers = lax.axis_size(axes)
    return exchange(jnp.broadcast_to(array[None], (peers, *array.shape)), axes)


def pack(array, peers, lanes=128):
    rows, columns = array.shape
    width = columns // peers
    fold = lanes // width
    parts = array.reshape(fold, rows // fold, peers, width)
    return jnp.transpose(parts, (2, 1, 0, 3)).reshape(peers, rows // fold, lanes)


def unpack(parts, width):
    peers, height, lanes = parts.shape
    fold = lanes // width
    parts = parts.reshape(peers, height, fold, width)
    return jnp.transpose(parts, (2, 1, 0, 3)).reshape(fold * height, peers * width)


def laplace(cross, sample_sq, centre_sq, width):
    mean_sq = (sample_sq[:, None] + centre_sq[None, :] - 2.0 * cross) / width
    return jnp.exp(-jnp.sqrt(mean_sq + EPS) / LENGTH_SCALE).astype(jnp.bfloat16)


def on_device(centres, pool, labels, picks, coefs):
    width = centres.shape[0]
    cen_dev = centres.shape[1]
    pool_dev = pool.shape[1]
    batch_dev = picks.shape[1]
    classes = coefs.shape[0]
    n_centre, n_sample = lax.axis_size(CENTRE), lax.axis_size(SAMPLE)
    total_centres = cen_dev * n_centre
    total_batch = batch_dev * n_sample
    rate = STEP_GAIN * LOGIT_GAIN / total_batch
    own = batch_dev // n_centre
    cen_own = coefs.shape[1]
    me = lax.axis_index(CENTRE)
    core = lax.axis_index("core")
    local_picks = picks - lax.axis_index(SAMPLE) * pool_dev
    centre_sq = jnp.sum(jnp.square(centres.astype(jnp.float32)), axis=0)

    kerns, labs = [], []
    for step in range(STEPS):
        chosen = local_picks[step]
        feats = jnp.take(pool, chosen, axis=1, mode="clip")
        labs.append(jnp.take(labels, lax.dynamic_slice(chosen, (me * own,), (own,)), mode="clip"))
        mine = lax.all_gather(feats, "y", axis=0)
        other = lax.ppermute(mine, "core", [(0, 1), (1, 0)])
        first = jnp.where(core == 0, mine, other)
        second = jnp.where(core == 0, other, mine)
        gathered = jnp.stack([first, second], axis=1).reshape(width, batch_dev)
        cross = lax.dot_general(
            gathered, centres, (((0,), (0,)), ((), ())), preferred_element_type=jnp.float32
        )
        sample_sq = jnp.sum(jnp.square(gathered.astype(jnp.float32)), axis=0)
        kerns.append(laplace(cross, sample_sq, centre_sq, width))

    current = coefs
    for step in range(STEPS):
        coef_half = unpack(spread(pack(current.astype(jnp.bfloat16), 1)[0], SAMPLE), cen_own)
        kern = kerns[step]
        partial_logits = lax.dot_general(
            coef_half, kern, (((1,), (1,)), ((), ())), preferred_element_type=jnp.float32
        )
        arrived = exchange(pack(partial_logits.astype(jnp.bfloat16), n_centre), CENTRE)
        total = jnp.sum(arrived.astype(jnp.float32), axis=0, keepdims=True)
        logits = unpack(total, own) * (LOGIT_GAIN / total_centres)
        top = jnp.max(logits, axis=0, keepdims=True)
        expo = jnp.exp(logits - top)
        probs = expo / jnp.sum(expo, axis=0, keepdims=True)
        class_ids = jnp.arange(classes, dtype=jnp.int32)
        onehot = (class_ids[:, None] == labs[step][None, :]).astype(jnp.float32)
        resid = (probs - onehot).astype(jnp.bfloat16)
        resid = unpack(spread(pack(resid, 1)[0], CENTRE), own)
        grad_part = jnp.dot(resid, kern, preferred_element_type=jnp.float32)
        arrived = exchange(pack(grad_part.astype(jnp.bfloat16), n_sample), SAMPLE)
        grad = unpack(jnp.sum(arrived.astype(jnp.float32), axis=0, keepdims=True), cen_own)
        current = current - rate * grad
    return current


def solution(mesh):
    sizes = (mesh.shape["centre"] // 2, 2, 8, mesh.shape["sample"] // 8)
    fine = Mesh(mesh.devices.reshape(sizes), (*CENTRE, *SAMPLE))
    placed = (
        P(None, CENTRE),
        P(CENTRE, SAMPLE),
        P(SAMPLE),
        P(None, SAMPLE),
        P(None, (*CENTRE, *SAMPLE)),
    )
    return jax.shard_map(
        on_device,
        mesh=fine,
        in_specs=placed,
        out_specs=P(None, (*CENTRE, *SAMPLE)),
        check_vma=False,
    )
```

```python
import functools

import jax
import jax.numpy as jnp
from jax import lax
from jax.experimental import pallas as pl
from jax.experimental.pallas import tpu as pltpu
from jax.sharding import Mesh, PartitionSpec as P

STEPS = 2


LOGIT_GAIN = 16.0
LENGTH_SCALE = 0.5
STEP_GAIN = 2048.0
EPS = 1e-06

LANES = 128
CENTRE = ("y", "core")
SAMPLE = ("z", "x")


def exchange(parts, axes):
    return lax.all_to_all(parts, axes, 0, 0, tiled=True)


def spread(array, axes):
    peers = lax.axis_size(axes)
    return exchange(jnp.broadcast_to(array[None], (peers, *array.shape)), axes)


def call(body, out, flops, *operands, scratch=()):
    vmem = pl.BlockSpec(memory_space=pltpu.VMEM)
    many = isinstance(out, (list, tuple))
    nbytes = sum(a.size * a.dtype.itemsize for a in operands)
    return pl.pallas_call(
        body,
        out_shape=out,
        in_specs=[vmem] * len(operands),
        out_specs=[vmem] * len(out) if many else vmem,
        scratch_shapes=list(scratch),
        cost_estimate=pl.CostEstimate(flops=flops, bytes_accessed=nbytes, transcendentals=0),
        compiler_params=pltpu.CompilerParams(vmem_limit_bytes=24 << 20),
    )(*operands)


def regroup(blocks, fold):
    width = LANES // fold
    lane_block = lax.broadcasted_iota(jnp.int32, blocks[0].shape, 1) // width
    out = []
    for q in range(fold):
        merged = None
        for k in range(fold):
            shift = width * (k - q) % LANES
            moved = pltpu.roll(blocks[k], shift, 1) if shift else blocks[k]
            merged = moved if merged is None else jnp.where(lane_block == k, moved, merged)
        out.append(merged)
    return out


def logits_body(coef_ref, kern_ref, out_ref, coef, logits):
    peers, height, _ = coef_ref.shape
    for pair in range(peers // 2):
        halves = regroup([coef_ref[2 * pair + i].astype(jnp.float32) for i in range(2)], 2)
        for h in range(2):
            coef[height * h : height * (h + 1), LANES * pair : LANES * (pair + 1)] = halves[h]
    logits[...] = lax.dot_general(
        coef[...].astype(jnp.bfloat16),
        kern_ref[...],
        (((1,), (1,)), ((), ())),
        preferred_element_type=jnp.float32,
    )
    receivers, rows, _ = out_ref.shape
    fold = coef.shape[0] // rows
    for group in range(receivers // fold):
        columns = slice(LANES * group, LANES * (group + 1))
        blocks = regroup([logits[rows * q : rows * (q + 1), columns] for q in range(fold)], fold)
        for k in range(fold):
            out_ref[fold * group + k] = blocks[k].astype(out_ref.dtype)


def partial_logits(coef_parts, kern, peers):
    classes = 2 * coef_parts.shape[1]
    batch, centres = kern.shape
    rows = classes * (batch // peers) // LANES
    return call(
        logits_body,
        jax.ShapeDtypeStruct((peers, rows, LANES), jnp.bfloat16),
        2 * classes * batch * centres,
        coef_parts,
        kern,
        scratch=[pltpu.VMEM((classes, centres), jnp.float32), pltpu.VMEM((classes, batch), jnp.float32)],
    )


def fold_all(row, fold, op):
    while fold > 1:
        row = op(row, pltpu.roll(row, LANES // fold, 1))
        fold //= 2
    return row


def residual_body(gain, fold, arrived_ref, labs_ref, out_ref):
    peers, rows, _ = arrived_ref.shape
    total = arrived_ref[0].astype(jnp.float32)
    for peer in range(1, peers):
        total = total + arrived_ref[peer].astype(jnp.float32)
    logits = total * gain
    top = fold_all(jnp.max(logits, axis=0, keepdims=True), fold, jnp.maximum)
    expo = jnp.exp(logits - top)
    mass = fold_all(jnp.sum(expo, axis=0, keepdims=True), fold, jnp.add)
    probs = expo / mass
    block = lax.broadcasted_iota(jnp.int32, logits.shape, 1) // (LANES // fold)
    class_ids = block * rows + lax.broadcasted_iota(jnp.int32, logits.shape, 0)
    onehot = (class_ids == labs_ref[...]).astype(jnp.float32)
    resid = (probs - onehot).astype(out_ref.dtype)
    for peer in range(peers):
        out_ref[peer] = resid


def residual(arrived, labs, gain, fold):
    return call(
        functools.partial(residual_body, gain, fold),
        jax.ShapeDtypeStruct(arrived.shape, jnp.bfloat16),
        8 * arrived.size,
        arrived,
        jnp.tile(labs, fold)[None],
    )


def grad_body(resid_ref, kern_ref, out_ref, resid):
    peers, rows, _ = resid_ref.shape
    classes = resid.shape[0]
    fold = classes // rows
    for group in range(peers // fold):
        blocks = regroup([resid_ref[fold * group + k].astype(jnp.float32) for k in range(fold)], fold)
        for q in range(fold):
            resid[rows * q : rows * (q + 1), LANES * group : LANES * (group + 1)] = blocks[q]
    held = resid[...].astype(jnp.bfloat16)
    receivers, height, _ = out_ref.shape
    step = 4 * LANES
    for start in range(0, kern_ref.shape[1], step):
        grad = jnp.dot(held, kern_ref[:, start : start + step], preferred_element_type=jnp.float32)
        for at in range(0, step, LANES):
            halves = [grad[height * h : height * (h + 1), at : at + LANES] for h in range(2)]
            first = 2 * (start + at) // LANES
            for i, block in enumerate(regroup(halves, 2)):
                out_ref[first + i] = block.astype(out_ref.dtype)


def partial_grad(resid_parts, kern, peers):
    batch, centres = kern.shape
    classes = resid_parts.size // batch
    height = classes * (centres // peers) // LANES
    return call(
        grad_body,
        jax.ShapeDtypeStruct((peers, height, LANES), jnp.bfloat16),
        2 * classes * batch * centres,
        resid_parts,
        kern,
        scratch=[pltpu.VMEM((classes, batch), jnp.float32)],
    )


def update_body(rate, arrived_ref, current_ref, new_ref, half_ref):
    peers = arrived_ref.shape[0]
    total = arrived_ref[0].astype(jnp.float32)
    for peer in range(1, peers):
        total = total + arrived_ref[peer].astype(jnp.float32)
    new = current_ref[...] - rate * total
    new_ref[...] = new
    half = new.astype(half_ref.dtype)
    for peer in range(peers):
        half_ref[peer] = half


def updated(arrived, current, rate):
    return call(
        functools.partial(update_body, rate),
        [
            jax.ShapeDtypeStruct(current.shape, jnp.float32),
            jax.ShapeDtypeStruct(arrived.shape, jnp.bfloat16),
        ],
        2 * arrived.size,
        arrived,
        current,
    )


def last_body(rate, arrived_ref, current_ref, new_ref):
    total = arrived_ref[0].astype(jnp.float32)
    for peer in range(1, arrived_ref.shape[0]):
        total = total + arrived_ref[peer].astype(jnp.float32)
    new_ref[...] = current_ref[...] - rate * total


def last_updated(arrived, current, rate):
    return call(
        functools.partial(last_body, rate),
        jax.ShapeDtypeStruct(current.shape, jnp.float32),
        2 * arrived.size,
        arrived,
        current,
    )


def laplace(cross, sample_sq, centre_sq, width):
    mean_sq = (sample_sq[:, None] + centre_sq[None, :] - 2.0 * cross) / width
    return jnp.exp(-jnp.sqrt(mean_sq + EPS) / LENGTH_SCALE).astype(jnp.bfloat16)


def on_device(centres, pool, labels, picks, coefs):
    width = centres.shape[0]
    cen_dev = centres.shape[1]
    pool_dev = pool.shape[1]
    batch_dev = picks.shape[1]
    classes, cen_own = coefs.shape
    n_centre, n_sample = lax.axis_size(CENTRE), lax.axis_size(SAMPLE)
    total_centres = cen_dev * n_centre
    total_batch = batch_dev * n_sample
    rate = STEP_GAIN * LOGIT_GAIN / total_batch
    own = batch_dev // n_centre
    fold = LANES // own
    me = lax.axis_index(CENTRE)
    core = lax.axis_index("core")
    local_picks = picks - lax.axis_index(SAMPLE) * pool_dev
    centre_sq = jnp.sum(jnp.square(centres.astype(jnp.float32)), axis=0)

    def picked(step):
        return jnp.take(pool, local_picks[step], axis=1, mode="clip")

    def own_labels(step):
        chosen = lax.dynamic_slice(local_picks[step], (me * own,), (own,))
        return jnp.take(labels, chosen, mode="clip")

    def kernel_matrix(gathered):
        cross = lax.dot_general(
            gathered, centres, (((0,), (0,)), ((), ())), preferred_element_type=jnp.float32
        )
        sample_sq = jnp.sum(jnp.square(gathered.astype(jnp.float32)), axis=0)
        return laplace(cross, sample_sq, centre_sq, width)

    mine = spread(picked(0), "y")
    other = lax.ppermute(mine, "core", [(0, 1), (1, 0)])
    first = jnp.where(core == 0, mine, other)
    second = jnp.where(core == 0, other, mine)
    later = lax.all_gather(picked(1), CENTRE, axis=0, tiled=True)
    kerns = [
        kernel_matrix(jnp.stack([first, second], axis=1).reshape(width, batch_dev)),
        kernel_matrix(later),
    ]
    labs = [own_labels(step) for step in range(STEPS)]

    current = jnp.concatenate([coefs[: classes // 2], coefs[classes // 2 :]], axis=1)
    half = jnp.broadcast_to(current.astype(jnp.bfloat16), (n_sample, *current.shape))
    for step in range(STEPS):
        coef_parts = exchange(half, SAMPLE)
        arrived = exchange(partial_logits(coef_parts, kerns[step], n_centre), CENTRE)
        resid = residual(arrived, labs[step], LOGIT_GAIN / total_centres, fold)
        arrived = exchange(partial_grad(exchange(resid, CENTRE), kerns[step], n_sample), SAMPLE)
        if step < STEPS - 1:
            current, half = updated(arrived, current, rate)
        else:
            current = last_updated(arrived, current, rate)
    return jnp.concatenate([current[:, :cen_own], current[:, cen_own:]], axis=0)


def solution(mesh):
    sizes = (mesh.shape["centre"] // 2, 2, 8, mesh.shape["sample"] // 8)
    fine = Mesh(mesh.devices.reshape(sizes), (*CENTRE, *SAMPLE))
    placed = (
        P(None, CENTRE),
        P(CENTRE, SAMPLE),
        P(SAMPLE),
        P(None, SAMPLE),
        P(None, (*CENTRE, *SAMPLE)),
    )
    return jax.shard_map(
        on_device,
        mesh=fine,
        in_specs=placed,
        out_specs=P(None, (*CENTRE, *SAMPLE)),
        check_vma=False,
    )
```

```python
import functools

import jax
import jax.numpy as jnp
from jax import lax
from jax.experimental import pallas as pl
from jax.experimental.pallas import tpu as pltpu
from jax.sharding import Mesh, PartitionSpec as P

STEPS = 2


LOGIT_GAIN = 16.0
LENGTH_SCALE = 0.5
STEP_GAIN = 2048.0
EPS = 1e-06

LANES = 128
CENTRE = ("y", "core")
SAMPLE = ("z", "x")


def exchange(parts, axes):
    return lax.all_to_all(parts, axes, 0, 0, tiled=True)


def spread(array, axes):
    peers = lax.axis_size(axes)
    return exchange(jnp.broadcast_to(array[None], (peers, *array.shape)), axes)


def call(body, out, flops, *operands, scratch=()):
    vmem = pl.BlockSpec(memory_space=pltpu.VMEM)
    many = isinstance(out, (list, tuple))
    nbytes = sum(a.size * a.dtype.itemsize for a in operands)
    return pl.pallas_call(
        body,
        out_shape=out,
        in_specs=[vmem] * len(operands),
        out_specs=[vmem] * len(out) if many else vmem,
        scratch_shapes=list(scratch),
        cost_estimate=pl.CostEstimate(flops=flops, bytes_accessed=nbytes, transcendentals=0),
        compiler_params=pltpu.CompilerParams(vmem_limit_bytes=24 << 20),
    )(*operands)


def regroup(blocks, fold):
    width = LANES // fold
    lane_block = lax.broadcasted_iota(jnp.int32, blocks[0].shape, 1) // width
    out = []
    for q in range(fold):
        merged = None
        for k in range(fold):
            shift = width * (k - q) % LANES
            moved = pltpu.roll(blocks[k], shift, 1) if shift else blocks[k]
            merged = moved if merged is None else jnp.where(lane_block == k, moved, merged)
        out.append(merged)
    return out


def logits_body(coef_ref, kern_ref, out_ref, coef, logits):
    over_x, over_z, height, _ = coef_ref.shape
    for pair in range(over_x * over_z // 2):
        at = [divmod(2 * pair + i, over_x) for i in range(2)]
        halves = regroup([coef_ref[x, z].astype(jnp.float32) for z, x in at], 2)
        for h in range(2):
            coef[height * h : height * (h + 1), LANES * pair : LANES * (pair + 1)] = halves[h]
    logits[...] = lax.dot_general(
        coef[...].astype(jnp.bfloat16),
        kern_ref[...],
        (((1,), (1,)), ((), ())),
        preferred_element_type=jnp.float32,
    )
    receivers, rows, _ = out_ref.shape
    fold = coef.shape[0] // rows
    for group in range(receivers // fold):
        columns = slice(LANES * group, LANES * (group + 1))
        blocks = regroup([logits[rows * q : rows * (q + 1), columns] for q in range(fold)], fold)
        for k in range(fold):
            out_ref[fold * group + k] = blocks[k].astype(out_ref.dtype)


def partial_logits(coef_parts, kern, peers):
    classes = 2 * coef_parts.shape[2]
    batch, centres = kern.shape
    rows = classes * (batch // peers) // LANES
    return call(
        logits_body,
        jax.ShapeDtypeStruct((peers, rows, LANES), jnp.bfloat16),
        2 * classes * batch * centres,
        coef_parts,
        kern,
        scratch=[pltpu.VMEM((classes, centres), jnp.float32), pltpu.VMEM((classes, batch), jnp.float32)],
    )


def fold_all(row, fold, op):
    while fold > 1:
        row = op(row, pltpu.roll(row, LANES // fold, 1))
        fold //= 2
    return row


def residual_body(gain, fold, arrived_ref, labs_ref, out_ref):
    peers, rows, _ = arrived_ref.shape
    total = arrived_ref[0].astype(jnp.float32)
    for peer in range(1, peers):
        total = total + arrived_ref[peer].astype(jnp.float32)
    logits = total * gain
    top = fold_all(jnp.max(logits, axis=0, keepdims=True), fold, jnp.maximum)
    expo = jnp.exp(logits - top)
    mass = fold_all(jnp.sum(expo, axis=0, keepdims=True), fold, jnp.add)
    probs = expo / mass
    block = lax.broadcasted_iota(jnp.int32, logits.shape, 1) // (LANES // fold)
    class_ids = block * rows + lax.broadcasted_iota(jnp.int32, logits.shape, 0)
    onehot = (class_ids == labs_ref[...]).astype(jnp.float32)
    resid = (probs - onehot).astype(out_ref.dtype)
    for peer in range(peers):
        out_ref[peer] = resid


def residual(arrived, labs, gain, fold):
    return call(
        functools.partial(residual_body, gain, fold),
        jax.ShapeDtypeStruct(arrived.shape, jnp.bfloat16),
        8 * arrived.size,
        arrived,
        jnp.tile(labs, fold)[None],
    )


def grad_body(resid_ref, kern_ref, out_ref, resid):
    peers, rows, _ = resid_ref.shape
    classes = resid.shape[0]
    fold = classes // rows
    for group in range(peers // fold):
        blocks = regroup([resid_ref[fold * group + k].astype(jnp.float32) for k in range(fold)], fold)
        for q in range(fold):
            resid[rows * q : rows * (q + 1), LANES * group : LANES * (group + 1)] = blocks[q]
    held = resid[...].astype(jnp.bfloat16)
    over_x, _, height, _ = out_ref.shape
    step = 4 * LANES
    for start in range(0, kern_ref.shape[1], step):
        grad = jnp.dot(held, kern_ref[:, start : start + step], preferred_element_type=jnp.float32)
        for at in range(0, step, LANES):
            halves = [grad[height * h : height * (h + 1), at : at + LANES] for h in range(2)]
            first = 2 * (start + at) // LANES
            for i, block in enumerate(regroup(halves, 2)):
                z, x = divmod(first + i, over_x)
                out_ref[x, z] = block.astype(out_ref.dtype)


def partial_grad(resid_parts, kern, over_x, over_z):
    batch, centres = kern.shape
    classes = resid_parts.size // batch
    height = classes * (centres // (over_x * over_z)) // LANES
    return call(
        grad_body,
        jax.ShapeDtypeStruct((over_x, over_z, height, LANES), jnp.bfloat16),
        2 * classes * batch * centres,
        resid_parts,
        kern,
        scratch=[pltpu.VMEM((classes, batch), jnp.float32)],
    )


def merged_body(arrived_ref, out_ref):
    for z in range(arrived_ref.shape[1]):
        total = arrived_ref[0, z].astype(jnp.float32)
        for peer in range(1, arrived_ref.shape[0]):
            total = total + arrived_ref[peer, z].astype(jnp.float32)
        out_ref[z] = total.astype(out_ref.dtype)


def merged(arrived):
    out = jax.ShapeDtypeStruct(arrived.shape[1:], jnp.bfloat16)
    return call(merged_body, out, arrived.size, arrived)


def assemble_body(offsets, mine_ref, other_ref, out_ref, square_ref):
    y, core = lax.axis_index("y"), lax.axis_index("core")
    total = None
    for i in range(mine_ref.shape[0]):
        at = i if offsets is None else lax.bitwise_xor(y, offsets[i])
        for which, ref in ((core, mine_ref), (1 - core, other_ref)):
            block = ref[i]
            out_ref[at, which] = block
            wide = block.astype(jnp.float32)
            square = jnp.sum(wide * wide, axis=0, keepdims=True)
            total = square if total is None else total + square
    square_ref[...] = total


def assembled(mine, other, offsets=None):
    blocks, rows, batch = mine.shape
    feats, squares = call(
        functools.partial(assemble_body, offsets),
        [
            jax.ShapeDtypeStruct((blocks, 2, rows, batch), mine.dtype),
            jax.ShapeDtypeStruct((1, batch), jnp.float32),
        ],
        4 * mine.size,
        mine,
        other,
    )
    return feats.reshape(blocks * 2 * rows, batch), squares[0]


def gathered_by_swaps(block):
    held, offsets = block[None], [0]
    peers = lax.axis_size("y")
    hop = peers // 2
    while hop:
        moved = lax.ppermute(held, "y", [(i, i ^ hop) for i in range(peers)])
        held = jnp.concatenate([held, moved])
        offsets = offsets + [o ^ hop for o in offsets]
        hop //= 2
    other = lax.ppermute(held, "core", [(0, 1), (1, 0)])
    return assembled(held, other, offsets)


def update_body(rate, arrived_ref, current_ref, new_ref, half_ref):
    peers = arrived_ref.shape[0]
    total = arrived_ref[0].astype(jnp.float32)
    for peer in range(1, peers):
        total = total + arrived_ref[peer].astype(jnp.float32)
    new = current_ref[...] - rate * total
    new_ref[...] = new
    half = new.astype(half_ref.dtype)
    for peer in range(peers):
        half_ref[peer] = half


def updated(arrived, current, rate):
    return call(
        functools.partial(update_body, rate),
        [
            jax.ShapeDtypeStruct(current.shape, jnp.float32),
            jax.ShapeDtypeStruct(arrived.shape, jnp.bfloat16),
        ],
        2 * arrived.size,
        arrived,
        current,
    )


def last_body(rate, arrived_ref, current_ref, new_ref):
    total = arrived_ref[0].astype(jnp.float32)
    for peer in range(1, arrived_ref.shape[0]):
        total = total + arrived_ref[peer].astype(jnp.float32)
    new_ref[...] = current_ref[...] - rate * total


def last_updated(arrived, current, rate):
    return call(
        functools.partial(last_body, rate),
        jax.ShapeDtypeStruct(current.shape, jnp.float32),
        2 * arrived.size,
        arrived,
        current,
    )


def laplace(cross, sample_sq, centre_sq, width):
    mean_sq = (sample_sq[:, None] + centre_sq[None, :] - 2.0 * cross) / width
    return jnp.exp(-jnp.sqrt(mean_sq + EPS) / LENGTH_SCALE).astype(jnp.bfloat16)


def on_device(centres, pool, labels, picks, coefs):
    width = centres.shape[0]
    cen_dev = centres.shape[1]
    pool_dev = pool.shape[1]
    batch_dev = picks.shape[1]
    classes, cen_own = coefs.shape
    n_centre, n_sample = lax.axis_size(CENTRE), lax.axis_size(SAMPLE)
    total_centres = cen_dev * n_centre
    total_batch = batch_dev * n_sample
    rate = STEP_GAIN * LOGIT_GAIN / total_batch
    own = batch_dev // n_centre
    fold = LANES // own
    me = lax.axis_index(CENTRE)
    over_z, over_x = lax.axis_size("z"), lax.axis_size("x")
    local_picks = picks - lax.axis_index(SAMPLE) * pool_dev
    centre_sq = jnp.sum(jnp.square(centres.astype(jnp.float32)), axis=0)

    def picked(step):
        return jnp.take(pool, local_picks[step], axis=1, mode="clip")

    def own_labels(step):
        chosen = lax.dynamic_slice(local_picks[step], (me * own,), (own,))
        return jnp.take(labels, chosen, mode="clip")

    def kernel_matrix(gathered, sample_sq):
        cross = lax.dot_general(
            gathered, centres, (((0,), (0,)), ((), ())), preferred_element_type=jnp.float32
        )
        return laplace(cross, sample_sq, centre_sq, width)

    mine = spread(picked(0), "y")
    other = lax.ppermute(mine, "core", [(0, 1), (1, 0)])
    kerns = [
        kernel_matrix(*assembled(mine, other)),
        kernel_matrix(*gathered_by_swaps(picked(1))),
    ]
    labs = [own_labels(step) for step in range(STEPS)]

    current = jnp.concatenate([coefs[: classes // 2], coefs[classes // 2 :]], axis=1)
    half = jnp.broadcast_to(current.astype(jnp.bfloat16), (over_z, *current.shape))
    for step in range(STEPS):
        coef_parts = spread(exchange(half, "z"), "x").reshape(over_x, over_z, *current.shape)
        arrived = exchange(partial_logits(coef_parts, kerns[step], n_centre), CENTRE)
        resid = residual(arrived, labs[step], LOGIT_GAIN / total_centres, fold)
        grads = partial_grad(exchange(resid, CENTRE), kerns[step], over_x, over_z)
        arrived = exchange(merged(exchange(grads, "x")), "z")
        if step < STEPS - 1:
            current, half = updated(arrived, current, rate)
        else:
            current = last_updated(arrived, current, rate)
    return jnp.concatenate([current[:, :cen_own], current[:, cen_own:]], axis=0)


def solution(mesh):
    sizes = (mesh.shape["centre"] // 2, 2, 8, mesh.shape["sample"] // 8)
    fine = Mesh(mesh.devices.reshape(sizes), (*CENTRE, *SAMPLE))
    placed = (
        P(None, CENTRE),
        P(CENTRE, SAMPLE),
        P(SAMPLE),
        P(None, SAMPLE),
        P(None, (*CENTRE, *SAMPLE)),
    )
    return jax.shard_map(
        on_device,
        mesh=fine,
        in_specs=placed,
        out_specs=P(None, (*CENTRE, *SAMPLE)),
        check_vma=False,
    )
```

```python
import functools

import jax
import jax.numpy as jnp
from jax import lax
from jax.experimental import pallas as pl
from jax.experimental.pallas import tpu as pltpu
from jax.sharding import Mesh, PartitionSpec as P

STEPS = 2


LOGIT_GAIN = 16.0
LENGTH_SCALE = 0.5
STEP_GAIN = 2048.0
EPS = 1e-06

LANES = 128
CENTRE = ("y", "core")
SAMPLE = ("z", "x")


def exchange(parts, axes):
    return lax.all_to_all(parts, axes, 0, 0, tiled=True)


def spread(array, axes):
    peers = lax.axis_size(axes)
    return exchange(jnp.broadcast_to(array[None], (peers, *array.shape)), axes)


def call(body, out, flops, *operands, scratch=()):
    vmem = pl.BlockSpec(memory_space=pltpu.VMEM)
    many = isinstance(out, (list, tuple))
    nbytes = sum(a.size * a.dtype.itemsize for a in operands)
    return pl.pallas_call(
        body,
        out_shape=out,
        in_specs=[vmem] * len(operands),
        out_specs=[vmem] * len(out) if many else vmem,
        scratch_shapes=list(scratch),
        cost_estimate=pl.CostEstimate(flops=flops, bytes_accessed=nbytes, transcendentals=0),
        compiler_params=pltpu.CompilerParams(vmem_limit_bytes=24 << 20),
    )(*operands)


def regroup(blocks, fold):
    width = LANES // fold
    lane_block = lax.broadcasted_iota(jnp.int32, blocks[0].shape, 1) // width
    out = []
    for q in range(fold):
        merged = None
        for k in range(fold):
            shift = width * (k - q) % LANES
            moved = pltpu.roll(blocks[k], shift, 1) if shift else blocks[k]
            merged = moved if merged is None else jnp.where(lane_block == k, moved, merged)
        out.append(merged)
    return out


def logits_body(offsets, coef_ref, kern_ref, out_ref, coef, logits):
    over_z, over_x, height, _ = coef_ref.shape
    if offsets is not None:
        over_z, over_x = over_x, over_z
    for i in range(over_z):
        for p in range(over_x // 2):
            if offsets is None:
                pair = coef_ref[i, 2 * p], coef_ref[i, 2 * p + 1]
                at = LANES * (i * over_x // 2 + p)
            else:
                pair = coef_ref[2 * p, i], coef_ref[2 * p + 1, i]
                at = LANES * (lax.bitwise_xor(lax.axis_index("z"), offsets[i]) * (over_x // 2) + p)
                at = pl.multiple_of(at, LANES)
            halves = regroup([block.astype(jnp.float32) for block in pair], 2)
            for h in range(2):
                coef[height * h : height * (h + 1), pl.ds(at, LANES)] = halves[h]
    logits[...] = lax.dot_general(
        coef[...].astype(jnp.bfloat16),
        kern_ref[...],
        (((1,), (1,)), ((), ())),
        preferred_element_type=jnp.float32,
    )
    receivers, rows, _ = out_ref.shape
    fold = coef.shape[0] // rows
    for group in range(receivers // fold):
        columns = slice(LANES * group, LANES * (group + 1))
        blocks = regroup([logits[rows * q : rows * (q + 1), columns] for q in range(fold)], fold)
        for k in range(fold):
            out_ref[fold * group + k] = blocks[k].astype(out_ref.dtype)


def partial_logits(coef_parts, kern, peers, offsets=None):
    classes = 2 * coef_parts.shape[2]
    batch, centres = kern.shape
    rows = classes * (batch // peers) // LANES
    return call(
        functools.partial(logits_body, offsets),
        jax.ShapeDtypeStruct((peers, rows, LANES), jnp.bfloat16),
        2 * classes * batch * centres,
        coef_parts,
        kern,
        scratch=[pltpu.VMEM((classes, centres), jnp.float32), pltpu.VMEM((classes, batch), jnp.float32)],
    )


def fold_all(row, fold, op):
    while fold > 1:
        row = op(row, pltpu.roll(row, LANES // fold, 1))
        fold //= 2
    return row


def residual_body(gain, fold, arrived_ref, labs_ref, out_ref):
    peers, rows, _ = arrived_ref.shape
    total = arrived_ref[0].astype(jnp.float32)
    for peer in range(1, peers):
        total = total + arrived_ref[peer].astype(jnp.float32)
    logits = total * gain
    top = fold_all(jnp.max(logits, axis=0, keepdims=True), fold, jnp.maximum)
    expo = jnp.exp(logits - top)
    mass = fold_all(jnp.sum(expo, axis=0, keepdims=True), fold, jnp.add)
    probs = expo / mass
    block = lax.broadcasted_iota(jnp.int32, logits.shape, 1) // (LANES // fold)
    class_ids = block * rows + lax.broadcasted_iota(jnp.int32, logits.shape, 0)
    onehot = (class_ids == labs_ref[...]).astype(jnp.float32)
    resid = (probs - onehot).astype(out_ref.dtype)
    for peer in range(peers):
        out_ref[peer] = resid


def residual(arrived, labs, gain, fold):
    return call(
        functools.partial(residual_body, gain, fold),
        jax.ShapeDtypeStruct(arrived.shape, jnp.bfloat16),
        8 * arrived.size,
        arrived,
        jnp.tile(labs, fold)[None],
    )


def grad_body(resid_ref, kern_ref, out_ref, resid):
    peers, rows, _ = resid_ref.shape
    classes = resid.shape[0]
    fold = classes // rows
    for group in range(peers // fold):
        blocks = regroup([resid_ref[fold * group + k].astype(jnp.float32) for k in range(fold)], fold)
        for q in range(fold):
            resid[rows * q : rows * (q + 1), LANES * group : LANES * (group + 1)] = blocks[q]
    held = resid[...].astype(jnp.bfloat16)
    _, height, _ = out_ref.shape
    step = 4 * LANES
    for start in range(0, kern_ref.shape[1], step):
        grad = jnp.dot(held, kern_ref[:, start : start + step], preferred_element_type=jnp.float32)
        for at in range(0, step, LANES):
            halves = [grad[height * h : height * (h + 1), at : at + LANES] for h in range(2)]
            first = 2 * (start + at) // LANES
            for i, block in enumerate(regroup(halves, 2)):
                out_ref[first + i] = block.astype(out_ref.dtype)


def partial_grad(resid_parts, kern, peers):
    batch, centres = kern.shape
    classes = resid_parts.size // batch
    height = classes * (centres // peers) // LANES
    return call(
        grad_body,
        jax.ShapeDtypeStruct((peers, height, LANES), jnp.bfloat16),
        2 * classes * batch * centres,
        resid_parts,
        kern,
        scratch=[pltpu.VMEM((classes, batch), jnp.float32)],
    )


def assemble_body(offsets, mine_ref, other_ref, out_ref, square_ref):
    y, core = lax.axis_index("y"), lax.axis_index("core")
    total = None
    for i in range(mine_ref.shape[0]):
        at = i if offsets is None else lax.bitwise_xor(y, offsets[i])
        for which, ref in ((core, mine_ref), (1 - core, other_ref)):
            block = ref[i]
            out_ref[at, which] = block
            wide = block.astype(jnp.float32)
            square = jnp.sum(wide * wide, axis=0, keepdims=True)
            total = square if total is None else total + square
    square_ref[...] = total


def assembled(mine, other, offsets=None):
    blocks, rows, batch = mine.shape
    feats, squares = call(
        functools.partial(assemble_body, offsets),
        [
            jax.ShapeDtypeStruct((blocks, 2, rows, batch), mine.dtype),
            jax.ShapeDtypeStruct((1, batch), jnp.float32),
        ],
        4 * mine.size,
        mine,
        other,
    )
    return feats.reshape(blocks * 2 * rows, batch), squares[0]


def doubled(block, axis):
    held, offsets = block[None], [0]
    peers = lax.axis_size(axis)
    hop = peers // 2
    while hop:
        moved = lax.ppermute(held, axis, [(i, i ^ hop) for i in range(peers)])
        held = jnp.concatenate([held, moved])
        offsets = offsets + [o ^ hop for o in offsets]
        hop //= 2
    return held, offsets


def swapped_cores(array):
    return lax.ppermute(array, "core", [(0, 1), (1, 0)])


def pick_body(step, pool_ref, picks_ref, out_ref):
    pool_dev = pool_ref.shape[1]
    first = (lax.axis_index("z") * lax.axis_size("x") + lax.axis_index("x")) * pool_dev
    chosen = picks_ref[step : step + 1, :] - first
    rows = lax.broadcasted_iota(jnp.int32, (pool_dev, chosen.shape[1]), 0)
    onehot = (rows == chosen).astype(jnp.float32).astype(jnp.bfloat16)
    feats = jnp.dot(pool_ref[...], onehot, preferred_element_type=jnp.float32).astype(out_ref.dtype)
    for peer in range(out_ref.shape[0]):
        out_ref[peer] = feats


def picked(pool, picks, step, copies):
    feats, batch = pool.shape[0], picks.shape[1]
    return call(
        functools.partial(pick_body, step),
        jax.ShapeDtypeStruct((copies, feats, batch), pool.dtype),
        2 * pool.size * batch,
        pool,
        picks,
    )


def update_body(rate, arrived_ref, current_ref, new_ref, half_ref):
    peers = arrived_ref.shape[0]
    total = arrived_ref[0].astype(jnp.float32)
    for peer in range(1, peers):
        total = total + arrived_ref[peer].astype(jnp.float32)
    new = current_ref[...] - rate * total
    new_ref[...] = new
    half = new.astype(half_ref.dtype)
    for peer in range(peers):
        half_ref[peer] = half


def updated(arrived, current, rate):
    return call(
        functools.partial(update_body, rate),
        [
            jax.ShapeDtypeStruct(current.shape, jnp.float32),
            jax.ShapeDtypeStruct(arrived.shape, jnp.bfloat16),
        ],
        2 * arrived.size,
        arrived,
        current,
    )


def last_body(rate, arrived_ref, current_ref, new_ref):
    total = arrived_ref[0].astype(jnp.float32)
    for peer in range(1, arrived_ref.shape[0]):
        total = total + arrived_ref[peer].astype(jnp.float32)
    new_ref[...] = current_ref[...] - rate * total


def last_updated(arrived, current, rate):
    return call(
        functools.partial(last_body, rate),
        jax.ShapeDtypeStruct(current.shape, jnp.float32),
        2 * arrived.size,
        arrived,
        current,
    )


def laplace(cross, sample_sq, centre_sq, width):
    mean_sq = (sample_sq[:, None] + centre_sq[None, :] - 2.0 * cross) / width
    return jnp.exp(-jnp.sqrt(mean_sq + EPS) / LENGTH_SCALE).astype(jnp.bfloat16)


def on_device(centres, pool, labels, picks, coefs):
    width = centres.shape[0]
    cen_dev = centres.shape[1]
    pool_dev = pool.shape[1]
    batch_dev = picks.shape[1]
    classes, cen_own = coefs.shape
    n_centre, n_sample = lax.axis_size(CENTRE), lax.axis_size(SAMPLE)
    total_centres = cen_dev * n_centre
    total_batch = batch_dev * n_sample
    rate = STEP_GAIN * LOGIT_GAIN / total_batch
    own = batch_dev // n_centre
    fold = LANES // own
    me = lax.axis_index(CENTRE)
    over_z, over_x = lax.axis_size("z"), lax.axis_size("x")
    local_picks = picks - lax.axis_index(SAMPLE) * pool_dev
    centre_sq = jnp.sum(jnp.square(centres.astype(jnp.float32)), axis=0)

    def own_labels(step):
        chosen = lax.dynamic_slice(local_picks[step], (me * own,), (own,))
        return jnp.take(labels, chosen, mode="clip")

    def kernel_matrix(gathered, sample_sq):
        cross = lax.dot_general(
            gathered, centres, (((0,), (0,)), ((), ())), preferred_element_type=jnp.float32
        )
        return laplace(cross, sample_sq, centre_sq, width)

    mine = exchange(picked(pool, picks, 0, lax.axis_size("y")), "y")
    later, offsets = doubled(picked(pool, picks, 1, 1)[0], "y")
    kerns = [
        kernel_matrix(*assembled(mine, swapped_cores(mine))),
        kernel_matrix(*assembled(later, swapped_cores(later), offsets)),
    ]
    labs = [own_labels(step) for step in range(STEPS)]

    current = jnp.concatenate([coefs[: classes // 2], coefs[classes // 2 :]], axis=1)
    held, offsets = doubled(current.astype(jnp.bfloat16), "z")
    coef_parts = spread(held, "x")
    for step in range(STEPS):
        if step > 0:
            coef_parts = exchange(half, SAMPLE).reshape(over_z, over_x, *current.shape)
            offsets = None
        arrived = exchange(partial_logits(coef_parts, kerns[step], n_centre, offsets), CENTRE)
        resid = residual(arrived, labs[step], LOGIT_GAIN / total_centres, fold)
        arrived = exchange(partial_grad(exchange(resid, CENTRE), kerns[step], n_sample), SAMPLE)
        if step < STEPS - 1:
            current, half = updated(arrived, current, rate)
        else:
            current = last_updated(arrived, current, rate)
    return jnp.concatenate([current[:, :cen_own], current[:, cen_own:]], axis=0)


def solution(mesh):
    sizes = (mesh.shape["centre"] // 2, 2, 8, mesh.shape["sample"] // 8)
    fine = Mesh(mesh.devices.reshape(sizes), (*CENTRE, *SAMPLE))
    placed = (
        P(None, CENTRE),
        P(CENTRE, SAMPLE),
        P(SAMPLE),
        P(None, SAMPLE),
        P(None, (*CENTRE, *SAMPLE)),
    )
    return jax.shard_map(
        on_device,
        mesh=fine,
        in_specs=placed,
        out_specs=P(None, (*CENTRE, *SAMPLE)),
        check_vma=False,
    )
```

```python
import functools

import jax
import jax.numpy as jnp
from jax import lax
from jax.experimental import pallas as pl
from jax.experimental.pallas import tpu as pltpu
from jax.sharding import Mesh, PartitionSpec as P

STEPS = 2


LOGIT_GAIN = 16.0
LENGTH_SCALE = 0.5
STEP_GAIN = 2048.0
EPS = 1e-06

LANES = 128
CENTRE = ("y", "core")
SAMPLE = ("z", "x")


def exchange(parts, axes):
    return lax.all_to_all(parts, axes, 0, 0, tiled=True)


def spread(array, axes):
    peers = lax.axis_size(axes)
    return exchange(jnp.broadcast_to(array[None], (peers, *array.shape)), axes)


def call(body, out, flops, *operands, scratch=()):
    vmem = pl.BlockSpec(memory_space=pltpu.VMEM)
    many = isinstance(out, (list, tuple))
    nbytes = sum(a.size * a.dtype.itemsize for a in operands)
    return pl.pallas_call(
        body,
        out_shape=out,
        in_specs=[vmem] * len(operands),
        out_specs=[vmem] * len(out) if many else vmem,
        scratch_shapes=list(scratch),
        cost_estimate=pl.CostEstimate(flops=flops, bytes_accessed=nbytes, transcendentals=0),
        compiler_params=pltpu.CompilerParams(vmem_limit_bytes=24 << 20),
    )(*operands)


def regroup(blocks, fold):
    width = LANES // fold
    lane_block = lax.broadcasted_iota(jnp.int32, blocks[0].shape, 1) // width
    out = []
    for q in range(fold):
        merged = None
        for k in range(fold):
            shift = width * (k - q) % LANES
            moved = pltpu.roll(blocks[k], shift, 1) if shift else blocks[k]
            merged = moved if merged is None else jnp.where(lane_block == k, moved, merged)
        out.append(merged)
    return out


def logits_body(offsets, coef_ref, kern_ref, out_ref, coef, logits):
    over_z, over_x, height, _ = coef_ref.shape
    if offsets is not None:
        over_z, over_x = over_x, over_z
    for i in range(over_z):
        for p in range(over_x // 2):
            if offsets is None:
                pair = coef_ref[i, 2 * p], coef_ref[i, 2 * p + 1]
                at = LANES * (i * over_x // 2 + p)
            else:
                pair = coef_ref[2 * p, i], coef_ref[2 * p + 1, i]
                at = LANES * (lax.bitwise_xor(lax.axis_index("z"), offsets[i]) * (over_x // 2) + p)
                at = pl.multiple_of(at, LANES)
            halves = regroup([block.astype(jnp.float32) for block in pair], 2)
            for h in range(2):
                coef[height * h : height * (h + 1), pl.ds(at, LANES)] = halves[h]
    logits[...] = lax.dot_general(
        coef[...].astype(jnp.bfloat16),
        kern_ref[...],
        (((1,), (1,)), ((), ())),
        preferred_element_type=jnp.float32,
    )
    receivers, rows, _ = out_ref.shape
    fold = coef.shape[0] // rows
    for group in range(receivers // fold):
        columns = slice(LANES * group, LANES * (group + 1))
        blocks = regroup([logits[rows * q : rows * (q + 1), columns] for q in range(fold)], fold)
        for k in range(fold):
            out_ref[fold * group + k] = blocks[k].astype(out_ref.dtype)


def partial_logits(coef_parts, kern, peers, offsets=None):
    classes = 2 * coef_parts.shape[2]
    batch, centres = kern.shape
    rows = classes * (batch // peers) // LANES
    return call(
        functools.partial(logits_body, offsets),
        jax.ShapeDtypeStruct((peers, rows, LANES), jnp.bfloat16),
        2 * classes * batch * centres,
        coef_parts,
        kern,
        scratch=[pltpu.VMEM((classes, centres), jnp.float32), pltpu.VMEM((classes, batch), jnp.float32)],
    )


def fold_all(row, fold, op):
    while fold > 1:
        row = op(row, pltpu.roll(row, LANES // fold, 1))
        fold //= 2
    return row


def residual_body(gain, fold, arrived_ref, labs_ref, out_ref):
    peers, rows, _ = arrived_ref.shape
    total = arrived_ref[0].astype(jnp.float32)
    for peer in range(1, peers):
        total = total + arrived_ref[peer].astype(jnp.float32)
    logits = total * gain
    top = fold_all(jnp.max(logits, axis=0, keepdims=True), fold, jnp.maximum)
    expo = jnp.exp(logits - top)
    mass = fold_all(jnp.sum(expo, axis=0, keepdims=True), fold, jnp.add)
    probs = expo / mass
    block = lax.broadcasted_iota(jnp.int32, logits.shape, 1) // (LANES // fold)
    class_ids = block * rows + lax.broadcasted_iota(jnp.int32, logits.shape, 0)
    onehot = (class_ids == labs_ref[...]).astype(jnp.float32)
    resid = (probs - onehot).astype(out_ref.dtype)
    for peer in range(peers):
        out_ref[peer] = resid


def residual(arrived, labs, gain, fold):
    return call(
        functools.partial(residual_body, gain, fold),
        jax.ShapeDtypeStruct(arrived.shape, jnp.bfloat16),
        8 * arrived.size,
        arrived,
        jnp.tile(labs, fold)[None],
    )


def grad_body(resid_ref, kern_ref, out_ref, resid):
    peers, rows, _ = resid_ref.shape
    classes = resid.shape[0]
    fold = classes // rows
    for group in range(peers // fold):
        blocks = regroup([resid_ref[fold * group + k].astype(jnp.float32) for k in range(fold)], fold)
        for q in range(fold):
            resid[rows * q : rows * (q + 1), LANES * group : LANES * (group + 1)] = blocks[q]
    held = resid[...].astype(jnp.bfloat16)
    _, height, _ = out_ref.shape
    step = 4 * LANES
    for start in range(0, kern_ref.shape[1], step):
        grad = jnp.dot(held, kern_ref[:, start : start + step], preferred_element_type=jnp.float32)
        for at in range(0, step, LANES):
            halves = [grad[height * h : height * (h + 1), at : at + LANES] for h in range(2)]
            first = 2 * (start + at) // LANES
            for i, block in enumerate(regroup(halves, 2)):
                out_ref[first + i] = block.astype(out_ref.dtype)


def partial_grad(resid_parts, kern, peers):
    batch, centres = kern.shape
    classes = resid_parts.size // batch
    height = classes * (centres // peers) // LANES
    return call(
        grad_body,
        jax.ShapeDtypeStruct((peers, height, LANES), jnp.bfloat16),
        2 * classes * batch * centres,
        resid_parts,
        kern,
        scratch=[pltpu.VMEM((classes, batch), jnp.float32)],
    )


def assemble_body(offsets, mine_ref, other_ref, out_ref, square_ref):
    y, core = lax.axis_index("y"), lax.axis_index("core")
    total = None
    for i in range(mine_ref.shape[0]):
        at = i if offsets is None else lax.bitwise_xor(y, offsets[i])
        for which, ref in ((core, mine_ref), (1 - core, other_ref)):
            block = ref[i]
            out_ref[at, which] = block
            wide = block.astype(jnp.float32)
            square = jnp.sum(wide * wide, axis=0, keepdims=True)
            total = square if total is None else total + square
    square_ref[...] = total


def assembled(mine, other, offsets=None):
    blocks, rows, batch = mine.shape
    feats, squares = call(
        functools.partial(assemble_body, offsets),
        [
            jax.ShapeDtypeStruct((blocks, 2, rows, batch), mine.dtype),
            jax.ShapeDtypeStruct((1, batch), jnp.float32),
        ],
        4 * mine.size,
        mine,
        other,
    )
    return feats.reshape(blocks * 2 * rows, batch), squares[0]


def swap_hops(axis):
    hops = [lax.axis_size(axis) // 2]
    while hops[-1] > 1:
        hops.append(hops[-1] // 2)
    return hops


def swap_offsets(axis):
    offsets = [0]
    for hop in swap_hops(axis):
        offsets = offsets + [o ^ hop for o in offsets]
    return offsets


def doubled(held, axis, hop):
    pairs = [(i, i ^ hop) for i in range(lax.axis_size(axis))]
    return jnp.concatenate([held, lax.ppermute(held, axis, pairs)])


def swapped_cores(array):
    return lax.ppermute(array, "core", [(0, 1), (1, 0)])


def pick_body(step, pool_ref, picks_ref, out_ref):
    pool_dev = pool_ref.shape[1]
    first = (lax.axis_index("z") * lax.axis_size("x") + lax.axis_index("x")) * pool_dev
    chosen = picks_ref[step : step + 1, :] - first
    rows = lax.broadcasted_iota(jnp.int32, (pool_dev, chosen.shape[1]), 0)
    onehot = (rows == chosen).astype(jnp.float32).astype(jnp.bfloat16)
    feats = jnp.dot(pool_ref[...], onehot, preferred_element_type=jnp.float32).astype(out_ref.dtype)
    for peer in range(out_ref.shape[0]):
        out_ref[peer] = feats


def picked(pool, picks, step, copies):
    feats, batch = pool.shape[0], picks.shape[1]
    return call(
        functools.partial(pick_body, step),
        jax.ShapeDtypeStruct((copies, feats, batch), pool.dtype),
        2 * pool.size * batch,
        pool,
        picks,
    )


def update_body(rate, arrived_ref, current_ref, new_ref, half_ref):
    peers = arrived_ref.shape[0]
    total = arrived_ref[0].astype(jnp.float32)
    for peer in range(1, peers):
        total = total + arrived_ref[peer].astype(jnp.float32)
    new = current_ref[...] - rate * total
    new_ref[...] = new
    half = new.astype(half_ref.dtype)
    for peer in range(peers):
        half_ref[peer] = half


def updated(arrived, current, rate):
    return call(
        functools.partial(update_body, rate),
        [
            jax.ShapeDtypeStruct(current.shape, jnp.float32),
            jax.ShapeDtypeStruct(arrived.shape, jnp.bfloat16),
        ],
        2 * arrived.size,
        arrived,
        current,
    )


def last_body(rate, arrived_ref, current_ref, new_ref):
    total = arrived_ref[0].astype(jnp.float32)
    for peer in range(1, arrived_ref.shape[0]):
        total = total + arrived_ref[peer].astype(jnp.float32)
    new_ref[...] = current_ref[...] - rate * total


def last_updated(arrived, current, rate):
    return call(
        functools.partial(last_body, rate),
        jax.ShapeDtypeStruct(current.shape, jnp.float32),
        2 * arrived.size,
        arrived,
        current,
    )


def laplace(cross, sample_sq, centre_sq, width):
    mean_sq = (sample_sq[:, None] + centre_sq[None, :] - 2.0 * cross) / width
    return jnp.exp(-jnp.sqrt(mean_sq + EPS) / LENGTH_SCALE).astype(jnp.bfloat16)


def on_device(centres, pool, labels, picks, coefs):
    width = centres.shape[0]
    cen_dev = centres.shape[1]
    pool_dev = pool.shape[1]
    batch_dev = picks.shape[1]
    classes, cen_own = coefs.shape
    n_centre, n_sample = lax.axis_size(CENTRE), lax.axis_size(SAMPLE)
    total_centres = cen_dev * n_centre
    total_batch = batch_dev * n_sample
    rate = STEP_GAIN * LOGIT_GAIN / total_batch
    own = batch_dev // n_centre
    fold = LANES // own
    me = lax.axis_index(CENTRE)
    over_z, over_x = lax.axis_size("z"), lax.axis_size("x")
    local_picks = picks - lax.axis_index(SAMPLE) * pool_dev
    centre_sq = jnp.sum(jnp.square(centres.astype(jnp.float32)), axis=0)

    def own_labels(step):
        chosen = lax.dynamic_slice(local_picks[step], (me * own,), (own,))
        return jnp.take(labels, chosen, mode="clip")

    packed = jnp.concatenate([coefs[: classes // 2], coefs[classes // 2 :]], axis=1)

    def kernel_matrix(gathered, sample_sq):
        cross = lax.dot_general(
            gathered, centres, (((0,), (0,)), ((), ())), preferred_element_type=jnp.float32
        )
        return laplace(cross, sample_sq, centre_sq, width)

    held = packed.astype(jnp.bfloat16)[None]
    held, first_picks = lax.optimization_barrier((held, picks))
    mine = exchange(picked(pool, first_picks, 0, lax.axis_size("y")), "y")
    *far, near = swap_hops("z")
    for hop in far:
        held = doubled(held, "z", hop)
    mine, held, centre_sq = lax.optimization_barrier((mine, held, centre_sq))
    other = swapped_cores(mine)
    held = doubled(held, "z", near)
    kern = kernel_matrix(*assembled(mine, other))
    labs = [own_labels(step) for step in range(STEPS)]

    logits = partial_logits(spread(held, "x"), kern, n_centre, swap_offsets("z"))

    later = picked(pool, picks, 1, 1)
    hops = swap_hops("y")
    gain = LOGIT_GAIN / total_centres

    logits, later = lax.optimization_barrier((logits, later))
    arrived = exchange(logits, CENTRE)
    later = doubled(later, "y", hops[0])
    arrived, later = lax.optimization_barrier((arrived, later))
    resid = residual(arrived, labs[0], gain, fold)
    resid, later = lax.optimization_barrier((resid, later))
    resid = exchange(resid, CENTRE)
    later = doubled(later, "y", hops[1])
    resid, later = lax.optimization_barrier((resid, later))
    grads = partial_grad(resid, kern, n_sample)
    grads, later = lax.optimization_barrier((grads, later))
    arrived = exchange(grads, SAMPLE)
    for hop in hops[2:]:
        later = doubled(later, "y", hop)
    other = swapped_cores(later)
    arrived, later, other = lax.optimization_barrier((arrived, later, other))
    current, half = updated(arrived, packed, rate)

    kern = kernel_matrix(*assembled(later, other, swap_offsets("y")))
    coef_parts = exchange(half, SAMPLE).reshape(over_z, over_x, *current.shape)
    arrived = exchange(partial_logits(coef_parts, kern, n_centre), CENTRE)
    resid = exchange(residual(arrived, labs[1], gain, fold), CENTRE)
    arrived = exchange(partial_grad(resid, kern, n_sample), SAMPLE)
    current = last_updated(arrived, current, rate)
    return jnp.concatenate([current[:, :cen_own], current[:, cen_own:]], axis=0)


def solution(mesh):
    sizes = (mesh.shape["centre"] // 2, 2, 8, mesh.shape["sample"] // 8)
    fine = Mesh(mesh.devices.reshape(sizes), (*CENTRE, *SAMPLE))
    placed = (
        P(None, CENTRE),
        P(CENTRE, SAMPLE),
        P(SAMPLE),
        P(None, SAMPLE),
        P(None, (*CENTRE, *SAMPLE)),
    )
    return jax.shard_map(
        on_device,
        mesh=fine,
        in_specs=placed,
        out_specs=P(None, (*CENTRE, *SAMPLE)),
        check_vma=False,
    )
```

```python
import functools

import jax
import jax.numpy as jnp
from jax import lax
from jax.experimental import pallas as pl
from jax.experimental.pallas import tpu as pltpu
from jax.sharding import Mesh, PartitionSpec as P

STEPS = 2


LOGIT_GAIN = 16.0
LENGTH_SCALE = 0.5
STEP_GAIN = 2048.0
EPS = 1e-06

LANES = 128
CENTRE = ("y", "core")
SAMPLE = ("z", "x")


def exchange(parts, axes):
    return lax.all_to_all(parts, axes, 0, 0, tiled=True)


def spread(array, axes):
    peers = lax.axis_size(axes)
    return exchange(jnp.broadcast_to(array[None], (peers, *array.shape)), axes)


def call(body, out, flops, *operands, scratch=()):
    vmem = pl.BlockSpec(memory_space=pltpu.VMEM)
    many = isinstance(out, (list, tuple))
    nbytes = sum(a.size * a.dtype.itemsize for a in operands)
    return pl.pallas_call(
        body,
        out_shape=out,
        in_specs=[vmem] * len(operands),
        out_specs=[vmem] * len(out) if many else vmem,
        scratch_shapes=list(scratch),
        cost_estimate=pl.CostEstimate(flops=flops, bytes_accessed=nbytes, transcendentals=0),
        compiler_params=pltpu.CompilerParams(vmem_limit_bytes=24 << 20),
    )(*operands)


def regroup(blocks, fold):
    width = LANES // fold
    lane_block = lax.broadcasted_iota(jnp.int32, blocks[0].shape, 1) // width
    out = []
    for q in range(fold):
        merged = None
        for k in range(fold):
            shift = width * (k - q) % LANES
            moved = pltpu.roll(blocks[k], shift, 1) if shift else blocks[k]
            merged = moved if merged is None else jnp.where(lane_block == k, moved, merged)
        out.append(merged)
    return out


def logits_body(offsets, coef_ref, kern_ref, out_ref, coef, logits):
    over_z, over_x, height, _ = coef_ref.shape
    if offsets is not None:
        over_z, over_x = over_x, over_z
    for i in range(over_z):
        for p in range(over_x // 2):
            if offsets is None:
                pair = coef_ref[i, 2 * p], coef_ref[i, 2 * p + 1]
                at = LANES * (i * over_x // 2 + p)
            else:
                pair = coef_ref[2 * p, i], coef_ref[2 * p + 1, i]
                at = LANES * (lax.bitwise_xor(lax.axis_index("z"), offsets[i]) * (over_x // 2) + p)
                at = pl.multiple_of(at, LANES)
            halves = regroup([block.astype(jnp.float32) for block in pair], 2)
            for h in range(2):
                coef[height * h : height * (h + 1), pl.ds(at, LANES)] = halves[h]
    logits[...] = lax.dot_general(
        coef[...].astype(jnp.bfloat16),
        kern_ref[...],
        (((1,), (1,)), ((), ())),
        preferred_element_type=jnp.float32,
    )
    receivers, rows, _ = out_ref.shape
    fold = coef.shape[0] // rows
    for group in range(receivers // fold):
        columns = slice(LANES * group, LANES * (group + 1))
        blocks = regroup([logits[rows * q : rows * (q + 1), columns] for q in range(fold)], fold)
        for k in range(fold):
            out_ref[fold * group + k] = blocks[k].astype(out_ref.dtype)


def partial_logits(coef_parts, kern, peers, offsets=None):
    classes = 2 * coef_parts.shape[2]
    batch, centres = kern.shape
    rows = classes * (batch // peers) // LANES
    return call(
        functools.partial(logits_body, offsets),
        jax.ShapeDtypeStruct((peers, rows, LANES), jnp.bfloat16),
        2 * classes * batch * centres,
        coef_parts,
        kern,
        scratch=[pltpu.VMEM((classes, centres), jnp.float32), pltpu.VMEM((classes, batch), jnp.float32)],
    )


def fold_all(row, fold, op):
    while fold > 1:
        row = op(row, pltpu.roll(row, LANES // fold, 1))
        fold //= 2
    return row


def residual_body(gain, fold, arrived_ref, labs_ref, out_ref):
    peers, rows, _ = arrived_ref.shape
    total = arrived_ref[0].astype(jnp.float32)
    for peer in range(1, peers):
        total = total + arrived_ref[peer].astype(jnp.float32)
    logits = total * gain
    top = fold_all(jnp.max(logits, axis=0, keepdims=True), fold, jnp.maximum)
    expo = jnp.exp(logits - top)
    mass = fold_all(jnp.sum(expo, axis=0, keepdims=True), fold, jnp.add)
    probs = expo / mass
    block = lax.broadcasted_iota(jnp.int32, logits.shape, 1) // (LANES // fold)
    class_ids = block * rows + lax.broadcasted_iota(jnp.int32, logits.shape, 0)
    onehot = (class_ids == labs_ref[...]).astype(jnp.float32)
    resid = (probs - onehot).astype(out_ref.dtype)
    for peer in range(peers):
        out_ref[peer] = resid


def residual(arrived, labs, gain, fold):
    return call(
        functools.partial(residual_body, gain, fold),
        jax.ShapeDtypeStruct(arrived.shape, jnp.bfloat16),
        8 * arrived.size,
        arrived,
        jnp.tile(labs, fold)[None],
    )


def grad_body(resid_ref, kern_ref, out_ref, resid):
    peers, rows, _ = resid_ref.shape
    classes = resid.shape[0]
    fold = classes // rows
    for group in range(peers // fold):
        blocks = regroup([resid_ref[fold * group + k].astype(jnp.float32) for k in range(fold)], fold)
        for q in range(fold):
            resid[rows * q : rows * (q + 1), LANES * group : LANES * (group + 1)] = blocks[q]
    held = resid[...].astype(jnp.bfloat16)
    _, height, _ = out_ref.shape
    step = 4 * LANES
    for start in range(0, kern_ref.shape[1], step):
        grad = jnp.dot(held, kern_ref[:, start : start + step], preferred_element_type=jnp.float32)
        for at in range(0, step, LANES):
            halves = [grad[height * h : height * (h + 1), at : at + LANES] for h in range(2)]
            first = 2 * (start + at) // LANES
            for i, block in enumerate(regroup(halves, 2)):
                out_ref[first + i] = block.astype(out_ref.dtype)


def partial_grad(resid_parts, kern, peers):
    batch, centres = kern.shape
    classes = resid_parts.size // batch
    height = classes * (centres // peers) // LANES
    return call(
        grad_body,
        jax.ShapeDtypeStruct((peers, height, LANES), jnp.bfloat16),
        2 * classes * batch * centres,
        resid_parts,
        kern,
        scratch=[pltpu.VMEM((classes, batch), jnp.float32)],
    )


def assemble_body(offsets, mine_ref, other_ref, out_ref, square_ref):
    y, core = lax.axis_index("y"), lax.axis_index("core")
    total = None
    for i in range(mine_ref.shape[0]):
        at = i if offsets is None else lax.bitwise_xor(y, offsets[i])
        for which, ref in ((core, mine_ref), (1 - core, other_ref)):
            block = ref[i]
            out_ref[at, which] = block
            wide = block.astype(jnp.float32)
            square = jnp.sum(wide * wide, axis=0, keepdims=True)
            total = square if total is None else total + square
    square_ref[...] = total


def assembled(mine, other, offsets=None):
    blocks, rows, batch = mine.shape
    feats, squares = call(
        functools.partial(assemble_body, offsets),
        [
            jax.ShapeDtypeStruct((blocks, 2, rows, batch), mine.dtype),
            jax.ShapeDtypeStruct((1, batch), jnp.float32),
        ],
        4 * mine.size,
        mine,
        other,
    )
    return feats.reshape(blocks * 2 * rows, batch), squares[0]


def swap_offsets(hops):
    offsets = [0]
    for hop in hops:
        offsets = offsets + [o ^ hop for o in offsets]
    return offsets


def doubled(held, axis, hop):
    pairs = [(i, i ^ hop) for i in range(lax.axis_size(axis))]
    return jnp.concatenate([held, lax.ppermute(held, axis, pairs)])


def swapped_cores(array):
    return lax.ppermute(array, "core", [(0, 1), (1, 0)])


def pick_body(step, pool_ref, picks_ref, out_ref):
    pool_dev = pool_ref.shape[1]
    first = (lax.axis_index("z") * lax.axis_size("x") + lax.axis_index("x")) * pool_dev
    chosen = picks_ref[step : step + 1, :] - first
    rows = lax.broadcasted_iota(jnp.int32, (pool_dev, chosen.shape[1]), 0)
    onehot = (rows == chosen).astype(jnp.float32).astype(jnp.bfloat16)
    feats = jnp.dot(pool_ref[...], onehot, preferred_element_type=jnp.float32).astype(out_ref.dtype)
    for peer in range(out_ref.shape[0]):
        out_ref[peer] = feats


def picked(pool, picks, step, copies):
    feats, batch = pool.shape[0], picks.shape[1]
    return call(
        functools.partial(pick_body, step),
        jax.ShapeDtypeStruct((copies, feats, batch), pool.dtype),
        2 * pool.size * batch,
        pool,
        picks,
    )


def update_body(rate, arrived_ref, current_ref, new_ref, half_ref):
    peers = arrived_ref.shape[0]
    total = arrived_ref[0].astype(jnp.float32)
    for peer in range(1, peers):
        total = total + arrived_ref[peer].astype(jnp.float32)
    new = current_ref[...] - rate * total
    new_ref[...] = new
    half = new.astype(half_ref.dtype)
    for peer in range(peers):
        half_ref[peer] = half


def updated(arrived, current, rate):
    return call(
        functools.partial(update_body, rate),
        [
            jax.ShapeDtypeStruct(current.shape, jnp.float32),
            jax.ShapeDtypeStruct(arrived.shape, jnp.bfloat16),
        ],
        2 * arrived.size,
        arrived,
        current,
    )


def last_body(rate, arrived_ref, current_ref, new_ref):
    total = arrived_ref[0].astype(jnp.float32)
    for peer in range(1, arrived_ref.shape[0]):
        total = total + arrived_ref[peer].astype(jnp.float32)
    new_ref[...] = current_ref[...] - rate * total


def last_updated(arrived, current, rate):
    return call(
        functools.partial(last_body, rate),
        jax.ShapeDtypeStruct(current.shape, jnp.float32),
        2 * arrived.size,
        arrived,
        current,
    )


def laplace(cross, sample_sq, centre_sq, width):
    mean_sq = (sample_sq[:, None] + centre_sq[None, :] - 2.0 * cross) / width
    return jnp.exp(-jnp.sqrt(mean_sq + EPS) / LENGTH_SCALE).astype(jnp.bfloat16)


def on_device(centres, pool, labels, picks, coefs):
    width = centres.shape[0]
    cen_dev = centres.shape[1]
    pool_dev = pool.shape[1]
    batch_dev = picks.shape[1]
    classes, cen_own = coefs.shape
    n_centre, n_sample = lax.axis_size(CENTRE), lax.axis_size(SAMPLE)
    total_centres = cen_dev * n_centre
    total_batch = batch_dev * n_sample
    rate = STEP_GAIN * LOGIT_GAIN / total_batch
    own = batch_dev // n_centre
    fold = LANES // own
    me = lax.axis_index(CENTRE)
    over_z, over_x = lax.axis_size("z"), lax.axis_size("x")
    local_picks = picks - lax.axis_index(SAMPLE) * pool_dev
    centre_sq = jnp.sum(jnp.square(centres.astype(jnp.float32)), axis=0)

    def own_labels(step):
        chosen = lax.dynamic_slice(local_picks[step], (me * own,), (own,))
        return jnp.take(labels, chosen, mode="clip")

    packed = jnp.concatenate([coefs[: classes // 2], coefs[classes // 2 :]], axis=1)

    def kernel_matrix(gathered, sample_sq):
        cross = lax.dot_general(
            gathered, centres, (((0,), (0,)), ((), ())), preferred_element_type=jnp.float32
        )
        return laplace(cross, sample_sq, centre_sq, width)

    z_hops = [1 << i for i in range(over_z.bit_length() - 1)]
    y_hops = [1 << i for i in reversed(range(lax.axis_size("y").bit_length() - 1))]
    held = doubled(packed.astype(jnp.bfloat16)[None], "z", z_hops[0])
    mine = picked(pool, picks, 0, lax.axis_size("y"))
    mine, held = lax.optimization_barrier((mine, held))
    mine = exchange(mine, "y")
    for hop in z_hops[1:]:
        held = doubled(held, "z", hop)
    later = doubled(picked(pool, picks, 1, 1), "y", y_hops[0])
    mine, held, later, centre_sq = lax.optimization_barrier((mine, held, later, centre_sq))
    coef_parts = spread(held, "x")
    kern = kernel_matrix(*assembled(mine, swapped_cores(mine)))
    labs = [own_labels(step) for step in range(STEPS)]

    gain = LOGIT_GAIN / total_centres
    logits = partial_logits(coef_parts, kern, n_centre, swap_offsets(z_hops))
    resid = exchange(residual(exchange(logits, CENTRE), labs[0], gain, fold), CENTRE)
    grads = partial_grad(resid, kern, n_sample)
    grads, later = lax.optimization_barrier((grads, later))
    arrived = exchange(grads, SAMPLE)
    for hop in y_hops[1:]:
        later = doubled(later, "y", hop)
    arrived, later = lax.optimization_barrier((arrived, later))
    current, half = updated(arrived, packed, rate)

    kern = kernel_matrix(*assembled(later, swapped_cores(later), swap_offsets(y_hops)))
    coef_parts = exchange(half, SAMPLE).reshape(over_z, over_x, *current.shape)
    arrived = exchange(partial_logits(coef_parts, kern, n_centre), CENTRE)
    resid = exchange(residual(arrived, labs[1], gain, fold), CENTRE)
    arrived = exchange(partial_grad(resid, kern, n_sample), SAMPLE)
    current = last_updated(arrived, current, rate)
    return jnp.concatenate([current[:, :cen_own], current[:, cen_own:]], axis=0)


def solution(mesh):
    sizes = (mesh.shape["centre"] // 2, 2, 8, mesh.shape["sample"] // 8)
    fine = Mesh(mesh.devices.reshape(sizes), (*CENTRE, *SAMPLE))
    placed = (
        P(None, CENTRE),
        P(CENTRE, SAMPLE),
        P(SAMPLE),
        P(None, SAMPLE),
        P(None, (*CENTRE, *SAMPLE)),
    )
    return jax.shard_map(
        on_device,
        mesh=fine,
        in_specs=placed,
        out_specs=P(None, (*CENTRE, *SAMPLE)),
        check_vma=False,
    )
```

```python
import functools

import jax
import jax.numpy as jnp
from jax import lax
from jax.experimental import pallas as pl
from jax.experimental.pallas import tpu as pltpu
from jax.sharding import Mesh, PartitionSpec as P

STEPS = 2


LOGIT_GAIN = 16.0
LENGTH_SCALE = 0.5
STEP_GAIN = 2048.0
EPS = 1e-06

LANES = 128
CENTRE = ("y", "core")
SAMPLE = ("z", "x")


def exchange(parts, axes):
    return lax.all_to_all(parts, axes, 0, 0, tiled=True)


def spread(array, axes):
    peers = lax.axis_size(axes)
    return exchange(jnp.broadcast_to(array[None], (peers, *array.shape)), axes)


def call(body, out, flops, *operands, scratch=()):
    vmem = pl.BlockSpec(memory_space=pltpu.VMEM)
    many = isinstance(out, (list, tuple))
    nbytes = sum(a.size * a.dtype.itemsize for a in operands)
    return pl.pallas_call(
        body,
        out_shape=out,
        in_specs=[vmem] * len(operands),
        out_specs=[vmem] * len(out) if many else vmem,
        scratch_shapes=list(scratch),
        cost_estimate=pl.CostEstimate(flops=flops, bytes_accessed=nbytes, transcendentals=0),
        compiler_params=pltpu.CompilerParams(vmem_limit_bytes=24 << 20),
    )(*operands)


def regroup(blocks, fold):
    width = LANES // fold
    lane_block = lax.broadcasted_iota(jnp.int32, blocks[0].shape, 1) // width
    out = []
    for q in range(fold):
        merged = None
        for k in range(fold):
            shift = width * (k - q) % LANES
            moved = pltpu.roll(blocks[k], shift, 1) if shift else blocks[k]
            merged = moved if merged is None else jnp.where(lane_block == k, moved, merged)
        out.append(merged)
    return out


def logits_body(offsets, coef_ref, kern_ref, out_ref, coef, logits):
    over_z, over_x, height, _ = coef_ref.shape
    if offsets is not None:
        over_z, over_x = over_x, over_z
    for i in range(over_z):
        for p in range(over_x // 2):
            if offsets is None:
                pair = coef_ref[i, 2 * p], coef_ref[i, 2 * p + 1]
                at = LANES * (i * over_x // 2 + p)
            else:
                pair = coef_ref[2 * p, i], coef_ref[2 * p + 1, i]
                at = LANES * (lax.bitwise_xor(lax.axis_index("z"), offsets[i]) * (over_x // 2) + p)
                at = pl.multiple_of(at, LANES)
            halves = regroup([block.astype(jnp.float32) for block in pair], 2)
            for h in range(2):
                coef[height * h : height * (h + 1), pl.ds(at, LANES)] = halves[h]
    logits[...] = lax.dot_general(
        coef[...].astype(jnp.bfloat16),
        kern_ref[...],
        (((1,), (1,)), ((), ())),
        preferred_element_type=jnp.float32,
    )
    receivers, rows, _ = out_ref.shape
    fold = coef.shape[0] // rows
    for group in range(receivers // fold):
        columns = slice(LANES * group, LANES * (group + 1))
        blocks = regroup([logits[rows * q : rows * (q + 1), columns] for q in range(fold)], fold)
        for k in range(fold):
            out_ref[fold * group + k] = blocks[k].astype(out_ref.dtype)


def partial_logits(coef_parts, kern, peers, offsets=None):
    classes = 2 * coef_parts.shape[2]
    batch, centres = kern.shape
    rows = classes * (batch // peers) // LANES
    return call(
        functools.partial(logits_body, offsets),
        jax.ShapeDtypeStruct((peers, rows, LANES), jnp.bfloat16),
        2 * classes * batch * centres,
        coef_parts,
        kern,
        scratch=[pltpu.VMEM((classes, centres), jnp.float32), pltpu.VMEM((classes, batch), jnp.float32)],
    )


def fold_all(row, fold, op):
    while fold > 1:
        row = op(row, pltpu.roll(row, LANES // fold, 1))
        fold //= 2
    return row


def residual_body(gain, fold, arrived_ref, labs_ref, out_ref):
    peers, rows, _ = arrived_ref.shape
    total = arrived_ref[0].astype(jnp.float32)
    for peer in range(1, peers):
        total = total + arrived_ref[peer].astype(jnp.float32)
    logits = total * gain
    top = fold_all(jnp.max(logits, axis=0, keepdims=True), fold, jnp.maximum)
    expo = jnp.exp(logits - top)
    mass = fold_all(jnp.sum(expo, axis=0, keepdims=True), fold, jnp.add)
    probs = expo / mass
    block = lax.broadcasted_iota(jnp.int32, logits.shape, 1) // (LANES // fold)
    class_ids = block * rows + lax.broadcasted_iota(jnp.int32, logits.shape, 0)
    onehot = (class_ids == labs_ref[...]).astype(jnp.float32)
    resid = (probs - onehot).astype(out_ref.dtype)
    for peer in range(peers):
        out_ref[peer] = resid


def residual(arrived, labs, gain, fold):
    return call(
        functools.partial(residual_body, gain, fold),
        jax.ShapeDtypeStruct(arrived.shape, jnp.bfloat16),
        8 * arrived.size,
        arrived,
        jnp.tile(labs, fold)[None],
    )


def grad_body(resid_ref, kern_ref, out_ref, resid):
    peers, rows, _ = resid_ref.shape
    classes = resid.shape[0]
    fold = classes // rows
    for group in range(peers // fold):
        blocks = regroup([resid_ref[fold * group + k].astype(jnp.float32) for k in range(fold)], fold)
        for q in range(fold):
            resid[rows * q : rows * (q + 1), LANES * group : LANES * (group + 1)] = blocks[q]
    held = resid[...].astype(jnp.bfloat16)
    _, height, _ = out_ref.shape
    step = 4 * LANES
    for start in range(0, kern_ref.shape[1], step):
        grad = jnp.dot(held, kern_ref[:, start : start + step], preferred_element_type=jnp.float32)
        for at in range(0, step, LANES):
            halves = [grad[height * h : height * (h + 1), at : at + LANES] for h in range(2)]
            first = 2 * (start + at) // LANES
            for i, block in enumerate(regroup(halves, 2)):
                out_ref[first + i] = block.astype(out_ref.dtype)


def partial_grad(resid_parts, kern, peers):
    batch, centres = kern.shape
    classes = resid_parts.size // batch
    height = classes * (centres // peers) // LANES
    return call(
        grad_body,
        jax.ShapeDtypeStruct((peers, height, LANES), jnp.bfloat16),
        2 * classes * batch * centres,
        resid_parts,
        kern,
        scratch=[pltpu.VMEM((classes, batch), jnp.float32)],
    )


def assemble_body(mine_ref, other_ref, *out_refs):
    core = lax.axis_index("core")
    steps = mine_ref.shape[1]
    for step in range(steps):
        feats_ref, square_ref = out_refs[step], out_refs[steps + step]
        total = None
        for i in range(mine_ref.shape[0]):
            for which, ref in ((core, mine_ref), (1 - core, other_ref)):
                block = ref[i, step]
                feats_ref[i, which] = block
                wide = block.astype(jnp.float32)
                square = jnp.sum(wide * wide, axis=0, keepdims=True)
                total = square if total is None else total + square
        square_ref[...] = total


def assembled(mine, other):
    blocks, steps, rows, batch = mine.shape
    feats = jax.ShapeDtypeStruct((blocks, 2, rows, batch), mine.dtype)
    squares = jax.ShapeDtypeStruct((1, batch), jnp.float32)
    out = call(assemble_body, [feats] * steps + [squares] * steps, 4 * mine.size, mine, other)
    return [(out[step].reshape(blocks * 2 * rows, batch), out[steps + step][0]) for step in range(steps)]


def swap_offsets(hops):
    offsets = [0]
    for hop in hops:
        offsets = offsets + [o ^ hop for o in offsets]
    return offsets


def doubled(held, axis, hop):
    pairs = [(i, i ^ hop) for i in range(lax.axis_size(axis))]
    return jnp.concatenate([held, lax.ppermute(held, axis, pairs)])


def swapped_cores(array):
    return lax.ppermute(array, "core", [(0, 1), (1, 0)])


def pick_body(pool_ref, picks_ref, out_ref):
    pool_dev = pool_ref.shape[1]
    copies, steps, _, batch = out_ref.shape
    first = (lax.axis_index("z") * lax.axis_size("x") + lax.axis_index("x")) * pool_dev
    rows = lax.broadcasted_iota(jnp.int32, (pool_dev, batch), 0)
    for step in range(steps):
        chosen = picks_ref[step : step + 1, :] - first
        onehot = (rows == chosen).astype(jnp.float32).astype(jnp.bfloat16)
        feats = jnp.dot(pool_ref[...], onehot, preferred_element_type=jnp.float32).astype(out_ref.dtype)
        for peer in range(copies):
            out_ref[peer, step] = feats


def picked(pool, picks, copies):
    steps, batch = picks.shape
    return call(
        pick_body,
        jax.ShapeDtypeStruct((copies, steps, pool.shape[0], batch), pool.dtype),
        2 * pool.size * batch * steps,
        pool,
        picks,
    )


def update_body(rate, arrived_ref, current_ref, new_ref, half_ref):
    peers = arrived_ref.shape[0]
    total = arrived_ref[0].astype(jnp.float32)
    for peer in range(1, peers):
        total = total + arrived_ref[peer].astype(jnp.float32)
    new = current_ref[...] - rate * total
    new_ref[...] = new
    half = new.astype(half_ref.dtype)
    for peer in range(peers):
        half_ref[peer] = half


def updated(arrived, current, rate):
    return call(
        functools.partial(update_body, rate),
        [
            jax.ShapeDtypeStruct(current.shape, jnp.float32),
            jax.ShapeDtypeStruct(arrived.shape, jnp.bfloat16),
        ],
        2 * arrived.size,
        arrived,
        current,
    )


def last_body(rate, arrived_ref, current_ref, new_ref):
    total = arrived_ref[0].astype(jnp.float32)
    for peer in range(1, arrived_ref.shape[0]):
        total = total + arrived_ref[peer].astype(jnp.float32)
    new_ref[...] = current_ref[...] - rate * total


def last_updated(arrived, current, rate):
    return call(
        functools.partial(last_body, rate),
        jax.ShapeDtypeStruct(current.shape, jnp.float32),
        2 * arrived.size,
        arrived,
        current,
    )


def laplace(cross, sample_sq, centre_sq, width):
    mean_sq = (sample_sq[:, None] + centre_sq[None, :] - 2.0 * cross) / width
    return jnp.exp(-jnp.sqrt(mean_sq + EPS) / LENGTH_SCALE).astype(jnp.bfloat16)


def on_device(centres, pool, labels, picks, coefs):
    width = centres.shape[0]
    cen_dev = centres.shape[1]
    pool_dev = pool.shape[1]
    batch_dev = picks.shape[1]
    classes, cen_own = coefs.shape
    n_centre, n_sample = lax.axis_size(CENTRE), lax.axis_size(SAMPLE)
    total_centres = cen_dev * n_centre
    total_batch = batch_dev * n_sample
    rate = STEP_GAIN * LOGIT_GAIN / total_batch
    own = batch_dev // n_centre
    fold = LANES // own
    me = lax.axis_index(CENTRE)
    over_z, over_x = lax.axis_size("z"), lax.axis_size("x")
    local_picks = picks - lax.axis_index(SAMPLE) * pool_dev
    centre_sq = jnp.sum(jnp.square(centres.astype(jnp.float32)), axis=0)

    def own_labels(step):
        chosen = lax.dynamic_slice(local_picks[step], (me * own,), (own,))
        return jnp.take(labels, chosen, mode="clip")

    packed = jnp.concatenate([coefs[: classes // 2], coefs[classes // 2 :]], axis=1)

    def kernel_matrix(gathered, sample_sq):
        cross = lax.dot_general(
            gathered, centres, (((0,), (0,)), ((), ())), preferred_element_type=jnp.float32
        )
        return laplace(cross, sample_sq, centre_sq, width)

    z_hops = [1 << i for i in reversed(range(over_z.bit_length() - 1))]
    held = packed.astype(jnp.bfloat16)[None]
    for hop in z_hops:
        held = doubled(held, "z", hop)
    mine = exchange(picked(pool, picks, lax.axis_size("y")), "y")
    mine, held, centre_sq = lax.optimization_barrier((mine, held, centre_sq))
    coef_parts = spread(held, "x")
    gathered = assembled(mine, swapped_cores(mine))
    kern = kernel_matrix(*gathered[0])
    labs = [own_labels(step) for step in range(STEPS)]

    gain = LOGIT_GAIN / total_centres
    logits = partial_logits(coef_parts, kern, n_centre, swap_offsets(z_hops))
    resid = exchange(residual(exchange(logits, CENTRE), labs[0], gain, fold), CENTRE)
    arrived = exchange(partial_grad(resid, kern, n_sample), SAMPLE)
    current, half = updated(arrived, packed, rate)

    kern = kernel_matrix(*gathered[1])
    coef_parts = exchange(half, SAMPLE).reshape(over_z, over_x, *current.shape)
    arrived = exchange(partial_logits(coef_parts, kern, n_centre), CENTRE)
    resid = exchange(residual(arrived, labs[1], gain, fold), CENTRE)
    arrived = exchange(partial_grad(resid, kern, n_sample), SAMPLE)
    current = last_updated(arrived, current, rate)
    return jnp.concatenate([current[:, :cen_own], current[:, cen_own:]], axis=0)


def solution(mesh):
    sizes = (mesh.shape["centre"] // 2, 2, 8, mesh.shape["sample"] // 8)
    fine = Mesh(mesh.devices.reshape(sizes), (*CENTRE, *SAMPLE))
    placed = (
        P(None, CENTRE),
        P(CENTRE, SAMPLE),
        P(SAMPLE),
        P(None, SAMPLE),
        P(None, (*CENTRE, *SAMPLE)),
    )
    return jax.shard_map(
        on_device,
        mesh=fine,
        in_specs=placed,
        out_specs=P(None, (*CENTRE, *SAMPLE)),
        check_vma=False,
    )
```

```python
import functools

import jax
import jax.numpy as jnp
from jax import lax
from jax.experimental import pallas as pl
from jax.experimental.pallas import tpu as pltpu
from jax.sharding import Mesh, PartitionSpec as P

STEPS = 2


LOGIT_GAIN = 16.0
LENGTH_SCALE = 0.5
STEP_GAIN = 2048.0
EPS = 1e-06

LANES = 128
KERN_VMEM = 48
CENTRE = ("y", "core")
SAMPLE = ("z", "x")


def exchange(parts, axes):
    return lax.all_to_all(parts, axes, 0, 0, tiled=True)


def spread(array, axes):
    peers = lax.axis_size(axes)
    return exchange(jnp.broadcast_to(array[None], (peers, *array.shape)), axes)


def call(body, out, flops, *operands, scratch=()):
    vmem = pl.BlockSpec(memory_space=pltpu.VMEM)
    many = isinstance(out, (list, tuple))
    nbytes = sum(a.size * a.dtype.itemsize for a in operands)
    return pl.pallas_call(
        body,
        out_shape=out,
        in_specs=[vmem] * len(operands),
        out_specs=[vmem] * len(out) if many else vmem,
        scratch_shapes=list(scratch),
        cost_estimate=pl.CostEstimate(flops=flops, bytes_accessed=nbytes, transcendentals=0),
        compiler_params=pltpu.CompilerParams(vmem_limit_bytes=24 << 20),
    )(*operands)


def regroup(blocks, fold):
    width = LANES // fold
    lane_block = lax.broadcasted_iota(jnp.int32, blocks[0].shape, 1) // width
    out = []
    for q in range(fold):
        merged = None
        for k in range(fold):
            shift = width * (k - q) % LANES
            moved = pltpu.roll(blocks[k], shift, 1) if shift else blocks[k]
            merged = moved if merged is None else jnp.where(lane_block == k, moved, merged)
        out.append(merged)
    return out


def logits_body(offsets, coef_ref, kern_ref, out_ref, coef, logits):
    over_z, over_x, height, _ = coef_ref.shape
    if offsets is not None:
        over_z, over_x = over_x, over_z
    for i in range(over_z):
        for p in range(over_x // 2):
            if offsets is None:
                pair = coef_ref[i, 2 * p], coef_ref[i, 2 * p + 1]
                at = LANES * (i * over_x // 2 + p)
            else:
                pair = coef_ref[2 * p, i], coef_ref[2 * p + 1, i]
                at = LANES * (lax.bitwise_xor(lax.axis_index("z"), offsets[i]) * (over_x // 2) + p)
                at = pl.multiple_of(at, LANES)
            halves = regroup([block.astype(jnp.float32) for block in pair], 2)
            for h in range(2):
                coef[height * h : height * (h + 1), pl.ds(at, LANES)] = halves[h]
    logits[...] = lax.dot_general(
        coef[...].astype(jnp.bfloat16),
        kern_ref[...],
        (((1,), (1,)), ((), ())),
        preferred_element_type=jnp.float32,
    )
    receivers, rows, _ = out_ref.shape
    fold = coef.shape[0] // rows
    for group in range(receivers // fold):
        columns = slice(LANES * group, LANES * (group + 1))
        blocks = regroup([logits[rows * q : rows * (q + 1), columns] for q in range(fold)], fold)
        for k in range(fold):
            out_ref[fold * group + k] = blocks[k].astype(out_ref.dtype)


def partial_logits(coef_parts, kern, peers, offsets=None):
    classes = 2 * coef_parts.shape[2]
    batch, centres = kern.shape
    rows = classes * (batch // peers) // LANES
    return call(
        functools.partial(logits_body, offsets),
        jax.ShapeDtypeStruct((peers, rows, LANES), jnp.bfloat16),
        2 * classes * batch * centres,
        coef_parts,
        kern,
        scratch=[pltpu.VMEM((classes, centres), jnp.float32), pltpu.VMEM((classes, batch), jnp.float32)],
    )


def fold_all(row, fold, op):
    while fold > 1:
        row = op(row, pltpu.roll(row, LANES // fold, 1))
        fold //= 2
    return row


def residual_body(gain, fold, arrived_ref, labs_ref, out_ref):
    peers, rows, _ = arrived_ref.shape
    total = arrived_ref[0].astype(jnp.float32)
    for peer in range(1, peers):
        total = total + arrived_ref[peer].astype(jnp.float32)
    logits = total * gain
    top = fold_all(jnp.max(logits, axis=0, keepdims=True), fold, jnp.maximum)
    expo = jnp.exp(logits - top)
    mass = fold_all(jnp.sum(expo, axis=0, keepdims=True), fold, jnp.add)
    probs = expo / mass
    block = lax.broadcasted_iota(jnp.int32, logits.shape, 1) // (LANES // fold)
    class_ids = block * rows + lax.broadcasted_iota(jnp.int32, logits.shape, 0)
    onehot = (class_ids == labs_ref[...]).astype(jnp.float32)
    resid = (probs - onehot).astype(out_ref.dtype)
    for peer in range(peers):
        out_ref[peer] = resid


def residual(arrived, labs, gain, fold):
    return call(
        functools.partial(residual_body, gain, fold),
        jax.ShapeDtypeStruct(arrived.shape, jnp.bfloat16),
        8 * arrived.size,
        arrived,
        jnp.tile(labs, fold)[None],
    )


def grad_body(resid_ref, kern_ref, out_ref, resid):
    peers, rows, _ = resid_ref.shape
    classes = resid.shape[0]
    fold = classes // rows
    for group in range(peers // fold):
        blocks = regroup([resid_ref[fold * group + k].astype(jnp.float32) for k in range(fold)], fold)
        for q in range(fold):
            resid[rows * q : rows * (q + 1), LANES * group : LANES * (group + 1)] = blocks[q]
    held = resid[...].astype(jnp.bfloat16)
    _, height, _ = out_ref.shape
    step = 4 * LANES
    for start in range(0, kern_ref.shape[1], step):
        grad = jnp.dot(held, kern_ref[:, start : start + step], preferred_element_type=jnp.float32)
        for at in range(0, step, LANES):
            halves = [grad[height * h : height * (h + 1), at : at + LANES] for h in range(2)]
            first = 2 * (start + at) // LANES
            for i, block in enumerate(regroup(halves, 2)):
                out_ref[first + i] = block.astype(out_ref.dtype)


def partial_grad(resid_parts, kern, peers):
    batch, centres = kern.shape
    classes = resid_parts.size // batch
    height = classes * (centres // peers) // LANES
    return call(
        grad_body,
        jax.ShapeDtypeStruct((peers, height, LANES), jnp.bfloat16),
        2 * classes * batch * centres,
        resid_parts,
        kern,
        scratch=[pltpu.VMEM((classes, batch), jnp.float32)],
    )


def laplace_body(feats, centres_ref, held, sems, centre_sq_ref, out_ref, arrivals, kept):
    blocks, _, rows, batch = feats.shape
    width, centres = held.shape
    columns = 2 * LANES
    parts = [slice(start, start + columns) for start in range(0, centres, columns)]
    staged = [
        pltpu.make_async_copy(centres_ref.at[:, part], held.at[:, part], sems.at[i])
        for i, part in enumerate(parts)
    ]
    for copy in arrivals + staged + kept:
        copy.start()
    for copy in arrivals:
        copy.wait()
    together = feats[...].reshape(width, batch)
    squares = jnp.sum(jnp.square(together.astype(jnp.float32)), axis=0, keepdims=True)
    sample_sq = jnp.transpose(jnp.broadcast_to(squares, (LANES, batch)))[:, :1]
    samples = jnp.transpose(together)
    for part, copy in zip(parts, staged):
        copy.wait()
        cross = jnp.dot(samples, held[:, part], preferred_element_type=jnp.float32)
        mean_sq = (sample_sq + centre_sq_ref[:, part] - 2.0 * cross) * (1.0 / width) + EPS
        mean_sq = jnp.maximum(mean_sq, 1e-37)
        root = mean_sq * lax.rsqrt(mean_sq)
        out_ref[:, part] = jnp.exp(root * (-1.0 / LENGTH_SCALE)).astype(out_ref.dtype)
    for copy in kept:
        copy.wait()


def first_laplace_body(mine_ref, other_ref, centres_ref, centre_sq_ref, out_ref, later_ref, feats, held, sems, more):
    core = lax.axis_index("core")
    sides = ((mine_ref, core), (other_ref, 1 - core))
    arrivals, kept = [
        [
            pltpu.make_async_copy(ref.at[:, step], into.at[:, which], more.at[2 * step + i])
            for i, (ref, which) in enumerate(sides)
        ]
        for step, into in enumerate((feats, later_ref))
    ]
    laplace_body(feats, centres_ref, held, sems, centre_sq_ref, out_ref, arrivals, kept)


def later_laplace_body(feats_ref, centres_ref, centre_sq_ref, out_ref, held, sems):
    laplace_body(feats_ref, centres_ref, held, sems, centre_sq_ref, out_ref, [], [])


def kernel_matrix(body, feats, centres, centre_sq, batch, later=None):
    width, columns = centres.shape
    vmem, anywhere = pl.BlockSpec(memory_space=pltpu.VMEM), pl.BlockSpec(memory_space=pl.ANY)
    out = [jax.ShapeDtypeStruct((batch, columns), jnp.bfloat16)]
    scratch = [
        pltpu.VMEM(centres.shape, jnp.bfloat16),
        pltpu.SemaphoreType.DMA((columns // (2 * LANES),)),
    ]
    if later is not None:
        out.append(later)
        scratch = [pltpu.VMEM(later.shape, later.dtype), *scratch, pltpu.SemaphoreType.DMA((4,))]
    return pl.pallas_call(
        body,
        out_shape=out,
        in_specs=[vmem if later is None else anywhere] * len(feats) + [anywhere, vmem],
        out_specs=[vmem] * len(out),
        scratch_shapes=scratch,
        cost_estimate=pl.CostEstimate(
            flops=2 * centres.size * batch, bytes_accessed=2 * centres.size, transcendentals=0
        ),
        compiler_params=pltpu.CompilerParams(vmem_limit_bytes=KERN_VMEM << 20),
    )(*feats, centres, centre_sq)


def swap_offsets(hops):
    offsets = [0]
    for hop in hops:
        offsets = offsets + [o ^ hop for o in offsets]
    return offsets


def doubled(held, axis, hop):
    pairs = [(i, i ^ hop) for i in range(lax.axis_size(axis))]
    return jnp.concatenate([held, lax.ppermute(held, axis, pairs)])


def swapped_cores(array):
    return lax.ppermute(array, "core", [(0, 1), (1, 0)])


def pick_body(pool_ref, picks_ref, out_ref):
    pool_dev = pool_ref.shape[1]
    copies, steps, _, batch = out_ref.shape
    first = (lax.axis_index("z") * lax.axis_size("x") + lax.axis_index("x")) * pool_dev
    rows = lax.broadcasted_iota(jnp.int32, (pool_dev, batch), 0)
    for step in range(steps):
        chosen = picks_ref[step : step + 1, :] - first
        onehot = (rows == chosen).astype(jnp.float32).astype(jnp.bfloat16)
        feats = jnp.dot(pool_ref[...], onehot, preferred_element_type=jnp.float32).astype(out_ref.dtype)
        for peer in range(copies):
            out_ref[peer, step] = feats


def picked(pool, picks, copies):
    steps, batch = picks.shape
    return call(
        pick_body,
        jax.ShapeDtypeStruct((copies, steps, pool.shape[0], batch), pool.dtype),
        2 * pool.size * batch * steps,
        pool,
        picks,
    )


def update_body(rate, arrived_ref, current_ref, new_ref, half_ref):
    peers = arrived_ref.shape[0]
    total = arrived_ref[0].astype(jnp.float32)
    for peer in range(1, peers):
        total = total + arrived_ref[peer].astype(jnp.float32)
    new = current_ref[...] - rate * total
    new_ref[...] = new
    half = new.astype(half_ref.dtype)
    for peer in range(peers):
        half_ref[peer] = half


def updated(arrived, current, rate):
    return call(
        functools.partial(update_body, rate),
        [
            jax.ShapeDtypeStruct(current.shape, jnp.float32),
            jax.ShapeDtypeStruct(arrived.shape, jnp.bfloat16),
        ],
        2 * arrived.size,
        arrived,
        current,
    )


def last_body(rate, arrived_ref, current_ref, new_ref):
    total = arrived_ref[0].astype(jnp.float32)
    for peer in range(1, arrived_ref.shape[0]):
        total = total + arrived_ref[peer].astype(jnp.float32)
    new_ref[...] = current_ref[...] - rate * total


def last_updated(arrived, current, rate):
    return call(
        functools.partial(last_body, rate),
        jax.ShapeDtypeStruct(current.shape, jnp.float32),
        2 * arrived.size,
        arrived,
        current,
    )


def on_device(centres, pool, labels, picks, coefs):
    cen_dev = centres.shape[1]
    pool_dev = pool.shape[1]
    batch_dev = picks.shape[1]
    classes, cen_own = coefs.shape
    n_centre, n_sample = lax.axis_size(CENTRE), lax.axis_size(SAMPLE)
    total_centres = cen_dev * n_centre
    total_batch = batch_dev * n_sample
    rate = STEP_GAIN * LOGIT_GAIN / total_batch
    own = batch_dev // n_centre
    fold = LANES // own
    me = lax.axis_index(CENTRE)
    over_z, over_x = lax.axis_size("z"), lax.axis_size("x")
    local_picks = picks - lax.axis_index(SAMPLE) * pool_dev
    centre_sq = jnp.sum(jnp.square(centres.astype(jnp.float32)), axis=0, keepdims=True)

    def own_labels(step):
        chosen = lax.dynamic_slice(local_picks[step], (me * own,), (own,))
        return jnp.take(labels, chosen, mode="clip")

    packed = jnp.concatenate([coefs[: classes // 2], coefs[classes // 2 :]], axis=1)

    z_hops = [1 << i for i in reversed(range(over_z.bit_length() - 1))]
    held = packed.astype(jnp.bfloat16)[None]
    for hop in z_hops:
        held = doubled(held, "z", hop)
    mine = exchange(picked(pool, picks, lax.axis_size("y")), "y")
    mine, held, centre_sq, packed = lax.optimization_barrier((mine, held, centre_sq, packed))
    coef_parts = spread(held, "x")
    other = swapped_cores(mine)
    later = jax.ShapeDtypeStruct((mine.shape[0], 2, *mine.shape[2:]), mine.dtype)
    kern, later = kernel_matrix(first_laplace_body, (mine, other), centres, centre_sq, batch_dev, later)
    labs = [own_labels(step) for step in range(STEPS)]

    gain = LOGIT_GAIN / total_centres
    logits = partial_logits(coef_parts, kern, n_centre, swap_offsets(z_hops))
    resid = exchange(residual(exchange(logits, CENTRE), labs[0], gain, fold), CENTRE)
    arrived = exchange(partial_grad(resid, kern, n_sample), SAMPLE)
    current, half = updated(arrived, packed, rate)

    (kern,) = kernel_matrix(later_laplace_body, (later,), centres, centre_sq, batch_dev)
    coef_parts = exchange(half, SAMPLE).reshape(over_z, over_x, *current.shape)
    arrived = exchange(partial_logits(coef_parts, kern, n_centre), CENTRE)
    resid = exchange(residual(arrived, labs[1], gain, fold), CENTRE)
    arrived = exchange(partial_grad(resid, kern, n_sample), SAMPLE)
    current = last_updated(arrived, current, rate)
    return jnp.concatenate([current[:, :cen_own], current[:, cen_own:]], axis=0)


def solution(mesh):
    sizes = (mesh.shape["centre"] // 2, 2, 8, mesh.shape["sample"] // 8)
    fine = Mesh(mesh.devices.reshape(sizes), (*CENTRE, *SAMPLE))
    placed = (
        P(None, CENTRE),
        P(CENTRE, SAMPLE),
        P(SAMPLE),
        P(None, SAMPLE),
        P(None, (*CENTRE, *SAMPLE)),
    )
    return jax.shard_map(
        on_device,
        mesh=fine,
        in_specs=placed,
        out_specs=P(None, (*CENTRE, *SAMPLE)),
        check_vma=False,
    )
```

```python
import functools

import jax
import jax.numpy as jnp
from jax import lax
from jax.experimental import pallas as pl
from jax.experimental.pallas import tpu as pltpu
from jax.sharding import Mesh, PartitionSpec as P

STEPS = 2


LOGIT_GAIN = 16.0
LENGTH_SCALE = 0.5
STEP_GAIN = 2048.0
EPS = 1e-06

LANES = 128
KERN_VMEM = 48
CENTRE = ("y", "core")
SAMPLE = ("z", "x")


def exchange(parts, axes):
    return lax.all_to_all(parts, axes, 0, 0, tiled=True)


def spread(array, axes):
    peers = lax.axis_size(axes)
    return exchange(jnp.broadcast_to(array[None], (peers, *array.shape)), axes)


def call(body, out, flops, *operands, scratch=()):
    vmem = pl.BlockSpec(memory_space=pltpu.VMEM)
    many = isinstance(out, (list, tuple))
    nbytes = sum(a.size * a.dtype.itemsize for a in operands)
    return pl.pallas_call(
        body,
        out_shape=out,
        in_specs=[vmem] * len(operands),
        out_specs=[vmem] * len(out) if many else vmem,
        scratch_shapes=list(scratch),
        cost_estimate=pl.CostEstimate(flops=flops, bytes_accessed=nbytes, transcendentals=0),
        compiler_params=pltpu.CompilerParams(vmem_limit_bytes=24 << 20),
    )(*operands)


def regroup(blocks, fold):
    width = LANES // fold
    lane_block = lax.broadcasted_iota(jnp.int32, blocks[0].shape, 1) // width
    out = []
    for q in range(fold):
        merged = None
        for k in range(fold):
            shift = width * (k - q) % LANES
            moved = pltpu.roll(blocks[k], shift, 1) if shift else blocks[k]
            merged = moved if merged is None else jnp.where(lane_block == k, moved, merged)
        out.append(merged)
    return out


def logits_body(offsets, coef_ref, kern_ref, out_ref, coef, logits):
    over_z, over_x, height, _ = coef_ref.shape
    if offsets is not None:
        over_z, over_x = over_x, over_z
    for i in range(over_z):
        for p in range(over_x // 2):
            if offsets is None:
                pair = coef_ref[i, 2 * p], coef_ref[i, 2 * p + 1]
                at = LANES * (i * over_x // 2 + p)
            else:
                pair = coef_ref[2 * p, i], coef_ref[2 * p + 1, i]
                at = LANES * (lax.bitwise_xor(lax.axis_index("z"), offsets[i]) * (over_x // 2) + p)
                at = pl.multiple_of(at, LANES)
            halves = regroup([block.astype(jnp.float32) for block in pair], 2)
            for h in range(2):
                coef[height * h : height * (h + 1), pl.ds(at, LANES)] = halves[h]
    logits[...] = lax.dot_general(
        coef[...].astype(jnp.bfloat16),
        kern_ref[...],
        (((1,), (1,)), ((), ())),
        preferred_element_type=jnp.float32,
    )
    receivers, rows, _ = out_ref.shape
    fold = coef.shape[0] // rows
    for group in range(receivers // fold):
        columns = slice(LANES * group, LANES * (group + 1))
        blocks = regroup([logits[rows * q : rows * (q + 1), columns] for q in range(fold)], fold)
        for k in range(fold):
            out_ref[fold * group + k] = blocks[k].astype(out_ref.dtype)


def partial_logits(coef_parts, kern, peers, offsets=None):
    classes = 2 * coef_parts.shape[2]
    batch, centres = kern.shape
    rows = classes * (batch // peers) // LANES
    return call(
        functools.partial(logits_body, offsets),
        jax.ShapeDtypeStruct((peers, rows, LANES), jnp.bfloat16),
        2 * classes * batch * centres,
        coef_parts,
        kern,
        scratch=[pltpu.VMEM((classes, centres), jnp.float32), pltpu.VMEM((classes, batch), jnp.float32)],
    )


def fold_all(row, fold, op):
    while fold > 1:
        row = op(row, pltpu.roll(row, LANES // fold, 1))
        fold //= 2
    return row


def residual_body(gain, fold, arrived_ref, labs_ref, out_ref):
    peers, rows, _ = arrived_ref.shape
    total = arrived_ref[0].astype(jnp.float32)
    for peer in range(1, peers):
        total = total + arrived_ref[peer].astype(jnp.float32)
    logits = total * gain
    top = fold_all(jnp.max(logits, axis=0, keepdims=True), fold, jnp.maximum)
    expo = jnp.exp(logits - top)
    mass = fold_all(jnp.sum(expo, axis=0, keepdims=True), fold, jnp.add)
    probs = expo / mass
    block = lax.broadcasted_iota(jnp.int32, logits.shape, 1) // (LANES // fold)
    class_ids = block * rows + lax.broadcasted_iota(jnp.int32, logits.shape, 0)
    onehot = (class_ids == labs_ref[...]).astype(jnp.float32)
    resid = (probs - onehot).astype(out_ref.dtype)
    for peer in range(peers):
        out_ref[peer] = resid


def residual(arrived, labs, gain, fold):
    return call(
        functools.partial(residual_body, gain, fold),
        jax.ShapeDtypeStruct(arrived.shape, jnp.bfloat16),
        8 * arrived.size,
        arrived,
        labs,
    )


def grad_body(resid_ref, kern_ref, out_ref, resid):
    peers, rows, _ = resid_ref.shape
    classes = resid.shape[0]
    fold = classes // rows
    for group in range(peers // fold):
        blocks = regroup([resid_ref[fold * group + k].astype(jnp.float32) for k in range(fold)], fold)
        for q in range(fold):
            resid[rows * q : rows * (q + 1), LANES * group : LANES * (group + 1)] = blocks[q]
    held = resid[...].astype(jnp.bfloat16)
    _, height, _ = out_ref.shape
    step = 4 * LANES
    for start in range(0, kern_ref.shape[1], step):
        grad = jnp.dot(held, kern_ref[:, start : start + step], preferred_element_type=jnp.float32)
        for at in range(0, step, LANES):
            halves = [grad[height * h : height * (h + 1), at : at + LANES] for h in range(2)]
            first = 2 * (start + at) // LANES
            for i, block in enumerate(regroup(halves, 2)):
                out_ref[first + i] = block.astype(out_ref.dtype)


def partial_grad(resid_parts, kern, peers):
    batch, centres = kern.shape
    classes = resid_parts.size // batch
    height = classes * (centres // peers) // LANES
    return call(
        grad_body,
        jax.ShapeDtypeStruct((peers, height, LANES), jnp.bfloat16),
        2 * classes * batch * centres,
        resid_parts,
        kern,
        scratch=[pltpu.VMEM((classes, batch), jnp.float32)],
    )


def assemble_body(mine_ref, other_ref, *out_refs):
    core = lax.axis_index("core")
    steps = mine_ref.shape[1]
    for step in range(steps):
        for i in range(mine_ref.shape[0]):
            for which, ref in ((core, mine_ref), (1 - core, other_ref)):
                out_refs[step][i, which] = ref[i, step]


def assembled(mine, other):
    blocks, steps, rows, batch = mine.shape
    feats = jax.ShapeDtypeStruct((blocks, 2, rows, batch), mine.dtype)
    return call(assemble_body, [feats] * steps, mine.size, mine, other)


def laplace_body(feats_ref, centres_ref, centre_sq_ref, out_ref, held, sems):
    width, centres = held.shape
    batch = feats_ref.shape[-1]
    rows = width // sems.shape[0]
    columns = 2 * LANES
    staged = [
        pltpu.make_async_copy(
            centres_ref.at[pl.ds(rows * i, rows)], held.at[pl.ds(rows * i, rows)], sems.at[i]
        )
        for i in range(sems.shape[0])
    ]
    for copy in staged:
        copy.start()
    feats = feats_ref[...].reshape(width, batch)
    squares = jnp.sum(jnp.square(feats.astype(jnp.float32)), axis=0, keepdims=True)
    sample_sq = jnp.transpose(jnp.broadcast_to(squares, (LANES, batch)))[:, :1]
    samples = jnp.transpose(feats)
    for copy in staged:
        copy.wait()
    for start in range(0, centres, columns):
        part = slice(start, start + columns)
        cross = jnp.dot(samples, held[:, part], preferred_element_type=jnp.float32)
        mean_sq = (sample_sq + centre_sq_ref[:, part] - 2.0 * cross) * (1.0 / width) + EPS
        mean_sq = jnp.maximum(mean_sq, 1e-37)
        root = mean_sq * lax.rsqrt(mean_sq)
        out_ref[:, part] = jnp.exp(root * (-1.0 / LENGTH_SCALE)).astype(out_ref.dtype)


def kernel_matrix(feats, centres, centre_sq):
    columns, batch = centres.shape[1], feats.shape[-1]
    vmem, anywhere = pl.BlockSpec(memory_space=pltpu.VMEM), pl.BlockSpec(memory_space=pl.ANY)
    return pl.pallas_call(
        laplace_body,
        out_shape=jax.ShapeDtypeStruct((batch, columns), jnp.bfloat16),
        in_specs=[vmem, anywhere, vmem],
        out_specs=vmem,
        scratch_shapes=[pltpu.VMEM(centres.shape, jnp.bfloat16), pltpu.SemaphoreType.DMA((4,))],
        cost_estimate=pl.CostEstimate(
            flops=2 * centres.size * batch, bytes_accessed=2 * centres.size, transcendentals=0
        ),
        compiler_params=pltpu.CompilerParams(vmem_limit_bytes=KERN_VMEM << 20),
    )(feats, centres, centre_sq)


def swap_offsets(hops):
    offsets = [0]
    for hop in hops:
        offsets = offsets + [o ^ hop for o in offsets]
    return offsets


def doubled(held, axis, hop):
    pairs = [(i, i ^ hop) for i in range(lax.axis_size(axis))]
    return jnp.concatenate([held, lax.ppermute(held, axis, pairs)])


def swapped_cores(array):
    return lax.ppermute(array, "core", [(0, 1), (1, 0)])


def pick_body(pool_ref, picks_ref, out_ref):
    pool_dev = pool_ref.shape[1]
    copies, steps, _, batch = out_ref.shape
    first = (lax.axis_index("z") * lax.axis_size("x") + lax.axis_index("x")) * pool_dev
    rows = lax.broadcasted_iota(jnp.int32, (pool_dev, batch), 0)
    for step in range(steps):
        chosen = picks_ref[step : step + 1, :] - first
        onehot = (rows == chosen).astype(jnp.float32).astype(jnp.bfloat16)
        feats = jnp.dot(pool_ref[...], onehot, preferred_element_type=jnp.float32).astype(out_ref.dtype)
        for peer in range(copies):
            out_ref[peer, step] = feats


def picked(pool, picks, copies):
    steps, batch = picks.shape
    return call(
        pick_body,
        jax.ShapeDtypeStruct((copies, steps, pool.shape[0], batch), pool.dtype),
        2 * pool.size * batch * steps,
        pool,
        picks,
    )


def update_body(rate, arrived_ref, current_ref, new_ref, half_ref):
    peers = arrived_ref.shape[0]
    total = arrived_ref[0].astype(jnp.float32)
    for peer in range(1, peers):
        total = total + arrived_ref[peer].astype(jnp.float32)
    new = current_ref[...] - rate * total
    new_ref[...] = new
    half = new.astype(half_ref.dtype)
    for peer in range(peers):
        half_ref[peer] = half


def updated(arrived, current, rate):
    return call(
        functools.partial(update_body, rate),
        [
            jax.ShapeDtypeStruct(current.shape, jnp.float32),
            jax.ShapeDtypeStruct(arrived.shape, jnp.bfloat16),
        ],
        2 * arrived.size,
        arrived,
        current,
    )


def last_body(rate, arrived_ref, current_ref, new_ref):
    total = arrived_ref[0].astype(jnp.float32)
    for peer in range(1, arrived_ref.shape[0]):
        total = total + arrived_ref[peer].astype(jnp.float32)
    turned = jnp.transpose(current_ref[...] - rate * total)
    own, height = new_ref.shape[0], total.shape[0]
    for h in range(LANES // own):
        new_ref[:, height * h : height * (h + 1)] = turned[own * h : own * (h + 1)]


def last_updated(arrived, current, rate, own):
    return call(
        functools.partial(last_body, rate),
        jax.ShapeDtypeStruct((own, current.size // own), jnp.float32),
        2 * arrived.size,
        arrived,
        current,
    )


def on_device(centres, pool, labels, picks, coefs):
    cen_dev = centres.shape[1]
    pool_dev = pool.shape[1]
    batch_dev = picks.shape[1]
    classes, cen_own = coefs.shape
    n_centre, n_sample = lax.axis_size(CENTRE), lax.axis_size(SAMPLE)
    total_centres = cen_dev * n_centre
    total_batch = batch_dev * n_sample
    rate = STEP_GAIN * LOGIT_GAIN / total_batch
    own = batch_dev // n_centre
    fold = LANES // own
    me = lax.axis_index(CENTRE)
    over_z, over_x = lax.axis_size("z"), lax.axis_size("x")
    local_picks = picks - lax.axis_index(SAMPLE) * pool_dev
    centre_sq = jnp.sum(jnp.square(centres.astype(jnp.float32)), axis=0, keepdims=True)

    def own_labels(step):
        chosen = lax.dynamic_slice(local_picks[step], (me * own,), (own,))
        return jnp.tile(jnp.take(labels, chosen, mode="clip"), fold)[None]

    packed = jnp.concatenate([coefs[: classes // 2], coefs[classes // 2 :]], axis=1)

    z_hops = [1 << i for i in reversed(range(over_z.bit_length() - 1))]
    held = packed.astype(jnp.bfloat16)[None]
    for hop in z_hops:
        held = doubled(held, "z", hop)
    mine = exchange(picked(pool, picks, lax.axis_size("y")), "y")
    labs = [own_labels(step) for step in range(STEPS)]
    mine, held, centre_sq, packed, labs = lax.optimization_barrier(
        (mine, held, centre_sq, packed, labs)
    )
    coef_parts = spread(held, "x")
    first, later = assembled(mine, swapped_cores(mine))
    kern = kernel_matrix(first, centres, centre_sq)

    gain = LOGIT_GAIN / total_centres
    logits = partial_logits(coef_parts, kern, n_centre, swap_offsets(z_hops))
    resid = exchange(residual(exchange(logits, CENTRE), labs[0], gain, fold), CENTRE)
    arrived = exchange(partial_grad(resid, kern, n_sample), SAMPLE)
    current, half = updated(arrived, packed, rate)

    kern = kernel_matrix(later, centres, centre_sq)
    coef_parts = exchange(half, SAMPLE).reshape(over_z, over_x, *current.shape)
    arrived = exchange(partial_logits(coef_parts, kern, n_centre), CENTRE)
    resid = exchange(residual(arrived, labs[1], gain, fold), CENTRE)
    arrived = exchange(partial_grad(resid, kern, n_sample), SAMPLE)
    return last_updated(arrived, current, rate, cen_own).T


def solution(mesh):
    sizes = (mesh.shape["centre"] // 2, 2, 8, mesh.shape["sample"] // 8)
    fine = Mesh(mesh.devices.reshape(sizes), (*CENTRE, *SAMPLE))
    placed = (
        P(None, CENTRE),
        P(CENTRE, SAMPLE),
        P(SAMPLE),
        P(None, SAMPLE),
        P(None, (*CENTRE, *SAMPLE)),
    )
    return jax.shard_map(
        on_device,
        mesh=fine,
        in_specs=placed,
        out_specs=P(None, (*CENTRE, *SAMPLE)),
        check_vma=False,
    )
```

```python
import functools

import jax
import jax.numpy as jnp
from jax import lax
from jax.experimental import pallas as pl
from jax.experimental.pallas import tpu as pltpu
from jax.sharding import Mesh, PartitionSpec as P

STEPS = 2


LOGIT_GAIN = 16.0
LENGTH_SCALE = 0.5
STEP_GAIN = 2048.0
EPS = 1e-06

LANES = 128
KERN_VMEM = 48
PICK_VMEM = 60
COPIES_COST = 4_000_000_000
CENTRE = ("y", "core")
SAMPLE = ("z", "x")


def exchange(parts, axes):
    return lax.all_to_all(parts, axes, 0, 0, tiled=True)


def spread(array, axes):
    peers = lax.axis_size(axes)
    return exchange(jnp.broadcast_to(array[None], (peers, *array.shape)), axes)


def call(body, out, flops, *operands, scratch=()):
    vmem = pl.BlockSpec(memory_space=pltpu.VMEM)
    many = isinstance(out, (list, tuple))
    nbytes = sum(a.size * a.dtype.itemsize for a in operands)
    return pl.pallas_call(
        body,
        out_shape=out,
        in_specs=[vmem] * len(operands),
        out_specs=[vmem] * len(out) if many else vmem,
        scratch_shapes=list(scratch),
        cost_estimate=pl.CostEstimate(flops=flops, bytes_accessed=nbytes, transcendentals=0),
        compiler_params=pltpu.CompilerParams(vmem_limit_bytes=24 << 20),
    )(*operands)


def regroup(blocks, fold):
    width = LANES // fold
    lane_block = lax.broadcasted_iota(jnp.int32, blocks[0].shape, 1) // width
    out = []
    for q in range(fold):
        merged = None
        for k in range(fold):
            shift = width * (k - q) % LANES
            moved = pltpu.roll(blocks[k], shift, 1) if shift else blocks[k]
            merged = moved if merged is None else jnp.where(lane_block == k, moved, merged)
        out.append(merged)
    return out


def logits_body(offsets, coef_ref, kern_ref, out_ref, coef, logits):
    over_z, over_x, height, _ = coef_ref.shape
    if offsets is not None:
        over_z, over_x = over_x, over_z
    for i in range(over_z):
        for p in range(over_x // 2):
            if offsets is None:
                pair = coef_ref[i, 2 * p], coef_ref[i, 2 * p + 1]
                at = LANES * (i * over_x // 2 + p)
            else:
                pair = coef_ref[2 * p, i], coef_ref[2 * p + 1, i]
                at = LANES * (lax.bitwise_xor(lax.axis_index("z"), offsets[i]) * (over_x // 2) + p)
                at = pl.multiple_of(at, LANES)
            halves = regroup([block.astype(jnp.float32) for block in pair], 2)
            for h in range(2):
                coef[height * h : height * (h + 1), pl.ds(at, LANES)] = halves[h]
    logits[...] = lax.dot_general(
        coef[...].astype(jnp.bfloat16),
        kern_ref[...],
        (((1,), (1,)), ((), ())),
        preferred_element_type=jnp.float32,
    )
    receivers, rows, _ = out_ref.shape
    fold = coef.shape[0] // rows
    for group in range(receivers // fold):
        columns = slice(LANES * group, LANES * (group + 1))
        blocks = regroup([logits[rows * q : rows * (q + 1), columns] for q in range(fold)], fold)
        for k in range(fold):
            out_ref[fold * group + k] = blocks[k].astype(out_ref.dtype)


def partial_logits(coef_parts, kern, peers, offsets=None):
    classes = 2 * coef_parts.shape[2]
    batch, centres = kern.shape
    rows = classes * (batch // peers) // LANES
    return call(
        functools.partial(logits_body, offsets),
        jax.ShapeDtypeStruct((peers, rows, LANES), jnp.bfloat16),
        2 * classes * batch * centres,
        coef_parts,
        kern,
        scratch=[pltpu.VMEM((classes, centres), jnp.float32), pltpu.VMEM((classes, batch), jnp.float32)],
    )


def fold_all(row, fold, op):
    while fold > 1:
        row = op(row, pltpu.roll(row, LANES // fold, 1))
        fold //= 2
    return row


def residual_body(gain, fold, arrived_ref, labs_ref, out_ref):
    peers, rows, _ = arrived_ref.shape
    total = arrived_ref[0].astype(jnp.float32)
    for peer in range(1, peers):
        total = total + arrived_ref[peer].astype(jnp.float32)
    logits = total * gain
    top = fold_all(jnp.max(logits, axis=0, keepdims=True), fold, jnp.maximum)
    expo = jnp.exp(logits - top)
    mass = fold_all(jnp.sum(expo, axis=0, keepdims=True), fold, jnp.add)
    probs = expo / mass
    block = lax.broadcasted_iota(jnp.int32, logits.shape, 1) // (LANES // fold)
    class_ids = block * rows + lax.broadcasted_iota(jnp.int32, logits.shape, 0)
    onehot = (class_ids == labs_ref[...]).astype(jnp.float32)
    resid = (probs - onehot).astype(out_ref.dtype)
    for peer in range(peers):
        out_ref[peer] = resid


def residual(arrived, labs, gain, fold):
    return call(
        functools.partial(residual_body, gain, fold),
        jax.ShapeDtypeStruct(arrived.shape, jnp.bfloat16),
        8 * arrived.size,
        arrived,
        labs,
    )


def grad_body(resid_ref, kern_ref, out_ref, resid):
    peers, rows, _ = resid_ref.shape
    classes = resid.shape[0]
    fold = classes // rows
    for group in range(peers // fold):
        blocks = regroup([resid_ref[fold * group + k].astype(jnp.float32) for k in range(fold)], fold)
        for q in range(fold):
            resid[rows * q : rows * (q + 1), LANES * group : LANES * (group + 1)] = blocks[q]
    held = resid[...].astype(jnp.bfloat16)
    _, height, _ = out_ref.shape
    step = 4 * LANES
    for start in range(0, kern_ref.shape[1], step):
        grad = jnp.dot(held, kern_ref[:, start : start + step], preferred_element_type=jnp.float32)
        for at in range(0, step, LANES):
            halves = [grad[height * h : height * (h + 1), at : at + LANES] for h in range(2)]
            first = 2 * (start + at) // LANES
            for i, block in enumerate(regroup(halves, 2)):
                out_ref[first + i] = block.astype(out_ref.dtype)


def partial_grad(resid_parts, kern, peers):
    batch, centres = kern.shape
    classes = resid_parts.size // batch
    height = classes * (centres // peers) // LANES
    return call(
        grad_body,
        jax.ShapeDtypeStruct((peers, height, LANES), jnp.bfloat16),
        2 * classes * batch * centres,
        resid_parts,
        kern,
        scratch=[pltpu.VMEM((classes, batch), jnp.float32)],
    )


def assemble_body(mine_ref, other_ref, *out_refs):
    core = lax.axis_index("core")
    steps = mine_ref.shape[1]
    for step in range(steps):
        for i in range(mine_ref.shape[0]):
            for which, ref in ((core, mine_ref), (1 - core, other_ref)):
                out_refs[step][i, which] = ref[i, step]


def assembled(mine, other):
    blocks, steps, rows, batch = mine.shape
    feats = jax.ShapeDtypeStruct((blocks, 2, rows, batch), mine.dtype)
    return call(assemble_body, [feats] * steps, mine.size, mine, other)


def laplace_body(feats_ref, centres_ref, centre_sq_ref, out_ref, held, sems):
    width, centres = held.shape
    batch = feats_ref.shape[-1]
    rows = width // sems.shape[0]
    columns = 2 * LANES
    staged = [
        pltpu.make_async_copy(
            centres_ref.at[pl.ds(rows * i, rows)], held.at[pl.ds(rows * i, rows)], sems.at[i]
        )
        for i in range(sems.shape[0])
    ]
    for copy in staged:
        copy.start()
    feats = feats_ref[...].reshape(width, batch)
    squares = jnp.sum(jnp.square(feats.astype(jnp.float32)), axis=0, keepdims=True)
    sample_sq = jnp.transpose(jnp.broadcast_to(squares, (LANES, batch)))[:, :1]
    samples = jnp.transpose(feats)
    for copy in staged:
        copy.wait()
    for start in range(0, centres, columns):
        part = slice(start, start + columns)
        cross = jnp.dot(samples, held[:, part], preferred_element_type=jnp.float32)
        mean_sq = (sample_sq + centre_sq_ref[:, part] - 2.0 * cross) * (1.0 / width) + EPS
        mean_sq = jnp.maximum(mean_sq, 1e-37)
        root = mean_sq * lax.rsqrt(mean_sq)
        out_ref[:, part] = jnp.exp(root * (-1.0 / LENGTH_SCALE)).astype(out_ref.dtype)


def kernel_matrix(feats, centres, centre_sq):
    columns, batch = centres.shape[1], feats.shape[-1]
    vmem, anywhere = pl.BlockSpec(memory_space=pltpu.VMEM), pl.BlockSpec(memory_space=pl.ANY)
    return pl.pallas_call(
        laplace_body,
        out_shape=jax.ShapeDtypeStruct((batch, columns), jnp.bfloat16),
        in_specs=[vmem, anywhere, vmem],
        out_specs=vmem,
        scratch_shapes=[pltpu.VMEM(centres.shape, jnp.bfloat16), pltpu.SemaphoreType.DMA((4,))],
        cost_estimate=pl.CostEstimate(
            flops=2 * centres.size * batch, bytes_accessed=2 * centres.size, transcendentals=0
        ),
        compiler_params=pltpu.CompilerParams(vmem_limit_bytes=KERN_VMEM << 20),
    )(feats, centres, centre_sq)


def swap_offsets(hops):
    offsets = [0]
    for hop in hops:
        offsets = offsets + [o ^ hop for o in offsets]
    return offsets


def doubled(held, axis, hop):
    pairs = [(i, i ^ hop) for i in range(lax.axis_size(axis))]
    return jnp.concatenate([held, lax.ppermute(held, axis, pairs)])


def copies_body(held_ref, moved_ref, out_ref):
    near = held_ref.shape[0]
    for copy in range(out_ref.shape[0]):
        out_ref[copy, :near] = held_ref[...]
        out_ref[copy, near:] = moved_ref[...]


def last_doubled(held, axis, hop, copies):
    pairs = [(i, i ^ hop) for i in range(lax.axis_size(axis))]
    moved = lax.ppermute(held, axis, pairs)
    out = jax.ShapeDtypeStruct((copies, 2 * held.shape[0], *held.shape[1:]), held.dtype)
    return call(copies_body, out, COPIES_COST, held, moved)


def swapped_cores(array):
    return lax.ppermute(array, "core", [(0, 1), (1, 0)])


def pick_body(pool_ref, picks_ref, out_ref, pool, picks, sems):
    fetches = [
        pltpu.make_async_copy(ref, into, sems.at[i])
        for i, (ref, into) in enumerate(((picks_ref, picks), (pool_ref, pool)))
    ]
    for copy in fetches:
        copy.start()
    for copy in fetches:
        copy.wait()
    pool_dev = pool.shape[1]
    copies, steps, _, batch = out_ref.shape
    first = (lax.axis_index("z") * lax.axis_size("x") + lax.axis_index("x")) * pool_dev
    rows = lax.broadcasted_iota(jnp.int32, (pool_dev, batch), 0)
    for step in range(steps):
        chosen = picks[step : step + 1, :] - first
        onehot = (rows == chosen).astype(jnp.float32).astype(jnp.bfloat16)
        feats = jnp.dot(pool[...], onehot, preferred_element_type=jnp.float32).astype(out_ref.dtype)
        for peer in range(copies):
            out_ref[peer, step] = feats


def picked(pool, picks, copies):
    steps, batch = picks.shape
    return pl.pallas_call(
        pick_body,
        out_shape=jax.ShapeDtypeStruct((copies, steps, pool.shape[0], batch), pool.dtype),
        in_specs=[pl.BlockSpec(memory_space=pl.ANY)] * 2,
        out_specs=pl.BlockSpec(memory_space=pltpu.VMEM),
        scratch_shapes=[
            pltpu.VMEM(pool.shape, pool.dtype),
            pltpu.VMEM(picks.shape, picks.dtype),
            pltpu.SemaphoreType.DMA((2,)),
        ],
        cost_estimate=pl.CostEstimate(
            flops=2 * pool.size * batch * steps, bytes_accessed=2 * pool.size, transcendentals=0
        ),
        compiler_params=pltpu.CompilerParams(vmem_limit_bytes=PICK_VMEM << 20),
    )(pool, picks)


def update_body(rate, arrived_ref, current_ref, new_ref, half_ref):
    peers = arrived_ref.shape[0]
    total = arrived_ref[0].astype(jnp.float32)
    for peer in range(1, peers):
        total = total + arrived_ref[peer].astype(jnp.float32)
    new = current_ref[...] - rate * total
    new_ref[...] = new
    half = new.astype(half_ref.dtype)
    for peer in range(peers):
        half_ref[peer] = half


def updated(arrived, current, rate):
    return call(
        functools.partial(update_body, rate),
        [
            jax.ShapeDtypeStruct(current.shape, jnp.float32),
            jax.ShapeDtypeStruct(arrived.shape, jnp.bfloat16),
        ],
        2 * arrived.size,
        arrived,
        current,
    )


def last_body(rate, arrived_ref, current_ref, new_ref):
    total = arrived_ref[0].astype(jnp.float32)
    for peer in range(1, arrived_ref.shape[0]):
        total = total + arrived_ref[peer].astype(jnp.float32)
    turned = jnp.transpose(current_ref[...] - rate * total)
    own, height = new_ref.shape[0], total.shape[0]
    for h in range(LANES // own):
        new_ref[:, height * h : height * (h + 1)] = turned[own * h : own * (h + 1)]


def last_updated(arrived, current, rate, own):
    return call(
        functools.partial(last_body, rate),
        jax.ShapeDtypeStruct((own, current.size // own), jnp.float32),
        2 * arrived.size,
        arrived,
        current,
    )


def on_device(centres, pool, labels, picks, coefs):
    cen_dev = centres.shape[1]
    pool_dev = pool.shape[1]
    batch_dev = picks.shape[1]
    classes, cen_own = coefs.shape
    n_centre, n_sample = lax.axis_size(CENTRE), lax.axis_size(SAMPLE)
    total_centres = cen_dev * n_centre
    total_batch = batch_dev * n_sample
    rate = STEP_GAIN * LOGIT_GAIN / total_batch
    own = batch_dev // n_centre
    fold = LANES // own
    me = lax.axis_index(CENTRE)
    over_z, over_x = lax.axis_size("z"), lax.axis_size("x")
    local_picks = picks - lax.axis_index(SAMPLE) * pool_dev
    centre_sq = jnp.sum(jnp.square(centres.astype(jnp.float32)), axis=0, keepdims=True)

    def own_labels(step):
        chosen = lax.dynamic_slice(local_picks[step], (me * own,), (own,))
        return jnp.tile(jnp.take(labels, chosen, mode="clip"), fold)[None]

    packed = jnp.concatenate([coefs[: classes // 2], coefs[classes // 2 :]], axis=1)

    z_hops = [1 << i for i in reversed(range(over_z.bit_length() - 1))]
    held = packed.astype(jnp.bfloat16)[None]
    for hop in z_hops[:-1]:
        held = doubled(held, "z", hop)
    mine = exchange(picked(pool, picks, lax.axis_size("y")), "y")
    labs = [own_labels(step) for step in range(STEPS)]
    spread_out = last_doubled(held, "z", z_hops[-1], over_x)
    mine, spread_out, centre_sq, packed, labs = lax.optimization_barrier(
        (mine, spread_out, centre_sq, packed, labs)
    )
    coef_parts = exchange(spread_out, "x")
    first, later = assembled(mine, swapped_cores(mine))
    kern = kernel_matrix(first, centres, centre_sq)

    gain = LOGIT_GAIN / total_centres
    logits = partial_logits(coef_parts, kern, n_centre, swap_offsets(z_hops))
    resid = exchange(residual(exchange(logits, CENTRE), labs[0], gain, fold), CENTRE)
    arrived = exchange(partial_grad(resid, kern, n_sample), SAMPLE)
    current, half = updated(arrived, packed, rate)

    kern = kernel_matrix(later, centres, centre_sq)
    coef_parts = exchange(half, SAMPLE).reshape(over_z, over_x, *current.shape)
    arrived = exchange(partial_logits(coef_parts, kern, n_centre), CENTRE)
    resid = exchange(residual(arrived, labs[1], gain, fold), CENTRE)
    arrived = exchange(partial_grad(resid, kern, n_sample), SAMPLE)
    return last_updated(arrived, current, rate, cen_own).T


def solution(mesh):
    sizes = (mesh.shape["centre"] // 2, 2, 8, mesh.shape["sample"] // 8)
    fine = Mesh(mesh.devices.reshape(sizes), (*CENTRE, *SAMPLE))
    placed = (
        P(None, CENTRE),
        P(CENTRE, SAMPLE),
        P(SAMPLE),
        P(None, SAMPLE),
        P(None, (*CENTRE, *SAMPLE)),
    )
    return jax.shard_map(
        on_device,
        mesh=fine,
        in_specs=placed,
        out_specs=P(None, (*CENTRE, *SAMPLE)),
        check_vma=False,
    )
```

```python
import functools

import jax
import jax.numpy as jnp
from jax import lax
from jax.experimental import pallas as pl
from jax.experimental.pallas import tpu as pltpu
from jax.sharding import Mesh, PartitionSpec as P

STEPS = 2


LOGIT_GAIN = 16.0
LENGTH_SCALE = 0.5
STEP_GAIN = 2048.0
EPS = 1e-06

LANES = 128
KERN_VMEM = 48
PICK_VMEM = 60
COPIES_COST = 1000
CENTRE = ("y", "core")
SAMPLE = ("z", "x")


def exchange(parts, axes):
    return lax.all_to_all(parts, axes, 0, 0, tiled=True)


def spread(array, axes):
    peers = lax.axis_size(axes)
    return exchange(jnp.broadcast_to(array[None], (peers, *array.shape)), axes)


def call(body, out, flops, *operands, scratch=()):
    vmem = pl.BlockSpec(memory_space=pltpu.VMEM)
    many = isinstance(out, (list, tuple))
    nbytes = sum(a.size * a.dtype.itemsize for a in operands)
    return pl.pallas_call(
        body,
        out_shape=out,
        in_specs=[vmem] * len(operands),
        out_specs=[vmem] * len(out) if many else vmem,
        scratch_shapes=list(scratch),
        cost_estimate=pl.CostEstimate(flops=flops, bytes_accessed=nbytes, transcendentals=0),
        compiler_params=pltpu.CompilerParams(vmem_limit_bytes=24 << 20),
    )(*operands)


def regroup(blocks, fold):
    width = LANES // fold
    lane_block = lax.broadcasted_iota(jnp.int32, blocks[0].shape, 1) // width
    out = []
    for q in range(fold):
        merged = None
        for k in range(fold):
            shift = width * (k - q) % LANES
            moved = pltpu.roll(blocks[k], shift, 1) if shift else blocks[k]
            merged = moved if merged is None else jnp.where(lane_block == k, moved, merged)
        out.append(merged)
    return out


def logits_body(offsets, coef_ref, kern_ref, out_ref, coef, logits):
    over_z, over_x, height, _ = coef_ref.shape
    if offsets is not None:
        over_z, over_x = over_x, over_z
    for i in range(over_z):
        for p in range(over_x // 2):
            if offsets is None:
                pair = coef_ref[i, 2 * p], coef_ref[i, 2 * p + 1]
                at = LANES * (i * over_x // 2 + p)
            else:
                pair = coef_ref[2 * p, i], coef_ref[2 * p + 1, i]
                at = LANES * (lax.bitwise_xor(lax.axis_index("z"), offsets[i]) * (over_x // 2) + p)
                at = pl.multiple_of(at, LANES)
            halves = regroup([block.astype(jnp.float32) for block in pair], 2)
            for h in range(2):
                coef[height * h : height * (h + 1), pl.ds(at, LANES)] = halves[h]
    logits[...] = lax.dot_general(
        coef[...].astype(jnp.bfloat16),
        kern_ref[...],
        (((1,), (1,)), ((), ())),
        preferred_element_type=jnp.float32,
    )
    receivers, rows, _ = out_ref.shape
    fold = coef.shape[0] // rows
    for group in range(receivers // fold):
        columns = slice(LANES * group, LANES * (group + 1))
        blocks = regroup([logits[rows * q : rows * (q + 1), columns] for q in range(fold)], fold)
        for k in range(fold):
            out_ref[fold * group + k] = blocks[k].astype(out_ref.dtype)


def partial_logits(coef_parts, kern, peers, offsets=None):
    classes = 2 * coef_parts.shape[2]
    batch, centres = kern.shape
    rows = classes * (batch // peers) // LANES
    return call(
        functools.partial(logits_body, offsets),
        jax.ShapeDtypeStruct((peers, rows, LANES), jnp.bfloat16),
        2 * classes * batch * centres,
        coef_parts,
        kern,
        scratch=[pltpu.VMEM((classes, centres), jnp.float32), pltpu.VMEM((classes, batch), jnp.float32)],
    )


def fold_all(row, fold, op):
    while fold > 1:
        row = op(row, pltpu.roll(row, LANES // fold, 1))
        fold //= 2
    return row


def residual_body(gain, fold, arrived_ref, labs_ref, out_ref):
    peers, rows, _ = arrived_ref.shape
    total = arrived_ref[0].astype(jnp.float32)
    for peer in range(1, peers):
        total = total + arrived_ref[peer].astype(jnp.float32)
    logits = total * gain
    top = fold_all(jnp.max(logits, axis=0, keepdims=True), fold, jnp.maximum)
    expo = jnp.exp(logits - top)
    mass = fold_all(jnp.sum(expo, axis=0, keepdims=True), fold, jnp.add)
    probs = expo / mass
    block = lax.broadcasted_iota(jnp.int32, logits.shape, 1) // (LANES // fold)
    class_ids = block * rows + lax.broadcasted_iota(jnp.int32, logits.shape, 0)
    onehot = (class_ids == labs_ref[...]).astype(jnp.float32)
    resid = (probs - onehot).astype(out_ref.dtype)
    for peer in range(peers):
        out_ref[peer] = resid


def residual(arrived, labs, gain, fold):
    return call(
        functools.partial(residual_body, gain, fold),
        jax.ShapeDtypeStruct(arrived.shape, jnp.bfloat16),
        8 * arrived.size,
        arrived,
        labs,
    )


def grad_body(resid_ref, kern_ref, out_ref, resid):
    peers, rows, _ = resid_ref.shape
    classes = resid.shape[0]
    fold = classes // rows
    for group in range(peers // fold):
        blocks = regroup([resid_ref[fold * group + k].astype(jnp.float32) for k in range(fold)], fold)
        for q in range(fold):
            resid[rows * q : rows * (q + 1), LANES * group : LANES * (group + 1)] = blocks[q]
    held = resid[...].astype(jnp.bfloat16)
    _, height, _ = out_ref.shape
    step = 4 * LANES
    for start in range(0, kern_ref.shape[1], step):
        grad = jnp.dot(held, kern_ref[:, start : start + step], preferred_element_type=jnp.float32)
        for at in range(0, step, LANES):
            halves = [grad[height * h : height * (h + 1), at : at + LANES] for h in range(2)]
            first = 2 * (start + at) // LANES
            for i, block in enumerate(regroup(halves, 2)):
                out_ref[first + i] = block.astype(out_ref.dtype)


def partial_grad(resid_parts, kern, peers):
    batch, centres = kern.shape
    classes = resid_parts.size // batch
    height = classes * (centres // peers) // LANES
    return call(
        grad_body,
        jax.ShapeDtypeStruct((peers, height, LANES), jnp.bfloat16),
        2 * classes * batch * centres,
        resid_parts,
        kern,
        scratch=[pltpu.VMEM((classes, batch), jnp.float32)],
    )


def assemble_body(mine_ref, other_ref, *out_refs):
    core = lax.axis_index("core")
    steps = mine_ref.shape[1]
    for step in range(steps):
        for i in range(mine_ref.shape[0]):
            for which, ref in ((core, mine_ref), (1 - core, other_ref)):
                out_refs[step][i, which] = ref[i, step]


def assembled(mine, other):
    blocks, steps, rows, batch = mine.shape
    feats = jax.ShapeDtypeStruct((blocks, 2, rows, batch), mine.dtype)
    return call(assemble_body, [feats] * steps, mine.size, mine, other)


def laplace_body(feats_ref, centres_ref, centre_sq_ref, out_ref, held, sems):
    width, centres = held.shape
    batch = feats_ref.shape[-1]
    rows = width // sems.shape[0]
    columns = 2 * LANES
    staged = [
        pltpu.make_async_copy(
            centres_ref.at[pl.ds(rows * i, rows)], held.at[pl.ds(rows * i, rows)], sems.at[i]
        )
        for i in range(sems.shape[0])
    ]
    for copy in staged:
        copy.start()
    feats = feats_ref[...].reshape(width, batch)
    squares = jnp.sum(jnp.square(feats.astype(jnp.float32)), axis=0, keepdims=True)
    sample_sq = jnp.transpose(jnp.broadcast_to(squares, (LANES, batch)))[:, :1]
    samples = jnp.transpose(feats)
    for copy in staged:
        copy.wait()
    for start in range(0, centres, columns):
        part = slice(start, start + columns)
        cross = jnp.dot(samples, held[:, part], preferred_element_type=jnp.float32)
        mean_sq = (sample_sq + centre_sq_ref[:, part] - 2.0 * cross) * (1.0 / width) + EPS
        mean_sq = jnp.maximum(mean_sq, 1e-37)
        root = mean_sq * lax.rsqrt(mean_sq)
        out_ref[:, part] = jnp.exp(root * (-1.0 / LENGTH_SCALE)).astype(out_ref.dtype)


def kernel_matrix(feats, centres, centre_sq):
    columns, batch = centres.shape[1], feats.shape[-1]
    vmem, anywhere = pl.BlockSpec(memory_space=pltpu.VMEM), pl.BlockSpec(memory_space=pl.ANY)
    return pl.pallas_call(
        laplace_body,
        out_shape=jax.ShapeDtypeStruct((batch, columns), jnp.bfloat16),
        in_specs=[vmem, anywhere, vmem],
        out_specs=vmem,
        scratch_shapes=[pltpu.VMEM(centres.shape, jnp.bfloat16), pltpu.SemaphoreType.DMA((4,))],
        cost_estimate=pl.CostEstimate(
            flops=2 * centres.size * batch, bytes_accessed=2 * centres.size, transcendentals=0
        ),
        compiler_params=pltpu.CompilerParams(vmem_limit_bytes=KERN_VMEM << 20),
    )(feats, centres, centre_sq)


def swap_offsets(hops):
    offsets = [0]
    for hop in hops:
        offsets = offsets + [o ^ hop for o in offsets]
    return offsets


def doubled(held, axis, hop):
    pairs = [(i, i ^ hop) for i in range(lax.axis_size(axis))]
    return jnp.concatenate([held, lax.ppermute(held, axis, pairs)])


def copies_body(held_ref, moved_ref, out_ref):
    near = held_ref.shape[0]
    for copy in range(out_ref.shape[0]):
        out_ref[copy, :near] = held_ref[...]
        out_ref[copy, near:] = moved_ref[...]


def last_doubled(held, axis, hop, copies):
    pairs = [(i, i ^ hop) for i in range(lax.axis_size(axis))]
    moved = lax.ppermute(held, axis, pairs)
    out = jax.ShapeDtypeStruct((copies, 2 * held.shape[0], *held.shape[1:]), held.dtype)
    return call(copies_body, out, COPIES_COST, held, moved)


def swapped_cores(array):
    return lax.ppermute(array, "core", [(0, 1), (1, 0)])


def pick_body(pool_ref, picks_ref, out_ref, pool, picks, sems):
    fetches = [
        pltpu.make_async_copy(ref, into, sems.at[i])
        for i, (ref, into) in enumerate(((picks_ref, picks), (pool_ref, pool)))
    ]
    for copy in fetches:
        copy.start()
    for copy in fetches:
        copy.wait()
    pool_dev = pool.shape[1]
    copies, steps, _, batch = out_ref.shape
    first = (lax.axis_index("z") * lax.axis_size("x") + lax.axis_index("x")) * pool_dev
    rows = lax.broadcasted_iota(jnp.int32, (pool_dev, batch), 0)
    for step in range(steps):
        chosen = picks[step : step + 1, :] - first
        onehot = (rows == chosen).astype(jnp.float32).astype(jnp.bfloat16)
        feats = jnp.dot(pool[...], onehot, preferred_element_type=jnp.float32).astype(out_ref.dtype)
        for peer in range(copies):
            out_ref[peer, step] = feats


def picked(pool, picks, copies):
    steps, batch = picks.shape
    return pl.pallas_call(
        pick_body,
        out_shape=jax.ShapeDtypeStruct((copies, steps, pool.shape[0], batch), pool.dtype),
        in_specs=[pl.BlockSpec(memory_space=pl.ANY)] * 2,
        out_specs=pl.BlockSpec(memory_space=pltpu.VMEM),
        scratch_shapes=[
            pltpu.VMEM(pool.shape, pool.dtype),
            pltpu.VMEM(picks.shape, picks.dtype),
            pltpu.SemaphoreType.DMA((2,)),
        ],
        cost_estimate=pl.CostEstimate(
            flops=2 * pool.size * batch * steps, bytes_accessed=2 * pool.size, transcendentals=0
        ),
        compiler_params=pltpu.CompilerParams(vmem_limit_bytes=PICK_VMEM << 20),
    )(pool, picks)


def update_body(rate, arrived_ref, current_ref, new_ref, half_ref):
    peers = arrived_ref.shape[0]
    total = arrived_ref[0].astype(jnp.float32)
    for peer in range(1, peers):
        total = total + arrived_ref[peer].astype(jnp.float32)
    new = current_ref[...] - rate * total
    new_ref[...] = new
    half = new.astype(half_ref.dtype)
    for peer in range(peers):
        half_ref[peer] = half


def updated(arrived, current, rate):
    return call(
        functools.partial(update_body, rate),
        [
            jax.ShapeDtypeStruct(current.shape, jnp.float32),
            jax.ShapeDtypeStruct(arrived.shape, jnp.bfloat16),
        ],
        2 * arrived.size,
        arrived,
        current,
    )


def last_body(rate, arrived_ref, current_ref, new_ref):
    total = arrived_ref[0].astype(jnp.float32)
    for peer in range(1, arrived_ref.shape[0]):
        total = total + arrived_ref[peer].astype(jnp.float32)
    turned = jnp.transpose(current_ref[...] - rate * total)
    own, height = new_ref.shape[0], total.shape[0]
    for h in range(LANES // own):
        new_ref[:, height * h : height * (h + 1)] = turned[own * h : own * (h + 1)]


def last_updated(arrived, current, rate, own):
    return call(
        functools.partial(last_body, rate),
        jax.ShapeDtypeStruct((own, current.size // own), jnp.float32),
        2 * arrived.size,
        arrived,
        current,
    )


def on_device(centres, pool, labels, picks, coefs):
    cen_dev = centres.shape[1]
    pool_dev = pool.shape[1]
    batch_dev = picks.shape[1]
    classes, cen_own = coefs.shape
    n_centre, n_sample = lax.axis_size(CENTRE), lax.axis_size(SAMPLE)
    total_centres = cen_dev * n_centre
    total_batch = batch_dev * n_sample
    rate = STEP_GAIN * LOGIT_GAIN / total_batch
    own = batch_dev // n_centre
    fold = LANES // own
    me = lax.axis_index(CENTRE)
    over_z, over_x = lax.axis_size("z"), lax.axis_size("x")
    local_picks = picks - lax.axis_index(SAMPLE) * pool_dev
    centre_sq = jnp.sum(jnp.square(centres.astype(jnp.float32)), axis=0, keepdims=True)

    def own_labels(step):
        chosen = lax.dynamic_slice(local_picks[step], (me * own,), (own,))
        return jnp.tile(jnp.take(labels, chosen, mode="clip"), fold)[None]

    packed = jnp.concatenate([coefs[: classes // 2], coefs[classes // 2 :]], axis=1)

    z_hops = [1 << i for i in reversed(range(over_z.bit_length() - 1))]
    held = packed.astype(jnp.bfloat16)[None]
    for hop in z_hops[:-1]:
        held = doubled(held, "z", hop)
    mine = exchange(picked(pool, picks, lax.axis_size("y")), "y")
    labs = [own_labels(step) for step in range(STEPS)]
    spread_out = last_doubled(held, "z", z_hops[-1], over_x)
    mine, spread_out, centre_sq, packed, labs = lax.optimization_barrier(
        (mine, spread_out, centre_sq, packed, labs)
    )
    coef_parts = exchange(spread_out, "x")
    first, later = assembled(mine, swapped_cores(mine))
    kern = kernel_matrix(first, centres, centre_sq)

    gain = LOGIT_GAIN / total_centres
    logits = partial_logits(coef_parts, kern, n_centre, swap_offsets(z_hops))
    resid = exchange(residual(exchange(logits, CENTRE), labs[0], gain, fold), CENTRE)
    arrived = exchange(partial_grad(resid, kern, n_sample), SAMPLE)
    current, half = updated(arrived, packed, rate)

    kern = kernel_matrix(later, centres, centre_sq)
    coef_parts = exchange(half, SAMPLE).reshape(over_z, over_x, *current.shape)
    arrived = exchange(partial_logits(coef_parts, kern, n_centre), CENTRE)
    resid = exchange(residual(arrived, labs[1], gain, fold), CENTRE)
    arrived = exchange(partial_grad(resid, kern, n_sample), SAMPLE)
    return last_updated(arrived, current, rate, cen_own).T


def solution(mesh):
    sizes = (mesh.shape["centre"] // 2, 2, 8, mesh.shape["sample"] // 8)
    fine = Mesh(mesh.devices.reshape(sizes), (*CENTRE, *SAMPLE))
    placed = (
        P(None, CENTRE),
        P(CENTRE, SAMPLE),
        P(SAMPLE),
        P(None, SAMPLE),
        P(None, (*CENTRE, *SAMPLE)),
    )
    return jax.shard_map(
        on_device,
        mesh=fine,
        in_specs=placed,
        out_specs=P(None, (*CENTRE, *SAMPLE)),
        check_vma=False,
    )
```

```python
import functools

import jax
import jax.numpy as jnp
from jax import lax
from jax.experimental import pallas as pl
from jax.experimental.pallas import tpu as pltpu
from jax.sharding import Mesh, PartitionSpec as P

STEPS = 2


LOGIT_GAIN = 16.0
LENGTH_SCALE = 0.5
STEP_GAIN = 2048.0
EPS = 1e-06

LANES = 128
KERN_VMEM = 48
PICK_VMEM = 60
CENTRE = ("y", "core")
SAMPLE = ("z", "x")


def exchange(parts, axes):
    return lax.all_to_all(parts, axes, 0, 0, tiled=True)


def spread(array, axes):
    peers = lax.axis_size(axes)
    return exchange(jnp.broadcast_to(array[None], (peers, *array.shape)), axes)


def call(body, out, flops, *operands, scratch=()):
    vmem = pl.BlockSpec(memory_space=pltpu.VMEM)
    many = isinstance(out, (list, tuple))
    nbytes = sum(a.size * a.dtype.itemsize for a in operands)
    return pl.pallas_call(
        body,
        out_shape=out,
        in_specs=[vmem] * len(operands),
        out_specs=[vmem] * len(out) if many else vmem,
        scratch_shapes=list(scratch),
        cost_estimate=pl.CostEstimate(flops=flops, bytes_accessed=nbytes, transcendentals=0),
        compiler_params=pltpu.CompilerParams(vmem_limit_bytes=24 << 20),
    )(*operands)


def regroup(blocks, fold):
    width = LANES // fold
    lane_block = lax.broadcasted_iota(jnp.int32, blocks[0].shape, 1) // width
    out = []
    for q in range(fold):
        merged = None
        for k in range(fold):
            shift = width * (k - q) % LANES
            moved = pltpu.roll(blocks[k], shift, 1) if shift else blocks[k]
            merged = moved if merged is None else jnp.where(lane_block == k, moved, merged)
        out.append(merged)
    return out


def first_coefs(offsets, part_refs):
    z, x = lax.axis_index("z"), lax.axis_index("x")
    odd = lax.rem(x, 2) == 1
    for i, offset in enumerate(offsets):
        for k in range(0, len(part_refs), 2):
            near, far = [part_refs[k + j][i].astype(jnp.float32) for j in range(2)]
            pair = jnp.where(odd, far, near), jnp.where(odd, near, far)
            row = lax.bitwise_xor(z, offset) * (len(part_refs) // 2)
            yield pair, pl.multiple_of(LANES * (row + lax.bitwise_xor(x // 2, k // 2)), LANES)


def later_coefs(coef_ref):
    for p in range(coef_ref.shape[0] // 2):
        yield [coef_ref[2 * p + j].astype(jnp.float32) for j in range(2)], LANES * p


def logits_body(offsets, *refs):
    *part_refs, kern_ref, out_ref, coef, logits = refs
    height = part_refs[0].shape[1]
    pairs = later_coefs(*part_refs) if offsets is None else first_coefs(offsets, part_refs)
    for pair, at in pairs:
        halves = regroup(pair, 2)
        for h in range(2):
            coef[height * h : height * (h + 1), pl.ds(at, LANES)] = halves[h]
    logits[...] = lax.dot_general(
        coef[...].astype(jnp.bfloat16),
        kern_ref[...],
        (((1,), (1,)), ((), ())),
        preferred_element_type=jnp.float32,
    )
    receivers, rows, _ = out_ref.shape
    fold = coef.shape[0] // rows
    for group in range(receivers // fold):
        columns = slice(LANES * group, LANES * (group + 1))
        blocks = regroup([logits[rows * q : rows * (q + 1), columns] for q in range(fold)], fold)
        for k in range(fold):
            out_ref[fold * group + k] = blocks[k].astype(out_ref.dtype)


def partial_logits(coef_parts, kern, peers, offsets=None):
    classes = 2 * coef_parts[0].shape[1]
    batch, centres = kern.shape
    rows = classes * (batch // peers) // LANES
    return call(
        functools.partial(logits_body, offsets),
        jax.ShapeDtypeStruct((peers, rows, LANES), jnp.bfloat16),
        2 * classes * batch * centres,
        *coef_parts,
        kern,
        scratch=[pltpu.VMEM((classes, centres), jnp.float32), pltpu.VMEM((classes, batch), jnp.float32)],
    )


def fold_all(row, fold, op):
    while fold > 1:
        row = op(row, pltpu.roll(row, LANES // fold, 1))
        fold //= 2
    return row


def residual_body(gain, fold, arrived_ref, labs_ref, out_ref):
    peers, rows, _ = arrived_ref.shape
    total = arrived_ref[0].astype(jnp.float32)
    for peer in range(1, peers):
        total = total + arrived_ref[peer].astype(jnp.float32)
    logits = total * gain
    top = fold_all(jnp.max(logits, axis=0, keepdims=True), fold, jnp.maximum)
    expo = jnp.exp(logits - top)
    mass = fold_all(jnp.sum(expo, axis=0, keepdims=True), fold, jnp.add)
    probs = expo / mass
    block = lax.broadcasted_iota(jnp.int32, logits.shape, 1) // (LANES // fold)
    class_ids = block * rows + lax.broadcasted_iota(jnp.int32, logits.shape, 0)
    onehot = (class_ids == labs_ref[...]).astype(jnp.float32)
    resid = (probs - onehot).astype(out_ref.dtype)
    for peer in range(peers):
        out_ref[peer] = resid


def residual(arrived, labs, gain, fold):
    return call(
        functools.partial(residual_body, gain, fold),
        jax.ShapeDtypeStruct(arrived.shape, jnp.bfloat16),
        8 * arrived.size,
        arrived,
        labs,
    )


def grad_body(resid_ref, kern_ref, out_ref, resid):
    peers, rows, _ = resid_ref.shape
    classes = resid.shape[0]
    fold = classes // rows
    for group in range(peers // fold):
        blocks = regroup([resid_ref[fold * group + k].astype(jnp.float32) for k in range(fold)], fold)
        for q in range(fold):
            resid[rows * q : rows * (q + 1), LANES * group : LANES * (group + 1)] = blocks[q]
    held = resid[...].astype(jnp.bfloat16)
    _, height, _ = out_ref.shape
    step = 4 * LANES
    for start in range(0, kern_ref.shape[1], step):
        grad = jnp.dot(held, kern_ref[:, start : start + step], preferred_element_type=jnp.float32)
        for at in range(0, step, LANES):
            halves = [grad[height * h : height * (h + 1), at : at + LANES] for h in range(2)]
            first = 2 * (start + at) // LANES
            for i, block in enumerate(regroup(halves, 2)):
                out_ref[first + i] = block.astype(out_ref.dtype)


def partial_grad(resid_parts, kern, peers):
    batch, centres = kern.shape
    classes = resid_parts.size // batch
    height = classes * (centres // peers) // LANES
    return call(
        grad_body,
        jax.ShapeDtypeStruct((peers, height, LANES), jnp.bfloat16),
        2 * classes * batch * centres,
        resid_parts,
        kern,
        scratch=[pltpu.VMEM((classes, batch), jnp.float32)],
    )


def assemble_body(mine_ref, other_ref, *out_refs):
    core = lax.axis_index("core")
    steps = mine_ref.shape[1]
    for step in range(steps):
        for i in range(mine_ref.shape[0]):
            for which, ref in ((core, mine_ref), (1 - core, other_ref)):
                out_refs[step][i, which] = ref[i, step]


def assembled(mine, other):
    blocks, steps, rows, batch = mine.shape
    feats = jax.ShapeDtypeStruct((blocks, 2, rows, batch), mine.dtype)
    return call(assemble_body, [feats] * steps, mine.size, mine, other)


def laplace_body(feats_ref, centres_ref, centre_sq_ref, out_ref, held, sems):
    width, centres = held.shape
    batch = feats_ref.shape[-1]
    rows = width // sems.shape[0]
    columns = 2 * LANES
    staged = [
        pltpu.make_async_copy(
            centres_ref.at[pl.ds(rows * i, rows)], held.at[pl.ds(rows * i, rows)], sems.at[i]
        )
        for i in range(sems.shape[0])
    ]
    for copy in staged:
        copy.start()
    feats = feats_ref[...].reshape(width, batch)
    squares = jnp.sum(jnp.square(feats.astype(jnp.float32)), axis=0, keepdims=True)
    sample_sq = jnp.transpose(jnp.broadcast_to(squares, (LANES, batch)))[:, :1]
    samples = jnp.transpose(feats)
    for copy in staged:
        copy.wait()
    for start in range(0, centres, columns):
        part = slice(start, start + columns)
        cross = jnp.dot(samples, held[:, part], preferred_element_type=jnp.float32)
        mean_sq = (sample_sq + centre_sq_ref[:, part] - 2.0 * cross) * (1.0 / width) + EPS
        mean_sq = jnp.maximum(mean_sq, 1e-37)
        root = mean_sq * lax.rsqrt(mean_sq)
        out_ref[:, part] = jnp.exp(root * (-1.0 / LENGTH_SCALE)).astype(out_ref.dtype)


def kernel_matrix(feats, centres, centre_sq):
    columns, batch = centres.shape[1], feats.shape[-1]
    vmem, anywhere = pl.BlockSpec(memory_space=pltpu.VMEM), pl.BlockSpec(memory_space=pl.ANY)
    return pl.pallas_call(
        laplace_body,
        out_shape=jax.ShapeDtypeStruct((batch, columns), jnp.bfloat16),
        in_specs=[vmem, anywhere, vmem],
        out_specs=vmem,
        scratch_shapes=[pltpu.VMEM(centres.shape, jnp.bfloat16), pltpu.SemaphoreType.DMA((4,))],
        cost_estimate=pl.CostEstimate(
            flops=2 * centres.size * batch, bytes_accessed=2 * centres.size, transcendentals=0
        ),
        compiler_params=pltpu.CompilerParams(vmem_limit_bytes=KERN_VMEM << 20),
    )(feats, centres, centre_sq)


def swap_offsets(hops):
    offsets = [0]
    for hop in hops:
        offsets = offsets + [o ^ hop for o in offsets]
    return offsets


def doubled(held, axis, hop):
    pairs = [(i, i ^ hop) for i in range(lax.axis_size(axis))]
    return jnp.concatenate([held, lax.ppermute(held, axis, pairs)])


def swapped_cores(array):
    return lax.ppermute(array, "core", [(0, 1), (1, 0)])


def pick_body(pool_ref, picks_ref, out_ref, pool, picks, sems):
    fetches = [
        pltpu.make_async_copy(ref, into, sems.at[i])
        for i, (ref, into) in enumerate(((picks_ref, picks), (pool_ref, pool)))
    ]
    for copy in fetches:
        copy.start()
    for copy in fetches:
        copy.wait()
    pool_dev = pool.shape[1]
    copies, steps, _, batch = out_ref.shape
    first = (lax.axis_index("z") * lax.axis_size("x") + lax.axis_index("x")) * pool_dev
    rows = lax.broadcasted_iota(jnp.int32, (pool_dev, batch), 0)
    for step in range(steps):
        chosen = picks[step : step + 1, :] - first
        onehot = (rows == chosen).astype(jnp.float32).astype(jnp.bfloat16)
        feats = jnp.dot(pool[...], onehot, preferred_element_type=jnp.float32).astype(out_ref.dtype)
        for peer in range(copies):
            out_ref[peer, step] = feats


def picked(pool, picks, copies):
    steps, batch = picks.shape
    return pl.pallas_call(
        pick_body,
        out_shape=jax.ShapeDtypeStruct((copies, steps, pool.shape[0], batch), pool.dtype),
        in_specs=[pl.BlockSpec(memory_space=pl.ANY)] * 2,
        out_specs=pl.BlockSpec(memory_space=pltpu.VMEM),
        scratch_shapes=[
            pltpu.VMEM(pool.shape, pool.dtype),
            pltpu.VMEM(picks.shape, picks.dtype),
            pltpu.SemaphoreType.DMA((2,)),
        ],
        cost_estimate=pl.CostEstimate(
            flops=2 * pool.size * batch * steps, bytes_accessed=2 * pool.size, transcendentals=0
        ),
        compiler_params=pltpu.CompilerParams(vmem_limit_bytes=PICK_VMEM << 20),
    )(pool, picks)


def update_body(rate, arrived_ref, current_ref, new_ref, half_ref):
    peers = arrived_ref.shape[0]
    total = arrived_ref[0].astype(jnp.float32)
    for peer in range(1, peers):
        total = total + arrived_ref[peer].astype(jnp.float32)
    new = current_ref[...] - rate * total
    new_ref[...] = new
    half = new.astype(half_ref.dtype)
    for peer in range(peers):
        half_ref[peer] = half


def updated(arrived, current, rate):
    return call(
        functools.partial(update_body, rate),
        [
            jax.ShapeDtypeStruct(current.shape, jnp.float32),
            jax.ShapeDtypeStruct(arrived.shape, jnp.bfloat16),
        ],
        2 * arrived.size,
        arrived,
        current,
    )


def last_body(rate, arrived_ref, current_ref, new_ref):
    total = arrived_ref[0].astype(jnp.float32)
    for peer in range(1, arrived_ref.shape[0]):
        total = total + arrived_ref[peer].astype(jnp.float32)
    turned = jnp.transpose(current_ref[...] - rate * total)
    own, height = new_ref.shape[0], total.shape[0]
    for h in range(LANES // own):
        new_ref[:, height * h : height * (h + 1)] = turned[own * h : own * (h + 1)]


def last_updated(arrived, current, rate, own):
    return call(
        functools.partial(last_body, rate),
        jax.ShapeDtypeStruct((own, current.size // own), jnp.float32),
        2 * arrived.size,
        arrived,
        current,
    )


def on_device(centres, pool, labels, picks, coefs):
    cen_dev = centres.shape[1]
    pool_dev = pool.shape[1]
    batch_dev = picks.shape[1]
    classes, cen_own = coefs.shape
    n_centre, n_sample = lax.axis_size(CENTRE), lax.axis_size(SAMPLE)
    total_centres = cen_dev * n_centre
    total_batch = batch_dev * n_sample
    rate = STEP_GAIN * LOGIT_GAIN / total_batch
    own = batch_dev // n_centre
    fold = LANES // own
    me = lax.axis_index(CENTRE)
    over_z, over_x = lax.axis_size("z"), lax.axis_size("x")
    local_picks = picks - lax.axis_index(SAMPLE) * pool_dev
    centre_sq = jnp.sum(jnp.square(centres.astype(jnp.float32)), axis=0, keepdims=True)

    def own_labels(step):
        chosen = lax.dynamic_slice(local_picks[step], (me * own,), (own,))
        return jnp.tile(jnp.take(labels, chosen, mode="clip"), fold)[None]

    packed = jnp.concatenate([coefs[: classes // 2], coefs[classes // 2 :]], axis=1)

    z_hops = [1 << i for i in reversed(range(over_z.bit_length() - 1))]
    held = packed.astype(jnp.bfloat16)[None]
    for hop in z_hops:
        held = doubled(held, "z", hop)
    coef_parts = [held] + [
        lax.ppermute(held, "x", [(i, i ^ k) for i in range(over_x)]) for k in range(1, over_x)
    ]
    mine = exchange(picked(pool, picks, lax.axis_size("y")), "y")
    labs = [own_labels(step) for step in range(STEPS)]
    mine, held, centre_sq, packed, labs = lax.optimization_barrier(
        (mine, held, centre_sq, packed, labs)
    )
    first, later = assembled(mine, swapped_cores(mine))
    kern = kernel_matrix(first, centres, centre_sq)

    gain = LOGIT_GAIN / total_centres
    logits = partial_logits(coef_parts, kern, n_centre, swap_offsets(z_hops))
    resid = exchange(residual(exchange(logits, CENTRE), labs[0], gain, fold), CENTRE)
    arrived = exchange(partial_grad(resid, kern, n_sample), SAMPLE)
    current, half = updated(arrived, packed, rate)

    kern = kernel_matrix(later, centres, centre_sq)
    coef_parts = [exchange(half, SAMPLE)]
    arrived = exchange(partial_logits(coef_parts, kern, n_centre), CENTRE)
    resid = exchange(residual(arrived, labs[1], gain, fold), CENTRE)
    arrived = exchange(partial_grad(resid, kern, n_sample), SAMPLE)
    return last_updated(arrived, current, rate, cen_own).T


def solution(mesh):
    sizes = (mesh.shape["centre"] // 2, 2, 8, mesh.shape["sample"] // 8)
    fine = Mesh(mesh.devices.reshape(sizes), (*CENTRE, *SAMPLE))
    placed = (
        P(None, CENTRE),
        P(CENTRE, SAMPLE),
        P(SAMPLE),
        P(None, SAMPLE),
        P(None, (*CENTRE, *SAMPLE)),
    )
    return jax.shard_map(
        on_device,
        mesh=fine,
        in_specs=placed,
        out_specs=P(None, (*CENTRE, *SAMPLE)),
        check_vma=False,
    )
```

```python
import functools

import jax
import jax.numpy as jnp
from jax import lax
from jax.experimental import pallas as pl
from jax.experimental.pallas import tpu as pltpu
from jax.sharding import Mesh, PartitionSpec as P

STEPS = 2


LOGIT_GAIN = 16.0
LENGTH_SCALE = 0.5
STEP_GAIN = 2048.0
EPS = 1e-06

LANES = 128
KERN_VMEM = 48
PICK_VMEM = 60
JOIN_COST = 4_000_000_000
CENTRE = ("y", "core")
SAMPLE = ("z", "x")


def exchange(parts, axes):
    return lax.all_to_all(parts, axes, 0, 0, tiled=True)


def spread(array, axes):
    peers = lax.axis_size(axes)
    return exchange(jnp.broadcast_to(array[None], (peers, *array.shape)), axes)


def call(body, out, flops, *operands, scratch=()):
    vmem = pl.BlockSpec(memory_space=pltpu.VMEM)
    many = isinstance(out, (list, tuple))
    nbytes = sum(a.size * a.dtype.itemsize for a in operands)
    return pl.pallas_call(
        body,
        out_shape=out,
        in_specs=[vmem] * len(operands),
        out_specs=[vmem] * len(out) if many else vmem,
        scratch_shapes=list(scratch),
        cost_estimate=pl.CostEstimate(flops=flops, bytes_accessed=nbytes, transcendentals=0),
        compiler_params=pltpu.CompilerParams(vmem_limit_bytes=24 << 20),
    )(*operands)


def regroup(blocks, fold):
    width = LANES // fold
    lane_block = lax.broadcasted_iota(jnp.int32, blocks[0].shape, 1) // width
    out = []
    for q in range(fold):
        merged = None
        for k in range(fold):
            shift = width * (k - q) % LANES
            moved = pltpu.roll(blocks[k], shift, 1) if shift else blocks[k]
            merged = moved if merged is None else jnp.where(lane_block == k, moved, merged)
        out.append(merged)
    return out


def first_coefs(offsets, part_refs):
    z, x = lax.axis_index("z"), lax.axis_index("x")
    odd = lax.rem(x, 2) == 1
    for i, offset in enumerate(offsets):
        for k in range(0, len(part_refs), 2):
            near, far = [part_refs[k + j][i].astype(jnp.float32) for j in range(2)]
            pair = jnp.where(odd, far, near), jnp.where(odd, near, far)
            row = lax.bitwise_xor(z, offset) * (len(part_refs) // 2)
            yield pair, pl.multiple_of(LANES * (row + lax.bitwise_xor(x // 2, k // 2)), LANES)


def later_coefs(coef_ref):
    for p in range(coef_ref.shape[0] // 2):
        yield [coef_ref[2 * p + j].astype(jnp.float32) for j in range(2)], LANES * p


def logits_body(offsets, *refs):
    *part_refs, kern_ref, out_ref, coef, logits = refs
    height = part_refs[0].shape[1]
    pairs = later_coefs(*part_refs) if offsets is None else first_coefs(offsets, part_refs)
    for pair, at in pairs:
        halves = regroup(pair, 2)
        for h in range(2):
            coef[height * h : height * (h + 1), pl.ds(at, LANES)] = halves[h]
    logits[...] = lax.dot_general(
        coef[...].astype(jnp.bfloat16),
        kern_ref[...],
        (((1,), (1,)), ((), ())),
        preferred_element_type=jnp.float32,
    )
    receivers, rows, _ = out_ref.shape
    fold = coef.shape[0] // rows
    for group in range(receivers // fold):
        columns = slice(LANES * group, LANES * (group + 1))
        blocks = regroup([logits[rows * q : rows * (q + 1), columns] for q in range(fold)], fold)
        for k in range(fold):
            out_ref[fold * group + k] = blocks[k].astype(out_ref.dtype)


def partial_logits(coef_parts, kern, peers, offsets=None):
    classes = 2 * coef_parts[0].shape[1]
    batch, centres = kern.shape
    rows = classes * (batch // peers) // LANES
    return call(
        functools.partial(logits_body, offsets),
        jax.ShapeDtypeStruct((peers, rows, LANES), jnp.bfloat16),
        2 * classes * batch * centres,
        *coef_parts,
        kern,
        scratch=[pltpu.VMEM((classes, centres), jnp.float32), pltpu.VMEM((classes, batch), jnp.float32)],
    )


def fold_all(row, fold, op):
    while fold > 1:
        row = op(row, pltpu.roll(row, LANES // fold, 1))
        fold //= 2
    return row


def residual_body(gain, fold, arrived_ref, labs_ref, out_ref):
    peers, rows, _ = arrived_ref.shape
    total = arrived_ref[0].astype(jnp.float32)
    for peer in range(1, peers):
        total = total + arrived_ref[peer].astype(jnp.float32)
    logits = total * gain
    top = fold_all(jnp.max(logits, axis=0, keepdims=True), fold, jnp.maximum)
    expo = jnp.exp(logits - top)
    mass = fold_all(jnp.sum(expo, axis=0, keepdims=True), fold, jnp.add)
    probs = expo / mass
    block = lax.broadcasted_iota(jnp.int32, logits.shape, 1) // (LANES // fold)
    class_ids = block * rows + lax.broadcasted_iota(jnp.int32, logits.shape, 0)
    onehot = (class_ids == labs_ref[...]).astype(jnp.float32)
    resid = (probs - onehot).astype(out_ref.dtype)
    for peer in range(peers):
        out_ref[peer] = resid


def residual(arrived, labs, gain, fold):
    return call(
        functools.partial(residual_body, gain, fold),
        jax.ShapeDtypeStruct(arrived.shape, jnp.bfloat16),
        8 * arrived.size,
        arrived,
        labs,
    )


def grad_body(resid_ref, kern_ref, out_ref, resid):
    peers, rows, _ = resid_ref.shape
    classes = resid.shape[0]
    fold = classes // rows
    for group in range(peers // fold):
        blocks = regroup([resid_ref[fold * group + k].astype(jnp.float32) for k in range(fold)], fold)
        for q in range(fold):
            resid[rows * q : rows * (q + 1), LANES * group : LANES * (group + 1)] = blocks[q]
    held = resid[...].astype(jnp.bfloat16)
    _, height, _ = out_ref.shape
    step = 4 * LANES
    for start in range(0, kern_ref.shape[1], step):
        grad = jnp.dot(held, kern_ref[:, start : start + step], preferred_element_type=jnp.float32)
        for at in range(0, step, LANES):
            halves = [grad[height * h : height * (h + 1), at : at + LANES] for h in range(2)]
            first = 2 * (start + at) // LANES
            for i, block in enumerate(regroup(halves, 2)):
                out_ref[first + i] = block.astype(out_ref.dtype)


def partial_grad(resid_parts, kern, peers):
    batch, centres = kern.shape
    classes = resid_parts.size // batch
    height = classes * (centres // peers) // LANES
    return call(
        grad_body,
        jax.ShapeDtypeStruct((peers, height, LANES), jnp.bfloat16),
        2 * classes * batch * centres,
        resid_parts,
        kern,
        scratch=[pltpu.VMEM((classes, batch), jnp.float32)],
    )


def assemble_body(mine_ref, other_ref, *out_refs):
    core = lax.axis_index("core")
    steps = mine_ref.shape[1]
    for step in range(steps):
        for i in range(mine_ref.shape[0]):
            for which, ref in ((core, mine_ref), (1 - core, other_ref)):
                out_refs[step][i, which] = ref[i, step]


def assembled(mine, other):
    blocks, steps, rows, batch = mine.shape
    feats = jax.ShapeDtypeStruct((blocks, 2, rows, batch), mine.dtype)
    return call(assemble_body, [feats] * steps, mine.size, mine, other)


def laplace_body(feats_ref, centres_ref, centre_sq_ref, out_ref, held, sems):
    width, centres = held.shape
    batch = feats_ref.shape[-1]
    rows = width // sems.shape[0]
    columns = 2 * LANES
    staged = [
        pltpu.make_async_copy(
            centres_ref.at[pl.ds(rows * i, rows)], held.at[pl.ds(rows * i, rows)], sems.at[i]
        )
        for i in range(sems.shape[0])
    ]
    for copy in staged:
        copy.start()
    feats = feats_ref[...].reshape(width, batch)
    squares = jnp.sum(jnp.square(feats.astype(jnp.float32)), axis=0, keepdims=True)
    sample_sq = jnp.transpose(jnp.broadcast_to(squares, (LANES, batch)))[:, :1]
    samples = jnp.transpose(feats)
    for copy in staged:
        copy.wait()
    for start in range(0, centres, columns):
        part = slice(start, start + columns)
        cross = jnp.dot(samples, held[:, part], preferred_element_type=jnp.float32)
        mean_sq = (sample_sq + centre_sq_ref[:, part] - 2.0 * cross) * (1.0 / width) + EPS
        mean_sq = jnp.maximum(mean_sq, 1e-37)
        root = mean_sq * lax.rsqrt(mean_sq)
        out_ref[:, part] = jnp.exp(root * (-1.0 / LENGTH_SCALE)).astype(out_ref.dtype)


def kernel_matrix(feats, centres, centre_sq):
    columns, batch = centres.shape[1], feats.shape[-1]
    vmem, anywhere = pl.BlockSpec(memory_space=pltpu.VMEM), pl.BlockSpec(memory_space=pl.ANY)
    return pl.pallas_call(
        laplace_body,
        out_shape=jax.ShapeDtypeStruct((batch, columns), jnp.bfloat16),
        in_specs=[vmem, anywhere, vmem],
        out_specs=vmem,
        scratch_shapes=[pltpu.VMEM(centres.shape, jnp.bfloat16), pltpu.SemaphoreType.DMA((4,))],
        cost_estimate=pl.CostEstimate(
            flops=2 * centres.size * batch, bytes_accessed=2 * centres.size, transcendentals=0
        ),
        compiler_params=pltpu.CompilerParams(vmem_limit_bytes=KERN_VMEM << 20),
    )(feats, centres, centre_sq)


def swap_offsets(hops):
    offsets = [0]
    for hop in hops:
        offsets = offsets + [o ^ hop for o in offsets]
    return offsets


def doubled(held, axis, hop):
    pairs = [(i, i ^ hop) for i in range(lax.axis_size(axis))]
    return jnp.concatenate([held, lax.ppermute(held, axis, pairs)])


def joined_body(held_ref, moved_ref, out_ref):
    near = held_ref.shape[0]
    out_ref[:near] = held_ref[...]
    out_ref[near:] = moved_ref[...]


def last_doubled(held, axis, hop):
    moved = lax.ppermute(held, axis, [(i, i ^ hop) for i in range(lax.axis_size(axis))])
    out = jax.ShapeDtypeStruct((2 * held.shape[0], *held.shape[1:]), held.dtype)
    return call(joined_body, out, JOIN_COST, held, moved)


def swapped_cores(array):
    return lax.ppermute(array, "core", [(0, 1), (1, 0)])


def pick_body(pool_ref, picks_ref, out_ref, pool, picks, sems):
    fetches = [
        pltpu.make_async_copy(ref, into, sems.at[i])
        for i, (ref, into) in enumerate(((picks_ref, picks), (pool_ref, pool)))
    ]
    for copy in fetches:
        copy.start()
    for copy in fetches:
        copy.wait()
    pool_dev = pool.shape[1]
    copies, steps, _, batch = out_ref.shape
    first = (lax.axis_index("z") * lax.axis_size("x") + lax.axis_index("x")) * pool_dev
    rows = lax.broadcasted_iota(jnp.int32, (pool_dev, batch), 0)
    for step in range(steps):
        chosen = picks[step : step + 1, :] - first
        onehot = (rows == chosen).astype(jnp.float32).astype(jnp.bfloat16)
        feats = jnp.dot(pool[...], onehot, preferred_element_type=jnp.float32).astype(out_ref.dtype)
        for peer in range(copies):
            out_ref[peer, step] = feats


def picked(pool, picks, copies):
    steps, batch = picks.shape
    return pl.pallas_call(
        pick_body,
        out_shape=jax.ShapeDtypeStruct((copies, steps, pool.shape[0], batch), pool.dtype),
        in_specs=[pl.BlockSpec(memory_space=pl.ANY)] * 2,
        out_specs=pl.BlockSpec(memory_space=pltpu.VMEM),
        scratch_shapes=[
            pltpu.VMEM(pool.shape, pool.dtype),
            pltpu.VMEM(picks.shape, picks.dtype),
            pltpu.SemaphoreType.DMA((2,)),
        ],
        cost_estimate=pl.CostEstimate(
            flops=2 * pool.size * batch * steps, bytes_accessed=2 * pool.size, transcendentals=0
        ),
        compiler_params=pltpu.CompilerParams(vmem_limit_bytes=PICK_VMEM << 20),
    )(pool, picks)


def update_body(rate, arrived_ref, current_ref, new_ref, half_ref):
    peers = arrived_ref.shape[0]
    total = arrived_ref[0].astype(jnp.float32)
    for peer in range(1, peers):
        total = total + arrived_ref[peer].astype(jnp.float32)
    new = current_ref[...] - rate * total
    new_ref[...] = new
    half = new.astype(half_ref.dtype)
    for peer in range(peers):
        half_ref[peer] = half


def updated(arrived, current, rate):
    return call(
        functools.partial(update_body, rate),
        [
            jax.ShapeDtypeStruct(current.shape, jnp.float32),
            jax.ShapeDtypeStruct(arrived.shape, jnp.bfloat16),
        ],
        2 * arrived.size,
        arrived,
        current,
    )


def last_body(rate, arrived_ref, current_ref, new_ref):
    total = arrived_ref[0].astype(jnp.float32)
    for peer in range(1, arrived_ref.shape[0]):
        total = total + arrived_ref[peer].astype(jnp.float32)
    turned = jnp.transpose(current_ref[...] - rate * total)
    own, height = new_ref.shape[0], total.shape[0]
    for h in range(LANES // own):
        new_ref[:, height * h : height * (h + 1)] = turned[own * h : own * (h + 1)]


def last_updated(arrived, current, rate, own):
    return call(
        functools.partial(last_body, rate),
        jax.ShapeDtypeStruct((own, current.size // own), jnp.float32),
        2 * arrived.size,
        arrived,
        current,
    )


def on_device(centres, pool, labels, picks, coefs):
    cen_dev = centres.shape[1]
    pool_dev = pool.shape[1]
    batch_dev = picks.shape[1]
    classes, cen_own = coefs.shape
    n_centre, n_sample = lax.axis_size(CENTRE), lax.axis_size(SAMPLE)
    total_centres = cen_dev * n_centre
    total_batch = batch_dev * n_sample
    rate = STEP_GAIN * LOGIT_GAIN / total_batch
    own = batch_dev // n_centre
    fold = LANES // own
    me = lax.axis_index(CENTRE)
    over_z, over_x = lax.axis_size("z"), lax.axis_size("x")
    local_picks = picks - lax.axis_index(SAMPLE) * pool_dev
    centre_sq = jnp.sum(jnp.square(centres.astype(jnp.float32)), axis=0, keepdims=True)

    def own_labels(step):
        chosen = lax.dynamic_slice(local_picks[step], (me * own,), (own,))
        return jnp.tile(jnp.take(labels, chosen, mode="clip"), fold)[None]

    packed = jnp.concatenate([coefs[: classes // 2], coefs[classes // 2 :]], axis=1)

    z_hops = [1 << i for i in reversed(range(over_z.bit_length() - 1))]
    held = packed.astype(jnp.bfloat16)[None]
    for hop in z_hops[:-1]:
        held = doubled(held, "z", hop)
    held = last_doubled(held, "z", z_hops[-1])
    coef_parts = [held] + [
        lax.ppermute(held, "x", [(i, i ^ k) for i in range(over_x)]) for k in range(1, over_x)
    ]
    mine = exchange(picked(pool, picks, lax.axis_size("y")), "y")
    labs = [own_labels(step) for step in range(STEPS)]
    mine, coef_parts, centre_sq, packed, labs = lax.optimization_barrier(
        (mine, coef_parts, centre_sq, packed, labs)
    )
    first, later = assembled(mine, swapped_cores(mine))
    kern = kernel_matrix(first, centres, centre_sq)

    gain = LOGIT_GAIN / total_centres
    logits = partial_logits(coef_parts, kern, n_centre, swap_offsets(z_hops))
    resid = exchange(residual(exchange(logits, CENTRE), labs[0], gain, fold), CENTRE)
    arrived = exchange(partial_grad(resid, kern, n_sample), SAMPLE)
    current, half = updated(arrived, packed, rate)

    kern = kernel_matrix(later, centres, centre_sq)
    coef_parts = [exchange(half, SAMPLE)]
    arrived = exchange(partial_logits(coef_parts, kern, n_centre), CENTRE)
    resid = exchange(residual(arrived, labs[1], gain, fold), CENTRE)
    arrived = exchange(partial_grad(resid, kern, n_sample), SAMPLE)
    return last_updated(arrived, current, rate, cen_own).T


def solution(mesh):
    sizes = (mesh.shape["centre"] // 2, 2, 8, mesh.shape["sample"] // 8)
    fine = Mesh(mesh.devices.reshape(sizes), (*CENTRE, *SAMPLE))
    placed = (
        P(None, CENTRE),
        P(CENTRE, SAMPLE),
        P(SAMPLE),
        P(None, SAMPLE),
        P(None, (*CENTRE, *SAMPLE)),
    )
    return jax.shard_map(
        on_device,
        mesh=fine,
        in_specs=placed,
        out_specs=P(None, (*CENTRE, *SAMPLE)),
        check_vma=False,
    )
```

```python
import functools

import jax
import jax.numpy as jnp
from jax import lax
from jax.experimental import pallas as pl
from jax.experimental.pallas import tpu as pltpu
from jax.sharding import Mesh, PartitionSpec as P

STEPS = 2


LOGIT_GAIN = 16.0
LENGTH_SCALE = 0.5
STEP_GAIN = 2048.0
EPS = 1e-06

LANES = 128
KERN_VMEM = 48
PICK_VMEM = 60
COPIES_COST = 1000
CENTRE = ("y", "core")
SAMPLE = ("z", "x")


def exchange(parts, axes):
    return lax.all_to_all(parts, axes, 0, 0, tiled=True)


def spread(array, axes):
    peers = lax.axis_size(axes)
    return exchange(jnp.broadcast_to(array[None], (peers, *array.shape)), axes)


def call(body, out, flops, *operands, scratch=()):
    vmem = pl.BlockSpec(memory_space=pltpu.VMEM)
    many = isinstance(out, (list, tuple))
    nbytes = sum(a.size * a.dtype.itemsize for a in operands)
    return pl.pallas_call(
        body,
        out_shape=out,
        in_specs=[vmem] * len(operands),
        out_specs=[vmem] * len(out) if many else vmem,
        scratch_shapes=list(scratch),
        cost_estimate=pl.CostEstimate(flops=flops, bytes_accessed=nbytes, transcendentals=0),
        compiler_params=pltpu.CompilerParams(vmem_limit_bytes=24 << 20),
    )(*operands)


def regroup(blocks, fold):
    width = LANES // fold
    lane_block = lax.broadcasted_iota(jnp.int32, blocks[0].shape, 1) // width
    out = []
    for q in range(fold):
        merged = None
        for k in range(fold):
            shift = width * (k - q) % LANES
            moved = pltpu.roll(blocks[k], shift, 1) if shift else blocks[k]
            merged = moved if merged is None else jnp.where(lane_block == k, moved, merged)
        out.append(merged)
    return out


def logits_body(offsets, coef_ref, kern_ref, out_ref, coef, logits):
    over_z, over_x, height, _ = coef_ref.shape
    if offsets is not None:
        over_z, over_x = over_x, over_z
    for i in range(over_z):
        for p in range(over_x // 2):
            if offsets is None:
                pair = coef_ref[i, 2 * p], coef_ref[i, 2 * p + 1]
                at = LANES * (i * over_x // 2 + p)
            else:
                pair = coef_ref[2 * p, i], coef_ref[2 * p + 1, i]
                at = LANES * (lax.bitwise_xor(lax.axis_index("z"), offsets[i]) * (over_x // 2) + p)
                at = pl.multiple_of(at, LANES)
            halves = regroup([block.astype(jnp.float32) for block in pair], 2)
            for h in range(2):
                coef[height * h : height * (h + 1), pl.ds(at, LANES)] = halves[h]
    logits[...] = lax.dot_general(
        coef[...].astype(jnp.bfloat16),
        kern_ref[...],
        (((1,), (1,)), ((), ())),
        preferred_element_type=jnp.float32,
    )
    receivers, rows, _ = out_ref.shape
    fold = coef.shape[0] // rows
    for group in range(receivers // fold):
        columns = slice(LANES * group, LANES * (group + 1))
        blocks = regroup([logits[rows * q : rows * (q + 1), columns] for q in range(fold)], fold)
        for k in range(fold):
            out_ref[fold * group + k] = blocks[k].astype(out_ref.dtype)


def partial_logits(coef_parts, kern, peers, offsets=None):
    classes = 2 * coef_parts.shape[2]
    batch, centres = kern.shape
    rows = classes * (batch // peers) // LANES
    return call(
        functools.partial(logits_body, offsets),
        jax.ShapeDtypeStruct((peers, rows, LANES), jnp.bfloat16),
        2 * classes * batch * centres,
        coef_parts,
        kern,
        scratch=[pltpu.VMEM((classes, centres), jnp.float32), pltpu.VMEM((classes, batch), jnp.float32)],
    )


def fold_all(row, fold, op):
    while fold > 1:
        row = op(row, pltpu.roll(row, LANES // fold, 1))
        fold //= 2
    return row


def residual_body(gain, fold, arrived_ref, labs_ref, out_ref):
    peers, rows, _ = arrived_ref.shape
    total = arrived_ref[0].astype(jnp.float32)
    for peer in range(1, peers):
        total = total + arrived_ref[peer].astype(jnp.float32)
    logits = total * gain
    top = fold_all(jnp.max(logits, axis=0, keepdims=True), fold, jnp.maximum)
    expo = jnp.exp(logits - top)
    mass = fold_all(jnp.sum(expo, axis=0, keepdims=True), fold, jnp.add)
    probs = expo / mass
    block = lax.broadcasted_iota(jnp.int32, logits.shape, 1) // (LANES // fold)
    class_ids = block * rows + lax.broadcasted_iota(jnp.int32, logits.shape, 0)
    onehot = (class_ids == labs_ref[...]).astype(jnp.float32)
    resid = (probs - onehot).astype(out_ref.dtype)
    for peer in range(peers):
        out_ref[peer] = resid


def residual(arrived, labs, gain, fold):
    return call(
        functools.partial(residual_body, gain, fold),
        jax.ShapeDtypeStruct(arrived.shape, jnp.bfloat16),
        8 * arrived.size,
        arrived,
        labs,
    )


def grad_body(resid_ref, kern_ref, out_ref, resid):
    peers, rows, _ = resid_ref.shape
    classes = resid.shape[0]
    fold = classes // rows
    for group in range(peers // fold):
        blocks = regroup([resid_ref[fold * group + k].astype(jnp.float32) for k in range(fold)], fold)
        for q in range(fold):
            resid[rows * q : rows * (q + 1), LANES * group : LANES * (group + 1)] = blocks[q]
    held = resid[...].astype(jnp.bfloat16)
    _, height, _ = out_ref.shape
    step = 4 * LANES
    for start in range(0, kern_ref.shape[1], step):
        grad = jnp.dot(held, kern_ref[:, start : start + step], preferred_element_type=jnp.float32)
        for at in range(0, step, LANES):
            halves = [grad[height * h : height * (h + 1), at : at + LANES] for h in range(2)]
            first = 2 * (start + at) // LANES
            for i, block in enumerate(regroup(halves, 2)):
                out_ref[first + i] = block.astype(out_ref.dtype)


def partial_grad(resid_parts, kern, peers):
    batch, centres = kern.shape
    classes = resid_parts.size // batch
    height = classes * (centres // peers) // LANES
    return call(
        grad_body,
        jax.ShapeDtypeStruct((peers, height, LANES), jnp.bfloat16),
        2 * classes * batch * centres,
        resid_parts,
        kern,
        scratch=[pltpu.VMEM((classes, batch), jnp.float32)],
    )


def assemble_body(mine_ref, other_ref, *out_refs):
    core = lax.axis_index("core")
    steps = mine_ref.shape[1]
    for step in range(steps):
        for i in range(mine_ref.shape[0]):
            for which, ref in ((core, mine_ref), (1 - core, other_ref)):
                out_refs[step][i, which] = ref[i, step]


def assembled(mine, other):
    blocks, steps, rows, batch = mine.shape
    feats = jax.ShapeDtypeStruct((blocks, 2, rows, batch), mine.dtype)
    return call(assemble_body, [feats] * steps, mine.size, mine, other)


def laplace_body(feats_ref, centres_ref, centre_sq_ref, out_ref, held, sems):
    width, centres = held.shape
    batch = feats_ref.shape[-1]
    rows = width // sems.shape[0]
    columns = 2 * LANES
    staged = [
        pltpu.make_async_copy(
            centres_ref.at[pl.ds(rows * i, rows)], held.at[pl.ds(rows * i, rows)], sems.at[i]
        )
        for i in range(sems.shape[0])
    ]
    for copy in staged:
        copy.start()
    feats = feats_ref[...].reshape(width, batch)
    squares = jnp.sum(jnp.square(feats.astype(jnp.float32)), axis=0, keepdims=True)
    sample_sq = jnp.transpose(jnp.broadcast_to(squares, (LANES, batch)))[:, :1]
    samples = jnp.transpose(feats)
    for copy in staged:
        copy.wait()
    for start in range(0, centres, columns):
        part = slice(start, start + columns)
        cross = jnp.dot(samples, held[:, part], preferred_element_type=jnp.float32)
        mean_sq = (sample_sq + centre_sq_ref[:, part] - 2.0 * cross) * (1.0 / width) + EPS
        mean_sq = jnp.maximum(mean_sq, 1e-37)
        root = mean_sq * lax.rsqrt(mean_sq)
        out_ref[:, part] = jnp.exp(root * (-1.0 / LENGTH_SCALE)).astype(out_ref.dtype)


def kernel_matrix(feats, centres, centre_sq):
    columns, batch = centres.shape[1], feats.shape[-1]
    vmem, anywhere = pl.BlockSpec(memory_space=pltpu.VMEM), pl.BlockSpec(memory_space=pl.ANY)
    return pl.pallas_call(
        laplace_body,
        out_shape=jax.ShapeDtypeStruct((batch, columns), jnp.bfloat16),
        in_specs=[vmem, anywhere, vmem],
        out_specs=vmem,
        scratch_shapes=[pltpu.VMEM(centres.shape, jnp.bfloat16), pltpu.SemaphoreType.DMA((4,))],
        cost_estimate=pl.CostEstimate(
            flops=2 * centres.size * batch, bytes_accessed=2 * centres.size, transcendentals=0
        ),
        compiler_params=pltpu.CompilerParams(vmem_limit_bytes=KERN_VMEM << 20),
    )(feats, centres, centre_sq)


def swap_offsets(hops):
    offsets = [0]
    for hop in hops:
        offsets = offsets + [o ^ hop for o in offsets]
    return offsets


def doubled(held, axis, hop):
    pairs = [(i, i ^ hop) for i in range(lax.axis_size(axis))]
    return jnp.concatenate([held, lax.ppermute(held, axis, pairs)])


def copies_body(held_ref, moved_ref, out_ref):
    near = held_ref.shape[0]
    for copy in range(out_ref.shape[0]):
        out_ref[copy, :near] = held_ref[...]
        out_ref[copy, near:] = moved_ref[...]


def last_doubled(held, axis, hop, copies):
    pairs = [(i, i ^ hop) for i in range(lax.axis_size(axis))]
    moved = lax.ppermute(held, axis, pairs)
    out = jax.ShapeDtypeStruct((copies, 2 * held.shape[0], *held.shape[1:]), held.dtype)
    return call(copies_body, out, COPIES_COST, held, moved)


def swapped_cores(array):
    return lax.ppermute(array, "core", [(0, 1), (1, 0)])


def pick_body(pool_ref, picks_ref, coefs_ref, out_ref, packed_ref, half_ref, pool, picks, coefs, sems):
    fetches = [
        pltpu.make_async_copy(ref, into, sems.at[i])
        for i, (ref, into) in enumerate(((coefs_ref, coefs), (picks_ref, picks), (pool_ref, pool)))
    ]
    for copy in fetches:
        copy.start()
    fetches[0].wait()
    height = packed_ref.shape[0]
    columns = coefs.shape[1]
    sides = [coefs[:, at : at + height] for at in range(0, columns, height)]
    packed = jnp.transpose(jnp.concatenate(sides, axis=0))
    packed_ref[...] = packed
    half_ref[0] = packed.astype(half_ref.dtype)
    for copy in fetches[1:]:
        copy.wait()
    pool_dev = pool.shape[1]
    copies, steps, _, batch = out_ref.shape
    first = (lax.axis_index("z") * lax.axis_size("x") + lax.axis_index("x")) * pool_dev
    rows = lax.broadcasted_iota(jnp.int32, (pool_dev, batch), 0)
    for step in range(steps):
        chosen = picks[step : step + 1, :] - first
        onehot = (rows == chosen).astype(jnp.float32).astype(jnp.bfloat16)
        feats = jnp.dot(pool[...], onehot, preferred_element_type=jnp.float32).astype(out_ref.dtype)
        for peer in range(copies):
            out_ref[peer, step] = feats


def picked(pool, picks, coefs, copies):
    steps, batch = picks.shape
    height = coefs.size // LANES
    return pl.pallas_call(
        pick_body,
        out_shape=[
            jax.ShapeDtypeStruct((copies, steps, pool.shape[0], batch), pool.dtype),
            jax.ShapeDtypeStruct((height, LANES), coefs.dtype),
            jax.ShapeDtypeStruct((1, height, LANES), jnp.bfloat16),
        ],
        in_specs=[pl.BlockSpec(memory_space=pl.ANY)] * 3,
        out_specs=[pl.BlockSpec(memory_space=pltpu.VMEM)] * 3,
        scratch_shapes=[
            pltpu.VMEM(pool.shape, pool.dtype),
            pltpu.VMEM(picks.shape, picks.dtype),
            pltpu.VMEM(coefs.shape, coefs.dtype),
            pltpu.SemaphoreType.DMA((3,)),
        ],
        cost_estimate=pl.CostEstimate(
            flops=2 * pool.size * batch * steps, bytes_accessed=2 * pool.size, transcendentals=0
        ),
        compiler_params=pltpu.CompilerParams(vmem_limit_bytes=PICK_VMEM << 20),
    )(pool, picks, coefs)


def update_body(rate, arrived_ref, current_ref, new_ref, half_ref):
    peers = arrived_ref.shape[0]
    total = arrived_ref[0].astype(jnp.float32)
    for peer in range(1, peers):
        total = total + arrived_ref[peer].astype(jnp.float32)
    new = current_ref[...] - rate * total
    new_ref[...] = new
    half = new.astype(half_ref.dtype)
    for peer in range(peers):
        half_ref[peer] = half


def updated(arrived, current, rate):
    return call(
        functools.partial(update_body, rate),
        [
            jax.ShapeDtypeStruct(current.shape, jnp.float32),
            jax.ShapeDtypeStruct(arrived.shape, jnp.bfloat16),
        ],
        2 * arrived.size,
        arrived,
        current,
    )


def last_body(rate, arrived_ref, current_ref, new_ref):
    total = arrived_ref[0].astype(jnp.float32)
    for peer in range(1, arrived_ref.shape[0]):
        total = total + arrived_ref[peer].astype(jnp.float32)
    turned = jnp.transpose(current_ref[...] - rate * total)
    own, height = new_ref.shape[0], total.shape[0]
    for h in range(LANES // own):
        new_ref[:, height * h : height * (h + 1)] = turned[own * h : own * (h + 1)]


def last_updated(arrived, current, rate, own):
    return call(
        functools.partial(last_body, rate),
        jax.ShapeDtypeStruct((own, current.size // own), jnp.float32),
        2 * arrived.size,
        arrived,
        current,
    )


def on_device(centres, pool, labels, picks, coefs):
    cen_dev = centres.shape[1]
    pool_dev = pool.shape[1]
    batch_dev = picks.shape[1]
    classes, cen_own = coefs.shape
    n_centre, n_sample = lax.axis_size(CENTRE), lax.axis_size(SAMPLE)
    total_centres = cen_dev * n_centre
    total_batch = batch_dev * n_sample
    rate = STEP_GAIN * LOGIT_GAIN / total_batch
    own = batch_dev // n_centre
    fold = LANES // own
    me = lax.axis_index(CENTRE)
    over_z, over_x = lax.axis_size("z"), lax.axis_size("x")
    local_picks = picks - lax.axis_index(SAMPLE) * pool_dev
    centre_sq = jnp.sum(jnp.square(centres.astype(jnp.float32)), axis=0, keepdims=True)

    def own_labels(step):
        chosen = lax.dynamic_slice(local_picks[step], (me * own,), (own,))
        return jnp.tile(jnp.take(labels, chosen, mode="clip"), fold)[None]

    z_hops = [1 << i for i in reversed(range(over_z.bit_length() - 1))]
    feats, packed, held = picked(pool, picks, coefs.T, lax.axis_size("y"))
    for hop in z_hops[:-1]:
        held = doubled(held, "z", hop)
    mine = exchange(feats, "y")
    labs = [own_labels(step) for step in range(STEPS)]
    spread_out = last_doubled(held, "z", z_hops[-1], over_x)
    mine, spread_out, centre_sq, packed, labs = lax.optimization_barrier(
        (mine, spread_out, centre_sq, packed, labs)
    )
    coef_parts = exchange(spread_out, "x")
    first, later = assembled(mine, swapped_cores(mine))
    kern = kernel_matrix(first, centres, centre_sq)

    gain = LOGIT_GAIN / total_centres
    logits = partial_logits(coef_parts, kern, n_centre, swap_offsets(z_hops))
    resid = exchange(residual(exchange(logits, CENTRE), labs[0], gain, fold), CENTRE)
    arrived = exchange(partial_grad(resid, kern, n_sample), SAMPLE)
    current, half = updated(arrived, packed, rate)

    kern = kernel_matrix(later, centres, centre_sq)
    coef_parts = exchange(half, SAMPLE).reshape(over_z, over_x, *current.shape)
    arrived = exchange(partial_logits(coef_parts, kern, n_centre), CENTRE)
    resid = exchange(residual(arrived, labs[1], gain, fold), CENTRE)
    arrived = exchange(partial_grad(resid, kern, n_sample), SAMPLE)
    return last_updated(arrived, current, rate, cen_own).T


def solution(mesh):
    sizes = (mesh.shape["centre"] // 2, 2, 8, mesh.shape["sample"] // 8)
    fine = Mesh(mesh.devices.reshape(sizes), (*CENTRE, *SAMPLE))
    placed = (
        P(None, CENTRE),
        P(CENTRE, SAMPLE),
        P(SAMPLE),
        P(None, SAMPLE),
        P(None, (*CENTRE, *SAMPLE)),
    )
    return jax.shard_map(
        on_device,
        mesh=fine,
        in_specs=placed,
        out_specs=P(None, (*CENTRE, *SAMPLE)),
        check_vma=False,
    )
```

```python
import functools

import jax
import jax.numpy as jnp
from jax import lax
from jax.experimental import pallas as pl
from jax.experimental.pallas import tpu as pltpu
from jax.sharding import Mesh, PartitionSpec as P

STEPS = 2


LOGIT_GAIN = 16.0
LENGTH_SCALE = 0.5
STEP_GAIN = 2048.0
EPS = 1e-06

LANES = 128
KERN_VMEM = 48
PICK_VMEM = 60
COPIES_COST = 1000
CENTRE = ("y", "core")
SAMPLE = ("z", "x")


def exchange(parts, axes):
    return lax.all_to_all(parts, axes, 0, 0, tiled=True)


def spread(array, axes):
    peers = lax.axis_size(axes)
    return exchange(jnp.broadcast_to(array[None], (peers, *array.shape)), axes)


def call(body, out, flops, *operands, scratch=()):
    vmem = pl.BlockSpec(memory_space=pltpu.VMEM)
    many = isinstance(out, (list, tuple))
    nbytes = sum(a.size * a.dtype.itemsize for a in operands)
    return pl.pallas_call(
        body,
        out_shape=out,
        in_specs=[vmem] * len(operands),
        out_specs=[vmem] * len(out) if many else vmem,
        scratch_shapes=list(scratch),
        cost_estimate=pl.CostEstimate(flops=flops, bytes_accessed=nbytes, transcendentals=0),
        compiler_params=pltpu.CompilerParams(vmem_limit_bytes=24 << 20),
    )(*operands)


def regroup(blocks, fold):
    width = LANES // fold
    lane_block = lax.broadcasted_iota(jnp.int32, blocks[0].shape, 1) // width
    out = []
    for q in range(fold):
        merged = None
        for k in range(fold):
            shift = width * (k - q) % LANES
            moved = pltpu.roll(blocks[k], shift, 1) if shift else blocks[k]
            merged = moved if merged is None else jnp.where(lane_block == k, moved, merged)
        out.append(merged)
    return out


def logits_body(offsets, coef_ref, kern_ref, out_ref, coef, logits):
    over_z, over_x, height, _ = coef_ref.shape
    if offsets is not None:
        over_z, over_x = over_x, over_z
    for i in range(over_z):
        for p in range(over_x // 2):
            if offsets is None:
                pair = coef_ref[i, 2 * p], coef_ref[i, 2 * p + 1]
                at = LANES * (i * over_x // 2 + p)
            else:
                pair = coef_ref[2 * p, i], coef_ref[2 * p + 1, i]
                at = LANES * (lax.bitwise_xor(lax.axis_index("z"), offsets[i]) * (over_x // 2) + p)
                at = pl.multiple_of(at, LANES)
            halves = regroup([block.astype(jnp.float32) for block in pair], 2)
            for h in range(2):
                coef[height * h : height * (h + 1), pl.ds(at, LANES)] = halves[h]
    logits[...] = lax.dot_general(
        coef[...].astype(jnp.bfloat16),
        kern_ref[...],
        (((1,), (1,)), ((), ())),
        preferred_element_type=jnp.float32,
    )
    receivers, rows, _ = out_ref.shape
    fold = coef.shape[0] // rows
    for group in range(receivers // fold):
        columns = slice(LANES * group, LANES * (group + 1))
        blocks = regroup([logits[rows * q : rows * (q + 1), columns] for q in range(fold)], fold)
        for k in range(fold):
            out_ref[fold * group + k] = blocks[k].astype(out_ref.dtype)


def partial_logits(coef_parts, kern, peers, offsets=None):
    classes = 2 * coef_parts.shape[2]
    batch, centres = kern.shape
    rows = classes * (batch // peers) // LANES
    return call(
        functools.partial(logits_body, offsets),
        jax.ShapeDtypeStruct((peers, rows, LANES), jnp.bfloat16),
        2 * classes * batch * centres,
        coef_parts,
        kern,
        scratch=[pltpu.VMEM((classes, centres), jnp.float32), pltpu.VMEM((classes, batch), jnp.float32)],
    )


def fold_all(row, fold, op):
    while fold > 1:
        row = op(row, pltpu.roll(row, LANES // fold, 1))
        fold //= 2
    return row


def residual_body(gain, fold, arrived_ref, labs_ref, out_ref):
    peers, rows, _ = arrived_ref.shape
    total = arrived_ref[0].astype(jnp.float32)
    for peer in range(1, peers):
        total = total + arrived_ref[peer].astype(jnp.float32)
    logits = total * gain
    top = fold_all(jnp.max(logits, axis=0, keepdims=True), fold, jnp.maximum)
    expo = jnp.exp(logits - top)
    mass = fold_all(jnp.sum(expo, axis=0, keepdims=True), fold, jnp.add)
    probs = expo / mass
    block = lax.broadcasted_iota(jnp.int32, logits.shape, 1) // (LANES // fold)
    class_ids = block * rows + lax.broadcasted_iota(jnp.int32, logits.shape, 0)
    onehot = (class_ids == labs_ref[...]).astype(jnp.float32)
    resid = (probs - onehot).astype(out_ref.dtype)
    for peer in range(peers):
        out_ref[peer] = resid


def residual(arrived, labs, gain, fold):
    return call(
        functools.partial(residual_body, gain, fold),
        jax.ShapeDtypeStruct(arrived.shape, jnp.bfloat16),
        8 * arrived.size,
        arrived,
        labs,
    )


def grad_body(resid_ref, kern_ref, out_ref, resid):
    peers, rows, _ = resid_ref.shape
    classes = resid.shape[0]
    fold = classes // rows
    for group in range(peers // fold):
        blocks = regroup([resid_ref[fold * group + k].astype(jnp.float32) for k in range(fold)], fold)
        for q in range(fold):
            resid[rows * q : rows * (q + 1), LANES * group : LANES * (group + 1)] = blocks[q]
    held = resid[...].astype(jnp.bfloat16)
    _, height, _ = out_ref.shape
    step = 4 * LANES
    for start in range(0, kern_ref.shape[1], step):
        grad = jnp.dot(held, kern_ref[:, start : start + step], preferred_element_type=jnp.float32)
        for at in range(0, step, LANES):
            halves = [grad[height * h : height * (h + 1), at : at + LANES] for h in range(2)]
            first = 2 * (start + at) // LANES
            for i, block in enumerate(regroup(halves, 2)):
                out_ref[first + i] = block.astype(out_ref.dtype)


def partial_grad(resid_parts, kern, peers):
    batch, centres = kern.shape
    classes = resid_parts.size // batch
    height = classes * (centres // peers) // LANES
    return call(
        grad_body,
        jax.ShapeDtypeStruct((peers, height, LANES), jnp.bfloat16),
        2 * classes * batch * centres,
        resid_parts,
        kern,
        scratch=[pltpu.VMEM((classes, batch), jnp.float32)],
    )


def assemble_body(mine_ref, other_ref, *out_refs):
    core = lax.axis_index("core")
    steps = mine_ref.shape[1]
    for step in range(steps):
        for i in range(mine_ref.shape[0]):
            for which, ref in ((core, mine_ref), (1 - core, other_ref)):
                out_refs[step][i, which] = ref[i, step]


def assembled(mine, other):
    blocks, steps, rows, batch = mine.shape
    feats = jax.ShapeDtypeStruct((blocks, 2, rows, batch), mine.dtype)
    return call(assemble_body, [feats] * steps, mine.size, mine, other)


def laplace_body(feats_ref, centres_ref, centre_sq_ref, out_ref, held, sems):
    width, centres = held.shape
    batch = feats_ref.shape[-1]
    rows = width // sems.shape[0]
    columns = 2 * LANES
    staged = [
        pltpu.make_async_copy(
            centres_ref.at[pl.ds(rows * i, rows)], held.at[pl.ds(rows * i, rows)], sems.at[i]
        )
        for i in range(sems.shape[0])
    ]
    for copy in staged:
        copy.start()
    feats = feats_ref[...].reshape(width, batch)
    squares = jnp.sum(jnp.square(feats.astype(jnp.float32)), axis=0, keepdims=True)
    sample_sq = jnp.transpose(jnp.broadcast_to(squares, (LANES, batch)))[:, :1]
    samples = jnp.transpose(feats)
    for copy in staged:
        copy.wait()
    for start in range(0, centres, columns):
        part = slice(start, start + columns)
        cross = jnp.dot(samples, held[:, part], preferred_element_type=jnp.float32)
        mean_sq = (sample_sq + centre_sq_ref[:, part] - 2.0 * cross) * (1.0 / width) + EPS
        mean_sq = jnp.maximum(mean_sq, 1e-37)
        root = mean_sq * lax.rsqrt(mean_sq)
        out_ref[:, part] = jnp.exp(root * (-1.0 / LENGTH_SCALE)).astype(out_ref.dtype)


def kernel_matrix(feats, centres, centre_sq):
    columns, batch = centres.shape[1], feats.shape[-1]
    vmem, anywhere = pl.BlockSpec(memory_space=pltpu.VMEM), pl.BlockSpec(memory_space=pl.ANY)
    return pl.pallas_call(
        laplace_body,
        out_shape=jax.ShapeDtypeStruct((batch, columns), jnp.bfloat16),
        in_specs=[vmem, anywhere, vmem],
        out_specs=vmem,
        scratch_shapes=[pltpu.VMEM(centres.shape, jnp.bfloat16), pltpu.SemaphoreType.DMA((4,))],
        cost_estimate=pl.CostEstimate(
            flops=2 * centres.size * batch, bytes_accessed=2 * centres.size, transcendentals=0
        ),
        compiler_params=pltpu.CompilerParams(vmem_limit_bytes=KERN_VMEM << 20),
    )(feats, centres, centre_sq)


def swap_offsets(hops):
    offsets = [0]
    for hop in hops:
        offsets = offsets + [o ^ hop for o in offsets]
    return offsets


def doubled(held, axis, hop):
    pairs = [(i, i ^ hop) for i in range(lax.axis_size(axis))]
    return jnp.concatenate([held, lax.ppermute(held, axis, pairs)])


def copies_body(held_ref, moved_ref, out_ref):
    near = held_ref.shape[0]
    for copy in range(out_ref.shape[0]):
        out_ref[copy, :near] = held_ref[...]
        out_ref[copy, near:] = moved_ref[...]


def last_doubled(held, axis, hop, copies):
    pairs = [(i, i ^ hop) for i in range(lax.axis_size(axis))]
    moved = lax.ppermute(held, axis, pairs)
    out = jax.ShapeDtypeStruct((copies, 2 * held.shape[0], *held.shape[1:]), held.dtype)
    return call(copies_body, out, COPIES_COST, held, moved)


def swapped_cores(array):
    return lax.ppermute(array, "core", [(0, 1), (1, 0)])


def pick_body(pool_ref, picks_ref, coefs_ref, out_ref, packed_ref, half_ref, pool, picks, coefs, sems):
    fetches = [
        pltpu.make_async_copy(ref, into, sems.at[i])
        for i, (ref, into) in enumerate(((coefs_ref, coefs), (picks_ref, picks), (pool_ref, pool)))
    ]
    for copy in fetches:
        copy.start()
    fetches[1].wait()
    pool_dev = pool.shape[1]
    copies, steps, _, batch = out_ref.shape
    first = (lax.axis_index("z") * lax.axis_size("x") + lax.axis_index("x")) * pool_dev
    rows = lax.broadcasted_iota(jnp.int32, (pool_dev, batch), 0)
    onehots = [
        (rows == picks[step : step + 1, :] - first).astype(jnp.float32).astype(jnp.bfloat16)
        for step in range(steps)
    ]
    fetches[0].wait()
    height = packed_ref.shape[0]
    sides = [coefs[:, at : at + height] for at in range(0, coefs.shape[1], height)]
    packed = jnp.transpose(jnp.concatenate(sides, axis=0))
    packed_ref[...] = packed
    half_ref[0] = packed.astype(half_ref.dtype)
    fetches[2].wait()
    for step in range(steps):
        feats = jnp.dot(pool[...], onehots[step], preferred_element_type=jnp.float32)
        for peer in range(copies):
            out_ref[peer, step] = feats.astype(out_ref.dtype)


def picked(pool, picks, coefs, copies):
    steps, batch = picks.shape
    height = coefs.size // LANES
    return pl.pallas_call(
        pick_body,
        out_shape=[
            jax.ShapeDtypeStruct((copies, steps, pool.shape[0], batch), pool.dtype),
            jax.ShapeDtypeStruct((height, LANES), coefs.dtype),
            jax.ShapeDtypeStruct((1, height, LANES), jnp.bfloat16),
        ],
        in_specs=[pl.BlockSpec(memory_space=pl.ANY)] * 3,
        out_specs=[pl.BlockSpec(memory_space=pltpu.VMEM)] * 3,
        scratch_shapes=[
            pltpu.VMEM(pool.shape, pool.dtype),
            pltpu.VMEM(picks.shape, picks.dtype),
            pltpu.VMEM(coefs.shape, coefs.dtype),
            pltpu.SemaphoreType.DMA((3,)),
        ],
        cost_estimate=pl.CostEstimate(
            flops=2 * pool.size * batch * steps, bytes_accessed=2 * pool.size, transcendentals=0
        ),
        compiler_params=pltpu.CompilerParams(vmem_limit_bytes=PICK_VMEM << 20),
    )(pool, picks, coefs)


def update_body(rate, arrived_ref, current_ref, new_ref, half_ref):
    peers = arrived_ref.shape[0]
    total = arrived_ref[0].astype(jnp.float32)
    for peer in range(1, peers):
        total = total + arrived_ref[peer].astype(jnp.float32)
    new = current_ref[...] - rate * total
    new_ref[...] = new
    half = new.astype(half_ref.dtype)
    for peer in range(peers):
        half_ref[peer] = half


def updated(arrived, current, rate):
    return call(
        functools.partial(update_body, rate),
        [
            jax.ShapeDtypeStruct(current.shape, jnp.float32),
            jax.ShapeDtypeStruct(arrived.shape, jnp.bfloat16),
        ],
        2 * arrived.size,
        arrived,
        current,
    )


def last_body(rate, arrived_ref, current_ref, new_ref):
    total = arrived_ref[0].astype(jnp.float32)
    for peer in range(1, arrived_ref.shape[0]):
        total = total + arrived_ref[peer].astype(jnp.float32)
    turned = jnp.transpose(current_ref[...] - rate * total)
    own, height = new_ref.shape[0], total.shape[0]
    for h in range(LANES // own):
        new_ref[:, height * h : height * (h + 1)] = turned[own * h : own * (h + 1)]


def last_updated(arrived, current, rate, own):
    return call(
        functools.partial(last_body, rate),
        jax.ShapeDtypeStruct((own, current.size // own), jnp.float32),
        2 * arrived.size,
        arrived,
        current,
    )


def on_device(centres, pool, labels, picks, coefs):
    cen_dev = centres.shape[1]
    pool_dev = pool.shape[1]
    batch_dev = picks.shape[1]
    classes, cen_own = coefs.shape
    n_centre, n_sample = lax.axis_size(CENTRE), lax.axis_size(SAMPLE)
    total_centres = cen_dev * n_centre
    total_batch = batch_dev * n_sample
    rate = STEP_GAIN * LOGIT_GAIN / total_batch
    own = batch_dev // n_centre
    fold = LANES // own
    me = lax.axis_index(CENTRE)
    over_z, over_x = lax.axis_size("z"), lax.axis_size("x")
    local_picks = picks - lax.axis_index(SAMPLE) * pool_dev
    centre_sq = jnp.sum(jnp.square(centres.astype(jnp.float32)), axis=0, keepdims=True)

    def own_labels(step):
        chosen = lax.dynamic_slice(local_picks[step], (me * own,), (own,))
        return jnp.tile(jnp.take(labels, chosen, mode="clip"), fold)[None]

    z_hops = [1 << i for i in reversed(range(over_z.bit_length() - 1))]
    feats, packed, held = picked(pool, picks, coefs.T, lax.axis_size("y"))
    for hop in z_hops[:-1]:
        held = doubled(held, "z", hop)
    mine = exchange(feats, "y")
    labs = [own_labels(step) for step in range(STEPS)]
    spread_out = last_doubled(held, "z", z_hops[-1], over_x)
    mine, spread_out, centre_sq, packed, labs = lax.optimization_barrier(
        (mine, spread_out, centre_sq, packed, labs)
    )
    coef_parts = exchange(spread_out, "x")
    first, later = assembled(mine, swapped_cores(mine))
    kern = kernel_matrix(first, centres, centre_sq)

    gain = LOGIT_GAIN / total_centres
    logits = partial_logits(coef_parts, kern, n_centre, swap_offsets(z_hops))
    resid = exchange(residual(exchange(logits, CENTRE), labs[0], gain, fold), CENTRE)
    arrived = exchange(partial_grad(resid, kern, n_sample), SAMPLE)
    current, half = updated(arrived, packed, rate)

    kern = kernel_matrix(later, centres, centre_sq)
    coef_parts = exchange(half, SAMPLE).reshape(over_z, over_x, *current.shape)
    arrived = exchange(partial_logits(coef_parts, kern, n_centre), CENTRE)
    resid = exchange(residual(arrived, labs[1], gain, fold), CENTRE)
    arrived = exchange(partial_grad(resid, kern, n_sample), SAMPLE)
    return last_updated(arrived, current, rate, cen_own).T


def solution(mesh):
    sizes = (mesh.shape["centre"] // 2, 2, 8, mesh.shape["sample"] // 8)
    fine = Mesh(mesh.devices.reshape(sizes), (*CENTRE, *SAMPLE))
    placed = (
        P(None, CENTRE),
        P(CENTRE, SAMPLE),
        P(SAMPLE),
        P(None, SAMPLE),
        P(None, (*CENTRE, *SAMPLE)),
    )
    return jax.shard_map(
        on_device,
        mesh=fine,
        in_specs=placed,
        out_specs=P(None, (*CENTRE, *SAMPLE)),
        check_vma=False,
    )
```
